32 devices in a mesh: fsdp: 8 (over z, y), dp: 4 (over x, core).
Axes of the slice: x: 2, y: 2, z: 4, core: 2. Of those that a mesh axis runs over, the one named last changes fastest.
Arguments:
- tokens: bfloat16 [32, 512, 768], P(None, ('fsdp', 'dp')), may hold values from -6 to 6
- cotangent: bfloat16 [32, 512, 768], P(None, ('fsdp', 'dp')), may hold values from -6 to 6
- lengths: int32 [32], replicated, may hold values from 1 to 512, 10240 in all
- device_sequence: int32 [32], replicated, may hold values from 0 to 31, each once
- slot_device: int32 [32], replicated, may hold values from 0 to 31, each once
- attention_master: float32 [3072, 768], P(('fsdp', 'dp')), may hold values from -0.649519 to 0.649519
- feedforward_master: float32 [2048, 3, 768], P(('fsdp', 'dp')), may hold values from -0.26516504 to 0.26516504
- gains_master: float32 [2, 768], P(None, ('fsdp', 'dp')), may hold values from 0.5 to 1.5
- attention_mean: float32 [3072, 768], P(('fsdp', 'dp')), may hold values from -384 to 384
- attention_square: float32 [3072, 768], P(('fsdp', 'dp')), may hold values from 1024 to 16384
- feedforward_mean: float32 [2048, 3, 768], P(('fsdp', 'dp')), may hold values from -320 to 320
- feedforward_square: float32 [2048, 3, 768], P(('fsdp', 'dp')), may hold values from 655.36 to 10485.76
- gains_mean: float32 [2, 768], P(None, ('fsdp', 'dp')), may hold values from -1280 to 1280
- gains_square: float32 [2, 768], P(None, ('fsdp', 'dp')), may hold values from 9830.4 to 163840
Outputs:
- output: bfloat16 [32, 512, 768], P(None, ('fsdp', 'dp'))
- input_gradient: bfloat16 [32, 512, 768], P(None, ('fsdp', 'dp'))
- attention_gradient: float32 [3072, 768], P(('fsdp', 'dp'))
- feedforward_gradient: float32 [2048, 3, 768], P(('fsdp', 'dp'))
- gains_gradient: float32 [2, 768], P(None, ('fsdp', 'dp'))
- mean_attention: float32 [3072, 768], P(('fsdp', 'dp'))
- square_attention: float32 [3072, 768], P(('fsdp', 'dp'))
- mean_feedforward: float32 [2048, 3, 768], P(('fsdp', 'dp'))
- square_feedforward: float32 [2048, 3, 768], P(('fsdp', 'dp'))
- mean_gains: float32 [2, 768], P(None, ('fsdp', 'dp'))
- square_gains: float32 [2, 768], P(None, ('fsdp', 'dp'))
- master_attention: float32 [3072, 768], P(('fsdp', 'dp'))
- master_feedforward: float32 [2048, 3, 768], P(('fsdp', 'dp'))
- gains_update: float32 [2, 768], P(None, ('fsdp', 'dp'))
- copy_attention: bfloat16 [3072, 768], P(('fsdp', 'dp'))
- copy_feedforward: bfloat16 [2048, 3, 768], P(('fsdp', 'dp'))
The draws below stay inside these ranges and needn't reach their ends.
Inputs may be any that keep to these rules, and one draw needn't show every extreme that they name: One sequence has exactly 512 tokens; the lengths sum to 10240. `device_sequence`: each sequence is dealt to exactly one device. `slot_device`: each device fills exactly one output slot.
All inputs are finite; a program needn't handle non-finite values.
Results may differ from the reference program's by a relative error of at most 0.02.
The reference program's roundings to bfloat16 on the way count: a program that leaves them out, or rounds other values in their place, can miss the bound.
Values may be sent and summed in bfloat16 or wider, within the bound.
A program may use at most 128 MiB of HBM per device.

```python
import math
import jax
import jax.numpy as jnp
import numpy as np
from jax import lax

D = 768
H = 12
KVH = 12
HD = 64
FF = 2048
TOK_DEV = 512
STEP = 4
NSEQ = 32
AR = 3072


def draw_attention_master(key, part):
    row_count = (2 * H + 2 * KVH) * HD
    base_draw = jnp.clip(jax.random.normal(key, (row_count, D), jnp.float32), -6.0, 6.0)
    row_index = jnp.arange(row_count)[:, None]
    row_scale = jnp.where(row_index < (H + KVH) * HD, 1.4 / D ** 0.5, jnp.where(row_index < (H + 2 * KVH) * HD, 1.0 / D ** 0.5, 3.0 / (H * HD) ** 0.5))
    return base_draw * row_scale


def draw_feedforward_master(key, part):
    base_draw = jnp.clip(jax.random.normal(key, (FF, 3, D), jnp.float32), -6.0, 6.0)
    slot_index = jnp.arange(3)[None, :, None]
    row_scale = jnp.where(slot_index < 2, 1.0 / D ** 0.5, 2.0 / FF ** 0.5)
    return base_draw * row_scale


def block_levels(own_key, dims, shards, low, top_value):
    level, own = 1.0, jax.random.fold_in(own_key, 6)
    for position, blocks in shards:
        steps = jnp.exp(jax.random.uniform(jax.random.fold_in(own, position), (blocks,), jnp.float32, low / len(shards), top_value / len(shards)))
        level = level * jnp.repeat(steps, dims[position] // blocks).reshape([-1 if axis == position else 1 for axis in range(len(dims))])
    return level


def profile(number_of, total, limit, lean):
    portions = [(1 << 20) // math.isqrt(standing ** lean) + 1 for standing in range(2, number_of + 1)]
    surplus, holding = total - limit - (number_of - 1), [1] * (number_of - 1)
    while surplus > 0:
        movable = [i for i in range(number_of - 1) if holding[i] < limit]
        pool, remaining = sum([portions[i] for i in movable]), surplus
        for i in movable:
            more = min(limit - holding[i], max(1, remaining * portions[i] // pool), surplus)
            holding[i] = holding[i] + more
            surplus = surplus - more
    return np.array([limit] + holding)


def uneven_parts(own_key, amount, total, bound, slope):
    if amount == 2:
        one = jax.random.randint(own_key, (), max(1, total - bound), min(bound, total - 1) + 1)
        return jnp.stack([one, total - one])
    sizes = jnp.asarray(profile(amount, total, bound, slope), jnp.int32)
    couples = (amount - 1) // 2
    source_of, receiver = sizes[1:1 + 2 * couples:2], sizes[2:2 + 2 * couples:2]
    margin = jnp.minimum(source_of - 1, bound - receiver)
    moved = jax.random.randint(jax.random.fold_in(own_key, 1), (couples,), 0, 1 << 20) % (margin + 1)
    sizes = sizes.at[1:1 + 2 * couples:2].set(source_of - moved).at[2:2 + 2 * couples:2].set(receiver + moved)
    return sizes[jax.random.permutation(jax.random.fold_in(own_key, 2), amount)]


def centred(key, shape, width, limit, split=(), held_as=jnp.bfloat16):
    values = width * jax.random.normal(key, shape, jnp.float32)
    if split:
        values = values * block_levels(key, shape, split, -0.22, 0.18)
    return jnp.clip(values, -limit, limit).astype(held_as)


def setup_inputs(seed: int = 0) -> dict:
    streams_of = jax.random.split(jax.random.key(seed), 15)
    tokens = centred(streams_of[0], (NSEQ, TOK_DEV, D), 1.0, 6.0, ((1, 32),))
    cotangent = centred(streams_of[1], (NSEQ, TOK_DEV, D), 1.0, 6.0, ((1, 32),))
    lengths = uneven_parts(streams_of[2], NSEQ, NSEQ * TOK_DEV * 5 // 8, TOK_DEV, 1).astype(jnp.int32)
    device_sequence = jax.random.permutation(streams_of[3], NSEQ).astype(jnp.int32)
    slot_device = jax.random.permutation(streams_of[4], NSEQ).astype(jnp.int32)
    attention_master = draw_attention_master(jax.random.fold_in(streams_of[14], 71), 0)
    feedforward_master = draw_feedforward_master(jax.random.fold_in(streams_of[14], 71), 0)
    gains_master = jnp.clip(1.0 + 0.1 * jax.random.normal(streams_of[7], (2, D), jnp.float32), 0.5, 1.5)
    attention_mean = centred(streams_of[8], (AR, D), (0.5 * (NSEQ * TOK_DEV) ** 0.5), 384.0, ((0, 32),), jnp.float32)
    attention_square = jnp.clip(jnp.exp(math.log(16384.0) - 2.7725887 * jax.random.uniform(streams_of[9], (AR, D), jnp.float32) ** block_levels(streams_of[9], (AR, D), ((0, 32),), -0.2, 0.2)), 1024.0, 16384.0)
    feedforward_mean = centred(streams_of[10], (FF, 3, D), (0.4 * (NSEQ * TOK_DEV) ** 0.5), 320.0, ((0, 32),), jnp.float32)
    feedforward_square = jnp.clip(jnp.exp(math.log(10485.76) - 2.7725887 * jax.random.uniform(streams_of[11], (FF, 3, D), jnp.float32) ** block_levels(streams_of[11], (FF, 3, D), ((0, 32),), -0.2, 0.2)), 655.36, 10485.76)
    gains_mean = centred(streams_of[12], (2, D), (1.6 * (NSEQ * TOK_DEV) ** 0.5), 1280.0, ((1, 32),), jnp.float32)
    gains_square = jnp.clip(jnp.exp(math.log(163840.0) - 2.8134107 * jax.random.uniform(streams_of[13], (2, D), jnp.float32) ** block_levels(streams_of[13], (2, D), ((1, 32),), -0.2, 0.2)), 9830.4, 163840.0)
    return {"tokens": tokens, "cotangent": cotangent, "lengths": lengths, "device_sequence": device_sequence, "slot_device": slot_device, "attention_master": attention_master, "feedforward_master": feedforward_master, "gains_master": gains_master, "attention_mean": attention_mean, "attention_square": attention_square, "feedforward_mean": feedforward_mean, "feedforward_square": feedforward_square, "gains_mean": gains_mean, "gains_square": gains_square}


norm_epsilon = 1e-05
attn_multiplier = 0.125
residual_multiplier = 1.0
rope_theta = 10000.0
beta_first = 0.5
beta_second = 0.5
learning_rate = 0.03
weight_decay = 0.1
adam_epsilon = 1e-08
highest_precision = lax.Precision.HIGHEST

@jax.custom_vjp
def low(v):
    return lax.optimization_barrier(v.astype(jnp.bfloat16)).astype(jnp.float32)

@jax.custom_vjp
def low_back(v):
    return v

def low_keep(v):
    return (low(v), None)

def low_pass(kept, grad):
    return (grad,)

def back_keep(v):
    return (v, None)

def back_low(kept, grad):
    return (low(grad),)
low.defvjp(low_keep, low_pass)
low_back.defvjp(back_keep, back_low)

def rms_scale(values, gain):
    inverse = lax.rsqrt(lax.optimization_barrier(jnp.mean(values * values, axis=-1, keepdims=True)) + norm_epsilon)
    return values * inverse * gain

def rope_tables(length):
    half_width = HD // 2
    frequency = rope_theta ** (-(jnp.arange(half_width, dtype=jnp.float32) * 2.0) / HD)
    angles = jnp.arange(length, dtype=jnp.float32)[:, None] * frequency[None, :]
    return (jnp.cos(angles), jnp.sin(angles))

def rotate(values, cosine, sine_table):
    half_width = values.shape[-1] // 2
    first_half = values[..., :half_width]
    second_half = values[..., half_width:]
    cosine = cosine[:, None, :]
    sine_table = sine_table[:, None, :]
    return jnp.concatenate([first_half * cosine - second_half * sine_table, second_half * cosine + first_half * sine_table], axis=-1)

def layer(tokens_in, attention_weight_matrix, feedforward_w, gains_w, valid):
    groups = tokens_in.shape[0]
    length = tokens_in.shape[1]
    repeat = H // KVH
    query_key_value_rows = (H + 2 * KVH) * HD
    cosine, sine_table = rope_tables(length)
    normed = low(rms_scale(tokens_in, gains_w[0]))
    projected = low_back(jnp.einsum('gld,rd->glr', normed, attention_weight_matrix[:query_key_value_rows], precision=highest_precision))
    query_heads = projected[..., :H * HD].reshape(groups, length, H, HD)
    key_heads = projected[..., H * HD:(H + KVH) * HD].reshape(groups, length, KVH, HD)
    value_heads = low(projected[..., (H + KVH) * HD:].reshape(groups, length, KVH, HD))
    query_heads = low(rotate(query_heads, cosine, sine_table)).reshape(groups, length, KVH, repeat, HD)
    key_heads = low(rotate(key_heads, cosine, sine_table))
    scores = low_back(jnp.einsum('gikrh,gjkh->gkrij', query_heads, key_heads, precision=highest_precision) * attn_multiplier)
    causal = jnp.arange(length)[:, None] >= jnp.arange(length)[None, :]
    weights = low(jax.nn.softmax(jnp.where(causal, scores, -1e+30), axis=-1))
    combined_heads = jnp.einsum('gkrij,gjkh->gikrh', weights, value_heads, precision=highest_precision).reshape(groups, length, H * HD)
    combined_heads = low(low_back(combined_heads))
    branch_path = low_back(jnp.einsum('xjz,zy->xjy', combined_heads, attention_weight_matrix[query_key_value_rows:], precision=highest_precision))
    hidden_state = tokens_in + residual_multiplier * branch_path
    normed_two = low(rms_scale(hidden_state, gains_w[1]))
    gate_values = low_back(jnp.einsum('gld,fd->glf', normed_two, feedforward_w[:, 0], precision=highest_precision))
    up_values = low_back(jnp.einsum('gld,fd->glf', normed_two, feedforward_w[:, 1], precision=highest_precision))
    activation = low(jax.nn.silu(gate_values) * up_values)
    branch_two = low_back(jnp.einsum('glf,fd->gld', activation, feedforward_w[:, 2], precision=highest_precision))
    result = hidden_state + residual_multiplier * branch_two
    return jnp.where(valid[..., None], result, 0.0)

def adam_update(master, gradient, first_moment, second_moment, decay):
    first_new = beta_first * first_moment + (1.0 - beta_first) * gradient
    second_new = beta_second * second_moment + (1.0 - beta_second) * gradient * gradient
    first_hat = first_new / (1.0 - beta_first ** STEP)
    second_hat = second_new / (1.0 - beta_second ** STEP)
    master_new = master - learning_rate * (first_hat / (jnp.sqrt(second_hat) + adam_epsilon) + decay * master)
    return (first_new, second_new, master_new)

def reference(tokens, cotangent, lengths, device_sequence, slot_device, attention_master, feedforward_master, gains_master, attention_mean, attention_square, feedforward_mean, feedforward_square, gains_mean, gains_square):
    slot_sequence = device_sequence[slot_device].astype(jnp.int32)
    inverse = jnp.zeros((NSEQ,), jnp.int32).at[slot_sequence].set(jnp.arange(NSEQ, dtype=jnp.int32))
    attention_weight_matrix = attention_master.astype(jnp.bfloat16).astype(jnp.float32)
    feedforward_w = feedforward_master.astype(jnp.bfloat16).astype(jnp.float32)
    gains_w = gains_master.astype(jnp.bfloat16).astype(jnp.float32)
    per_block = math.gcd(NSEQ, max(1, 2048 // TOK_DEV))
    blocks = NSEQ // per_block
    slot_tokens = tokens.astype(jnp.float32)[slot_sequence].reshape(blocks, per_block, TOK_DEV, D)
    slot_cotangent = cotangent.astype(jnp.float32).reshape(blocks, per_block, TOK_DEV, D)
    slot_lengths = lengths[slot_sequence].reshape(blocks, per_block)
    valid_all = jnp.arange(TOK_DEV, dtype=jnp.int32)[None, None, :] < slot_lengths[..., None]

    def step_block(carry, items):
        block_tokens, block_cotangent, block_valid = items

        def closed(tokens_in, aw_in, fw_in, gw_in):
            return layer(tokens_in, aw_in, fw_in, gw_in, block_valid)
        result, pullback = jax.vjp(closed, block_tokens, attention_weight_matrix, feedforward_w, gains_w)
        token_grad, attention_grad, feedforward_grad, gains_grad = pullback(block_cotangent)
        return ((carry[0] + attention_grad, carry[1] + feedforward_grad, carry[2] + gains_grad), (result, token_grad))
    start = (jnp.zeros(attention_weight_matrix.shape, jnp.float32), jnp.zeros(feedforward_w.shape, jnp.float32), jnp.zeros(gains_w.shape, jnp.float32))
    sums, (results, token_grads) = lax.scan(step_block, start, (slot_tokens, slot_cotangent, valid_all))
    attention_gradient, feedforward_gradient, gains_gradient = sums
    output = results.reshape(NSEQ, TOK_DEV, D).astype(jnp.bfloat16)
    input_gradient = token_grads.reshape(NSEQ, TOK_DEV, D)[inverse].astype(jnp.bfloat16)
    mean_attention, square_attention, master_attention = adam_update(attention_master, attention_gradient, attention_mean, attention_square, weight_decay)
    mean_feedforward, square_feedforward, master_feedforward = adam_update(feedforward_master, feedforward_gradient, feedforward_mean, feedforward_square, weight_decay)
    mean_gains, square_gains, master_gains = adam_update(gains_master, gains_gradient, gains_mean, gains_square, 0.0)
    gains_update = master_gains - gains_master
    return (output, input_gradient, attention_gradient, feedforward_gradient, gains_gradient, mean_attention, square_attention, mean_feedforward, square_feedforward, mean_gains, square_gains, master_attention, master_feedforward, gains_update, master_attention.astype(jnp.bfloat16), master_feedforward.astype(jnp.bfloat16))
```

```python
import functools
import jax, jax.numpy as jnp, numpy as np
from jax import lax
from jax.experimental import pallas as pl
from jax.experimental.pallas import tpu as pltpu
H=12; KVH=12; HD=64; STEP=4
norm_epsilon=1e-05; attn_multiplier=0.125; rope_theta=10000.0
f32=jnp.float32; bf16=jnp.bfloat16
LOG2E=1.4426950408889634

def dot_nt(a,b):
    return lax.dot_general(a,b,(((1,),(1,)),((),())),preferred_element_type=f32)
def dot_nn(a,b):
    return lax.dot_general(a,b,(((1,),(0,)),((),())),preferred_element_type=f32)
def dot_tn(a,b):
    return lax.dot_general(a,b,(((0,),(0,)),((),())),preferred_element_type=f32)

def tables(length):
    half=HD//2
    freq=(np.float32(rope_theta)**(-(np.arange(half,dtype=np.float32)*np.float32(2.0))/np.float32(HD))).astype(np.float32)
    ang=(np.arange(length,dtype=np.float32)[:,None]*freq[None,:]).astype(np.float32)
    c=np.cos(ang.astype(np.float64)).astype(np.float32); s=np.sin(ang.astype(np.float64)).astype(np.float32)
    C=np.concatenate([c,c,c,c],1); S=np.concatenate([-s,s,-s,s],1)
    return C,S

RB=64
def rows_loop(length, body):
    def it(i,carry):
        body(pl.ds(pl.multiple_of(i*RB,RB),RB), i*RB)
        return carry
    lax.fori_loop(0,length//RB,it,0)

def norm_block(xv, gain):
    inv=lax.rsqrt(jnp.mean(xv*xv,axis=-1,keepdims=True)+norm_epsilon)
    return inv

def swap_halves(x):
    lane=lax.broadcasted_iota(jnp.int32,x.shape,1)
    return jnp.where(lax.rem(lane,64)<32, pltpu.roll(x,96,1), pltpu.roll(x,32,1))

def phase_norm1(x_ref,g_ref,n1_ref):
    L=x_ref.shape[0]
    def body(r,_):
        xv=x_ref[r,:].astype(f32)
        inv=norm_block(xv,None)
        n1_ref[r,:]=(xv*inv*g_ref[0:1,:]).astype(bf16)
    rows_loop(L,body)

def phase_qkv(n1_ref,w_ref,cos_ref,sin_ref,qkv_ref):
    def rt(n,carry):
        o=pl.multiple_of(n*256,256)
        p=dot_nt(n1_ref[...],w_ref[pl.ds(o,256),:])
        for j in range(2):
            x=p[:,128*j:128*j+128]
            qkv_ref[:,pl.ds(pl.multiple_of(o+128*j,128),128)]=(x*cos_ref[...]+swap_halves(x)*sin_ref[...]).astype(bf16)
        return carry
    lax.fori_loop(0,6,rt,0)
    def vt(n,carry):
        o=pl.multiple_of(n*256,256)
        qkv_ref[:,pl.ds(o,256)]=dot_nt(n1_ref[...],w_ref[pl.ds(o,256),:]).astype(bf16)
        return carry
    lax.fori_loop(6,9,vt,0)

def lane_masks(a):
    lane=lax.broadcasted_iota(jnp.int32,a.shape,1)
    z=jnp.zeros_like(a)
    return jnp.where(lane<64,a,z), jnp.where(lane<64,z,a)

def phase_attn_fwd(qkv_ref,p_ref,o_ref):
    L=qkv_ref.shape[0]; QB=256
    def pair(t,carry):
        oq=pl.multiple_of(t*128,128); ok=pl.multiple_of(768+t*128,128); ov=pl.multiple_of(1536+t*128,128)
        for i in range(L//QB):
            kl=(i+1)*QB
            q=lane_masks(qkv_ref[i*QB:(i+1)*QB,pl.ds(oq,128)])
            k=qkv_ref[0:kl,pl.ds(ok,128)]
            v=lane_masks(qkv_ref[0:kl,pl.ds(ov,128)])
            ps=[]
            for h in range(2):
                s=dot_nt(q[h],k)
                row=lax.broadcasted_iota(jnp.int32,s.shape,0)+i*QB
                col=lax.broadcasted_iota(jnp.int32,s.shape,1)
                s=jnp.where(row>=col,s,-1e30)
                m=jnp.max(s,axis=-1,keepdims=True)
                e=jnp.exp2((s-m)*(attn_multiplier*LOG2E))
                pr=(e*(1.0/jnp.sum(e,axis=-1,keepdims=True))).astype(bf16)
                p_ref[2*t+h,i*QB:(i+1)*QB,0:kl]=pr
                ps.append(pr)
            o_ref[i*QB:(i+1)*QB,pl.ds(oq,128)]=dot_nn(jnp.concatenate(ps,1),jnp.concatenate(v,0)).astype(bf16)
        return carry
    lax.fori_loop(0,H//2,pair,0)

def phase_wo_norm2(o_ref,w_ref,x_ref,g_ref,hs_ref,n2_ref):
    L=x_ref.shape[0]; R=128
    def it(i,carry):
        r=pl.ds(pl.multiple_of(i*R,R),R)
        hs=x_ref[r,:].astype(f32)+dot_nn(o_ref[r,:],w_ref[2304:3072,:])
        hs_ref[r,:]=hs
        inv=norm_block(hs,None)
        n2_ref[r,:]=(hs*inv*g_ref[1:2,:]).astype(bf16)
        return carry
    lax.fori_loop(0,L//R,it,0)

def phase_ff(n2_ref,db2_ref,wff_ref,gff_ref,b2_ref,dn2_ref):
    sh=wff_ref.shape[2]; per=256//sh; nt=wff_ref.shape[0]//per
    def tile(t,carry):
        sl=pl.ds(t*per,per)
        wg=wff_ref[sl,0].reshape(256,768); wu=wff_ref[sl,1].reshape(256,768); wd=wff_ref[sl,2].reshape(256,768)
        n2=n2_ref[...]
        g=dot_nt(n2,wg); u=dot_nt(n2,wu)
        da=dot_nt(db2_ref[...],wd)
        sg=1.0/(1.0+jnp.exp2(g*(-LOG2E)))
        silu=g*sg
        a=(silu*u).astype(bf16)
        dg=(da*u*(sg*(1.0+g*(1.0-sg)))).astype(bf16)
        du=(da*silu).astype(bf16)
        b2=dot_nn(a,wd)
        dn=dot_nn(dg,wg)+dot_nn(du,wu)
        @pl.when(t==0)
        def _():
            b2_ref[...]=b2; dn2_ref[...]=dn
        @pl.when(t>0)
        def _():
            b2_ref[...]+=b2; dn2_ref[...]+=dn
        gff_ref[sl,0]=dot_tn(dg,n2).astype(bf16).reshape(per,sh,768)
        gff_ref[sl,1]=dot_tn(du,n2).astype(bf16).reshape(per,sh,768)
        gff_ref[sl,2]=dot_tn(a,db2_ref[...]).astype(bf16).reshape(per,sh,768)
        return carry
    lax.fori_loop(0,nt,tile,0)

def phase_mid(len_ref,c_ref,hs_ref,b2_ref,dn2_ref,g_ref,out_ref,dhs_ref,db1_ref,gg_ref):
    L=hs_ref.shape[0]
    n=len_ref[0]
    gg_ref[...]=jnp.zeros_like(gg_ref)
    def body(r,o):
        row=lax.broadcasted_iota(jnp.int32,(RB,768),0)+o
        hs=hs_ref[r,:]
        out_ref[r,:]=jnp.where(row<n,hs+b2_ref[r,:],0.0).astype(bf16)
        dy=jnp.where(row<n,c_ref[r,:].astype(f32),0.0)
        inv=norm_block(hs,None)
        dn=dn2_ref[r,:]
        q=dn*g_ref[1:2,:]
        gg_ref[1:2,:]+=jnp.sum(hs*inv*dn,axis=0,keepdims=True)
        dh=dy+(inv*q-hs*inv*inv*inv*jnp.mean(hs*q,axis=-1,keepdims=True))
        dhs_ref[r,:]=dh
        db1_ref[r,:]=dh.astype(bf16)
    rows_loop(L,body)

def phase_db2(len_ref,c_ref,db2_ref):
    n=len_ref[0]
    def body(r,o):
        row=lax.broadcasted_iota(jnp.int32,(RB,768),0)+o
        db2_ref[r,:]=jnp.where(row<n,c_ref[r,:].astype(f32),0.0).astype(bf16)
    rows_loop(c_ref.shape[0],body)

def phase_wo_back(db1_ref,o_ref,w_ref,do_ref,gatt_ref):
    def it(n,carry):
        o=pl.multiple_of(n*256,256)
        do_ref[:,pl.ds(o,256)]=dot_nt(db1_ref[...],w_ref[pl.ds(pl.multiple_of(2304+o,256),256),:]).astype(bf16)
        gatt_ref[pl.ds(pl.multiple_of(2304+o,256),256),:]=dot_tn(o_ref[:,pl.ds(o,256)],db1_ref[...]).astype(bf16)
        return carry
    lax.fori_loop(0,3,it,0)

def phase_attn_bwd(qkv_ref,p_ref,do_ref,cos_ref,sin_ref,dp_ref):
    L=qkv_ref.shape[0]; QB=256
    def pair(t,carry):
        oq=pl.multiple_of(t*128,128); ok=pl.multiple_of(768+t*128,128); ov=pl.multiple_of(1536+t*128,128)
        dkt=None; dvt=None
        for i in range(L//QB):
            kl=(i+1)*QB; r=slice(i*QB,(i+1)*QB)
            q=lane_masks(qkv_ref[r,pl.ds(oq,128)])
            k=lane_masks(qkv_ref[0:kl,pl.ds(ok,128)])
            v=qkv_ref[0:kl,pl.ds(ov,128)]
            do=lane_masks(do_ref[r,pl.ds(oq,128)])
            dss=[]; pls=[]
            for h in range(2):
                pb=p_ref[2*t+h,r,0:kl]
                p=pb.astype(f32)
                if i<L//QB:
                    row=lax.broadcasted_iota(jnp.int32,p.shape,0)+i*QB
                dpr=dot_nt(do[h],v)
                pd=p*dpr
                ds=(pd-p*jnp.sum(pd,axis=-1,keepdims=True)).astype(bf16)
                dss.append(ds); pls.append(pb)
            dq=dot_nn(jnp.concatenate(dss,1),jnp.concatenate(k,0))*attn_multiplier
            c=cos_ref[r,:]; s=sin_ref[r,:]
            dp_ref[r,pl.ds(oq,128)]=(dq*c-swap_halves(dq)*s).astype(bf16)
            a=dot_tn(jnp.concatenate(q,0),jnp.concatenate(dss,0))
            b=dot_tn(jnp.concatenate(do,0),jnp.concatenate(pls,0))
            if dkt is None: dkt,dvt=a,b
            else:
                w=dkt.shape[1]
                dkt=jnp.concatenate([dkt+a[:,:w],a[:,w:]],1); dvt=jnp.concatenate([dvt+b[:,:w],b[:,w:]],1)
        dk=dkt.T*attn_multiplier
        dp_ref[:,pl.ds(ok,128)]=(dk*cos_ref[...]-swap_halves(dk)*sin_ref[...]).astype(bf16)
        dp_ref[:,pl.ds(ov,128)]=dvt.T.astype(bf16)
        return carry
    lax.fori_loop(0,H//2,pair,0)

def phase_dn1(dp_ref,w_ref,x_ref,g_ref,dhs_ref,in_ref,gg_ref):
    L=x_ref.shape[0]; R=128
    def it(i,carry):
        r=pl.ds(pl.multiple_of(i*R,R),R)
        dn=dot_nn(dp_ref[r,:],w_ref[0:2304,:])
        xv=x_ref[r,:].astype(f32)
        inv=norm_block(xv,None)
        gg_ref[0:1,:]+=jnp.sum(xv*inv*dn,axis=0,keepdims=True)
        q=dn*g_ref[0:1,:]
        in_ref[r,:]=(dhs_ref[r,:]+(inv*q-xv*inv*inv*inv*jnp.mean(xv*q,axis=-1,keepdims=True))).astype(bf16)
        return carry
    lax.fori_loop(0,L//R,it,0)

def phase_wqkv_grad(dp_ref,n1_ref,gatt_ref):
    def it(n,carry):
        o=pl.multiple_of(n*256,256)
        gatt_ref[pl.ds(o,256),:]=dot_tn(dp_ref[:,pl.ds(o,256)],n1_ref[...]).astype(bf16)
        return carry
    lax.fori_loop(0,9,it,0)

def k2_kernel(len_ref,x_ref,c_ref,watt_ref,wff_ref,g_ref,cos_ref,sin_ref,
              out_ref,in_ref,gatt_ref,gff_ref,gg_ref,
              n1,qkv,pm,o,hs,n2,db2,b2,dn2,dhs,db1,do,dpj):
    phase_norm1(x_ref,g_ref,n1)
    phase_qkv(n1,watt_ref,cos_ref,sin_ref,qkv)
    phase_attn_fwd(qkv,pm,o)
    phase_wo_norm2(o,watt_ref,x_ref,g_ref,hs,n2)
    phase_db2(len_ref,c_ref,db2)
    phase_ff(n2,db2,wff_ref,gff_ref,b2,dn2)
    phase_mid(len_ref,c_ref,hs,b2,dn2,g_ref,out_ref,dhs,db1,gg_ref)
    phase_wo_back(db1,o,watt_ref,do,gatt_ref)
    phase_attn_bwd(qkv,pm,do,cos_ref,sin_ref,dpj)
    phase_dn1(dpj,watt_ref,x_ref,g_ref,dhs,in_ref,gg_ref)
    phase_wqkv_grad(dpj,n1,gatt_ref)

def k2(length,x,c,watt,wff,gains,cos,sin,kern=k2_kernel):
    L,D=x.shape
    V=pl.BlockSpec(memory_space=pltpu.VMEM)
    vm=lambda *s,dt=bf16: pltpu.VMEM(s,dt)
    return pl.pallas_call(kern,
        out_shape=(jax.ShapeDtypeStruct((L,D),bf16),jax.ShapeDtypeStruct((L,D),bf16),jax.ShapeDtypeStruct(watt.shape,bf16),jax.ShapeDtypeStruct(wff.shape,bf16),jax.ShapeDtypeStruct((8,D),f32)),
        in_specs=[pl.BlockSpec(memory_space=pltpu.SMEM)]+[V]*7,out_specs=(V,)*5,
        scratch_shapes=[vm(L,D),vm(L,3*D),vm(H,L,L),vm(L,D),vm(L,D,dt=f32),vm(L,D),vm(L,D),vm(L,D,dt=f32),vm(L,D,dt=f32),vm(L,D,dt=f32),vm(L,D),vm(L,D),vm(L,3*D)],
        compiler_params=pltpu.CompilerParams(vmem_limit_bytes=63*2**20),
        )(length,x,c,watt,wff,gains,cos,sin)
MESH=pl.DeviceIdType.MESH

class Topo:
    def __init__(s, nf, nd):
        assert nd==4 and nf%2==0
        s.Z=nf//2; s.N=nf*nd
        f=lax.axis_index("fsdp"); d=lax.axis_index("dp")
        s.z=f//2; s.y=lax.rem(f,2); s.x=d//2; s.c=lax.rem(d,2)
        s.me=f*4+d
        c=s.c
        s.y1=s.y+c*(1-2*s.y); s.x1=s.x+(1-c)*(1-2*s.x)
        s.y2=s.y+(1-c)*(1-2*s.y); s.x2=s.x+c*(1-2*s.x)
        s.yb=1-s.y; s.xb=1-s.x; s.cb=1-c
    def slot(s,z,y,x,c): return ((z*2+y)*2+x)*2+c
    def dev(s,z,y,x,c): return (z*2+y, x*2+c)
    def flat(s,i): return (i//4, lax.rem(i,4))
    def zk(s,k): return lax.rem(s.z+k,s.Z)
    @property
    def p1(s): return s.dev(s.z,s.y1,s.x1,s.c)
    @property
    def p2(s): return s.dev(s.z,s.y2,s.x2,s.c)
    @property
    def sib(s): return s.dev(s.z,s.y,s.x,s.cb)

def loop(lo,hi,body):
    lax.fori_loop(lo,hi,lambda i,c:(body(i),c)[1],0)

def rcopy(src,dst,ssem,rsem,dev):
    return pltpu.make_async_remote_copy(src_ref=src,dst_ref=dst,send_sem=ssem,recv_sem=rsem,device_id=dev,device_id_type=MESH)

def wait_bytes(ref,sem):
    pltpu.make_async_copy(ref,ref,sem).wait()

def barrier_all(t):
    b=pltpu.get_barrier_semaphore()
    def sig(k): pl.semaphore_signal(b,inc=1,device_id=t.flat(lax.rem(t.me+k,t.N)),device_id_type=MESH)
    loop(1,t.N,sig)
    pl.semaphore_wait(b,t.N-1)

class A2A:
    def __init__(s,t,src,dst,ssem,rsem,lsem): s.t,s.src,s.dst,s.ssem,s.rsem,s.lsem=t,src,dst,ssem,rsem,lsem
    def start(s):
        t=s.t
        pltpu.make_async_copy(s.src.at[t.me],s.dst.at[t.me],s.lsem).start()
        def f(k):
            d=lax.rem(t.me+k,t.N)
            rcopy(s.src.at[d],s.dst.at[t.me],s.ssem,s.rsem,t.flat(d)).start()
        loop(1,t.N,f)
    def wait_recv(s):
        n=s.t.N-1
        pltpu.make_async_copy(s.src.at[s.t.me],s.dst.at[s.t.me],s.lsem).wait()
        wait_bytes(s.dst.at[pl.ds(0,n)],s.rsem)
    def wait_send(s):
        wait_bytes(s.src.at[pl.ds(0,s.t.N-1)],s.ssem)

class Gather:
    def __init__(s,t,src,dst,ssem,rsem,lsem): s.t,s.src,s.dst,s.ssem,s.rsem,s.lsem=t,src,dst,ssem,rsem,lsem
    def send(s,slot,dev,src=None):
        rcopy(s.dst.at[slot] if src is None else src,s.dst.at[slot],s.ssem,s.rsem.at[slot],dev).start()
    def wait(s,slot):
        wait_bytes(s.dst.at[slot],s.rsem.at[slot])
    def start(s):
        t=s.t
        pltpu.make_async_copy(s.src,s.dst.at[t.me],s.lsem).start()
        for dev in (t.p1,t.p2,t.sib): s.send(t.me,dev,s.src)
        loop(1,t.Z,lambda k: s.send(t.me,t.dev(t.zk(k),t.y,t.x,t.c),s.src))
    def phase1(s):
        t=s.t
        def f(k):
            sl=t.slot(t.zk(k),t.y,t.x,t.c); s.wait(sl)
            for dev in (t.p1,t.p2,t.sib): s.send(sl,dev)
        loop(1,t.Z,f)
    def phase2(s):
        t=s.t
        def f(k):
            sl=t.slot(t.zk(k),t.y1,t.x1,t.c); s.wait(sl)
            for dev in (t.p2,t.sib): s.send(sl,dev)
        loop(0,t.Z,f)
    def phase3(s):
        t=s.t
        for y,x in ((t.y2,t.x2),(t.yb,t.xb)):
            def f(k):
                sl=t.slot(t.zk(k),y,x,t.c); s.wait(sl); s.send(sl,t.sib)
            loop(0,t.Z,f)
    def phase4(s):
        t=s.t
        for y,x in ((0,0),(0,1),(1,0),(1,1)):
            loop(0,t.Z,lambda k: s.wait(t.slot(t.zk(k),y,x,t.cb)))
    def finish(s):
        t=s.t
        pltpu.make_async_copy(s.src,s.dst.at[t.me],s.lsem).wait()
        wait_bytes(s.dst.at[pl.ds(0,t.N-1)],s.ssem)

def k1_kernel(nf,nd,perm,tok,cot0,gn,att,ff,xg,cg,gg,wa,wf,cot,ss,rs,ls,ars,frs):
    t=Topo(nf,nd)
    barrier_all(t)
    tk=A2A(t,tok,xg,ss.at[0],rs.at[0],ls.at[0])
    ct=A2A(t,cot,cg,ss.at[1],rs.at[1],ls.at[1])
    A=Gather(t,att,wa,ss.at[3],ars,ls.at[3]); F=Gather(t,ff,wf,ss.at[4],frs,ls.at[4])
    pltpu.make_async_copy(gn,gg.at[t.me],ls.at[2]).start()
    def gs(k): rcopy(gn,gg.at[t.me],ss.at[2],rs.at[2],t.flat(lax.rem(t.me+k,t.N))).start()
    loop(1,t.N,gs)
    A.start()
    tk.start()
    def pm(i): cot[i]=cot0[perm[i]]
    loop(0,t.N,pm)
    A.phase1()
    F.start()
    A.phase2()
    F.phase1()
    A.phase3()
    F.phase2()
    ct.start()
    A.phase4()
    F.phase3(); F.phase4()
    tk.wait_recv(); ct.wait_recv()
    pltpu.make_async_copy(gn,gg.at[t.me],ls.at[2]).wait()
    wait_bytes(gg.at[pl.ds(0,t.N-1)],rs.at[2]); wait_bytes(gg.at[pl.ds(0,t.N-1)],ss.at[2])
    A.finish(); F.finish(); tk.wait_send(); ct.wait_send()

def k1(perm,tok,cot,gn,att,ff):
    nf,nd=lax.axis_size("fsdp"),lax.axis_size("dp"); N=nf*nd
    anyv=pl.BlockSpec(memory_space=pl.ANY); D=pltpu.SemaphoreType.DMA
    sd=jax.ShapeDtypeStruct
    return pl.pallas_call(functools.partial(k1_kernel,nf,nd),
        out_shape=(sd(tok.shape,tok.dtype),sd(cot.shape,cot.dtype),sd((N,)+gn.shape,gn.dtype),sd((N,)+att.shape,att.dtype),sd((N,)+ff.shape,ff.dtype)),
        in_specs=[pl.BlockSpec(memory_space=pltpu.SMEM),anyv,pl.BlockSpec(memory_space=pltpu.VMEM),anyv,anyv,anyv],out_specs=(anyv,)*5,
        scratch_shapes=[pltpu.VMEM(cot.shape,cot.dtype),D((5,)),D((5,)),D((5,)),D((N,)),D((N,))],
        compiler_params=pltpu.CompilerParams(collective_id=0,has_side_effects=True))(perm,tok,cot,gn,att,ff)

class Scatter:
    def __init__(s,t,g,rc,r1,r2,rz,ss,rcs,r1s,r2s,rzs):
        s.t,s.g,s.rc,s.r1,s.r2,s.rz,s.ss,s.rcs,s.r1s,s.r2s,s.rzs=t,g,rc,r1,r2,rz,ss,rcs,r1s,r2s,rzs
        s.Z=t.Z
    def groups(s,sibling):
        t=s.t
        if sibling:
            return ((t.yb,t.xb),(t.y1,t.x1),(t.y2,t.x2),(t.y,t.x))
        return ((t.yb,t.xb),(t.y2,t.x2),(t.y1,t.x1),(t.y,t.x))
    def start(s):
        t=s.t; Z=s.Z
        for gi,(y,x) in enumerate(s.groups(True)):
            def f(k):
                rcopy(s.g.at[t.slot(t.zk(k),y,x,t.cb)],s.rc.at[gi*Z+k],s.ss.at[0],s.rcs.at[gi*Z+k],t.sib).start()
            loop(0,Z,f)
    def stage_c(s):
        t=s.t; Z=s.Z
        for gi,(y,x) in enumerate(s.groups(False)):
            def f(k):
                j=gi*Z+k
                wait_bytes(s.rc.at[j],s.rcs.at[j])
                s.rc[j]=s.rc[j]+s.g[t.slot(t.zk(k),y,x,t.c)]
                if gi<2: rcopy(s.rc.at[j],s.r1.at[j],s.ss.at[1],s.r1s.at[j],t.p2).start()
            loop(0,Z,f)
    def stage_1(s):
        t=s.t; Z=s.Z
        for gi in range(2):
            def f(k):
                j=gi*Z+k
                wait_bytes(s.r1.at[j],s.r1s.at[j])
                s.r1[j]=s.r1[j]+s.rc[2*Z+j]
                if gi==0: rcopy(s.r1.at[j],s.r2.at[k],s.ss.at[2],s.r2s.at[k],t.p1).start()
            loop(0,Z,f)
    def stage_2(s):
        t=s.t; Z=s.Z
        def f(k):
            wait_bytes(s.r2.at[k],s.r2s.at[k])
            s.r2[k]=s.r2[k]+s.r1[Z+k]
            rcopy(s.r2.at[k],s.rz.at[Z-k-1],s.ss.at[3],s.rzs.at[Z-k-1],t.dev(t.zk(k),t.y,t.x,t.c)).start()
        loop(1,Z,f)
        wait_bytes(s.r2.at[0],s.r2s.at[0])
    def final(s,out):
        Z=s.Z
        tot=s.r2[0].astype(f32)+s.r1[Z].astype(f32)
        for k in range(Z-1):
            wait_bytes(s.rz.at[k],s.rzs.at[k])
            tot=tot+s.rz[k].astype(f32)
        out[...]=tot
    def wait_send(s):
        Z=s.Z
        wait_bytes(s.rc,s.ss.at[0])
        wait_bytes(s.r1,s.ss.at[1])
        wait_bytes(s.r2,s.ss.at[2])
        wait_bytes(s.rz,s.ss.at[3])

def k3_kernel(nf,nd,perm,orow,irow,gg,ga,gf,oo0,io,ggo,ao,fo,oo,ggr,arc,ar1,ar2,arz,frc,fr1,fr2,frz,ss,rs,ls,ass,fss,acs,a1s,a2s,azs,fcs,f1s,f2s,fzs):
    t=Topo(nf,nd)
    barrier_all(t)
    A=Scatter(t,ga,arc,ar1,ar2,arz,ass,acs,a1s,a2s,azs)
    F=Scatter(t,gf,frc,fr1,fr2,frz,fss,fcs,f1s,f2s,fzs)
    F.start(); A.start()
    pltpu.make_async_copy(gg.at[t.me],ggr.at[t.me],ls.at[2]).start()
    def gs(k):
        d=lax.rem(t.me+k,t.N)
        rcopy(gg.at[d],ggr.at[t.me],ss.at[2],rs.at[2],t.flat(d)).start()
    loop(1,t.N,gs)
    F.stage_c()
    o=A2A(t,orow,oo,ss.at[0],rs.at[0],ls.at[0])
    i=A2A(t,irow,io,ss.at[1],rs.at[1],ls.at[1])
    o.start()
    A.stage_c()
    i.start()
    F.stage_1(); F.stage_2()
    A.stage_1(); A.stage_2()
    pltpu.make_async_copy(gg.at[t.me],ggr.at[t.me],ls.at[2]).wait()
    wait_bytes(ggr.at[pl.ds(0,t.N-1)],rs.at[2]); wait_bytes(ggr.at[pl.ds(0,t.N-1)],ss.at[2])
    tot=ggr[0]
    for k in range(1,t.N): tot=tot+ggr[k]
    ggo[...]=tot
    F.final(fo); A.final(ao)
    o.wait_recv()
    def pm(j): oo0[j]=oo[perm[j]]
    loop(0,t.N,pm)
    i.wait_recv(); o.wait_send(); i.wait_send()
    F.wait_send(); A.wait_send()

def k3(perm,orow,irow,gg,ga,gf):
    nf,nd=lax.axis_size("fsdp"),lax.axis_size("dp"); N=nf*nd; Z=nf//2
    anyv=pl.BlockSpec(memory_space=pl.ANY); V=pl.BlockSpec(memory_space=pltpu.VMEM); D=pltpu.SemaphoreType.DMA
    sd=jax.ShapeDtypeStruct
    ash,fsh=ga.shape[1:],gf.shape[1:]
    vm=lambda n,sh: pltpu.VMEM((n,)+sh,bf16)
    return pl.pallas_call(functools.partial(k3_kernel,nf,nd),
        out_shape=(sd(orow.shape,bf16),sd(irow.shape,bf16),sd(gg.shape[1:],f32),sd(ash,f32),sd(fsh,f32)),
        in_specs=[pl.BlockSpec(memory_space=pltpu.SMEM),anyv,anyv,V,V,V],out_specs=(V,anyv,V,V,V),
        scratch_shapes=[pltpu.VMEM(orow.shape,bf16),pltpu.VMEM(gg.shape,f32)]+[vm(n,sh) for sh in (ash,fsh) for n in (4*Z,2*Z,Z,Z-1)]+[D((3,)),D((3,)),D((3,)),D((4,)),D((4,))]+[D((n,)) for _ in range(2) for n in (4*Z,2*Z,Z,Z-1)],
        compiler_params=pltpu.CompilerParams(collective_id=1,has_side_effects=True,vmem_limit_bytes=60*2**20))(perm,orow,irow,gg,ga,gf)


from jax.sharding import PartitionSpec as P
AX = ("fsdp", "dp")
beta_first = 0.5
beta_second = 0.5
learning_rate = 0.03
weight_decay = 0.1
adam_epsilon = 1e-08


def adam_update(master, gradient, first_moment, second_moment, decay):
    first_new = beta_first * first_moment + (1.0 - beta_first) * gradient
    second_new = beta_second * second_moment + (1.0 - beta_second) * gradient * gradient
    first_hat = first_new / (1.0 - beta_first**STEP)
    second_hat = second_new / (1.0 - beta_second**STEP)
    master_new = master - learning_rate * (
        first_hat / (jnp.sqrt(second_hat) + adam_epsilon) + decay * master
    )
    return (first_new, second_new, master_new)


def local(tokens, cotangent, lengths, device_sequence, slot_device, attention_master, feedforward_master, gains_master,
          attention_mean, attention_square, feedforward_mean, feedforward_square, gains_mean, gains_square):
    N = lax.axis_size(AX)
    me = lax.axis_index(AX)
    positions, width = tokens.shape[1], tokens.shape[2]
    length = positions * N
    gl = gains_master.shape[1]
    counter = jnp.arange(N, dtype=jnp.int32)
    slot_sequence = jnp.sum(jnp.where(slot_device[:, None] == counter[None, :], device_sequence[None, :], 0), axis=1)
    slot_of_sequence = jnp.sum(jnp.where(slot_sequence[:, None] == counter[None, :], counter[:, None], 0), axis=0)
    att_low = attention_master.astype(bf16)
    ff_low = feedforward_master.transpose(1, 0, 2).astype(bf16)
    gn = jnp.zeros((8, 128), f32).at[:2, :gl].set(gains_master.astype(bf16).astype(f32))
    xg, cg, gg, wa, wf = k1(slot_of_sequence, tokens, cotangent, gn, att_low, ff_low)
    gains = jnp.zeros((8, width), f32).at[:2].set(gg[:, :2, :gl].transpose(1, 0, 2).reshape(2, width))
    C, S = tables(length)
    orow, irow, gatt, gff, ggr = k2(jnp.sum(jnp.where(counter == me, lengths, 0))[None], xg.reshape(length, width), cg.reshape(length, width),
                                    wa.reshape(-1, width), wf, gains, jnp.asarray(C), jnp.asarray(S))
    gblocks = jnp.zeros((N, 8, 128), f32).at[:, :2, :gl].set(ggr[:2].reshape(2, N, gl).transpose(1, 0, 2))
    oo, io, gsum, ag, fg = k3(slot_sequence, orow.reshape(N, positions, width), irow.reshape(N, positions, width), gblocks,
                              gatt.reshape(N, -1, width), gff)
    output = oo
    attention_gradient = ag
    feedforward_gradient = fg.transpose(1, 0, 2)
    gains_gradient = gsum[:2, :gl]
    mean_attention, square_attention, master_attention = adam_update(
        attention_master, attention_gradient, attention_mean, attention_square, weight_decay)
    mean_feedforward, square_feedforward, master_feedforward = adam_update(
        feedforward_master, feedforward_gradient, feedforward_mean, feedforward_square, weight_decay)
    mean_gains, square_gains, master_gains = adam_update(gains_master, gains_gradient, gains_mean, gains_square, 0.0)
    return (output, io, attention_gradient, feedforward_gradient, gains_gradient, mean_attention, square_attention,
            mean_feedforward, square_feedforward, mean_gains, square_gains, master_attention, master_feedforward,
            master_gains - gains_master, master_attention.astype(bf16), master_feedforward.astype(bf16))


def solution(mesh):
    t, r, f, g = P(None, AX, None), P(AX, None), P(AX, None, None), P(None, AX)
    in_specs = (t, t, P(), P(), P(), r, f, g, r, r, f, f, g, g)
    out_specs = (t, t, r, f, g, r, r, f, f, g, g, r, f, g, r, f)
    return jax.shard_map(local, mesh=mesh, in_specs=in_specs, out_specs=out_specs, check_vma=False)
```

```python
import functools
import jax, jax.numpy as jnp, numpy as np
from jax import lax
from jax.experimental import pallas as pl
from jax.experimental.pallas import tpu as pltpu
H=12; KVH=12; HD=64; STEP=4
norm_epsilon=1e-05; attn_multiplier=0.125; rope_theta=10000.0
f32=jnp.float32; bf16=jnp.bfloat16
LOG2E=1.4426950408889634

def dot_nt(a,b):
    return lax.dot_general(a,b,(((1,),(1,)),((),())),preferred_element_type=f32)
def dot_nn(a,b):
    return lax.dot_general(a,b,(((1,),(0,)),((),())),preferred_element_type=f32)
def dot_tn(a,b):
    return lax.dot_general(a,b,(((0,),(0,)),((),())),preferred_element_type=f32)

def tables(length):
    half=HD//2
    freq=(np.float32(rope_theta)**(-(np.arange(half,dtype=np.float32)*np.float32(2.0))/np.float32(HD))).astype(np.float32)
    ang=(np.arange(length,dtype=np.float32)[:,None]*freq[None,:]).astype(np.float32)
    c=np.cos(ang.astype(np.float64)).astype(np.float32); s=np.sin(ang.astype(np.float64)).astype(np.float32)
    C=np.concatenate([c,c,c,c],1); S=np.concatenate([-s,s,-s,s],1)
    return C,S

RB=64
def rows_loop(length, body):
    def it(i,carry):
        body(pl.ds(pl.multiple_of(i*RB,RB),RB), i*RB)
        return carry
    lax.fori_loop(0,length//RB,it,0)

def norm_block(xv, gain):
    inv=lax.rsqrt(jnp.mean(xv*xv,axis=-1,keepdims=True)+norm_epsilon)
    return inv

def swap_halves(x):
    lane=lax.broadcasted_iota(jnp.int32,x.shape,1)
    return jnp.where(lax.rem(lane,64)<32, pltpu.roll(x,96,1), pltpu.roll(x,32,1))

def phase_norm1(x_ref,g_ref,n1_ref):
    L=x_ref.shape[0]
    def body(r,_):
        xv=x_ref[r,:].astype(f32)
        inv=norm_block(xv,None)
        n1_ref[r,:]=(xv*inv*g_ref[0:1,:]).astype(bf16)
    rows_loop(L,body)

def phase_qkv(n1_ref,w_ref,cos_ref,sin_ref,qkv_ref):
    def rt(n,carry):
        o=pl.multiple_of(n*256,256)
        p=dot_nt(n1_ref[...],w_ref[pl.ds(o,256),:])
        for j in range(2):
            x=p[:,128*j:128*j+128]
            qkv_ref[:,pl.ds(pl.multiple_of(o+128*j,128),128)]=(x*cos_ref[...]+swap_halves(x)*sin_ref[...]).astype(bf16)
        return carry
    lax.fori_loop(0,6,rt,0)
    def vt(n,carry):
        o=pl.multiple_of(n*256,256)
        qkv_ref[:,pl.ds(o,256)]=dot_nt(n1_ref[...],w_ref[pl.ds(o,256),:]).astype(bf16)
        return carry
    lax.fori_loop(6,9,vt,0)

def lane_masks(a):
    lane=lax.broadcasted_iota(jnp.int32,a.shape,1)
    z=jnp.zeros_like(a)
    return jnp.where(lane<64,a,z), jnp.where(lane<64,z,a)

def phase_attn_fwd(qkv_ref,p_ref,o_ref):
    L=qkv_ref.shape[0]; QB=256
    def pair(t,carry):
        oq=pl.multiple_of(t*128,128); ok=pl.multiple_of(768+t*128,128); ov=pl.multiple_of(1536+t*128,128)
        for i in range(L//QB):
            kl=(i+1)*QB
            q=lane_masks(qkv_ref[i*QB:(i+1)*QB,pl.ds(oq,128)])
            k=qkv_ref[0:kl,pl.ds(ok,128)]
            v=lane_masks(qkv_ref[0:kl,pl.ds(ov,128)])
            ps=[]
            for h in range(2):
                s=dot_nt(q[h],k)
                row=lax.broadcasted_iota(jnp.int32,s.shape,0)+i*QB
                col=lax.broadcasted_iota(jnp.int32,s.shape,1)
                s=jnp.where(row>=col,s,-1e30)
                m=jnp.max(s,axis=-1,keepdims=True)
                e=jnp.exp2((s-m)*(attn_multiplier*LOG2E))
                pr=(e*(1.0/jnp.sum(e,axis=-1,keepdims=True))).astype(bf16)
                p_ref[2*t+h,i*QB:(i+1)*QB,0:kl]=pr
                ps.append(pr)
            o_ref[i*QB:(i+1)*QB,pl.ds(oq,128)]=dot_nn(jnp.concatenate(ps,1),jnp.concatenate(v,0)).astype(bf16)
        return carry
    lax.fori_loop(0,H//2,pair,0)

def phase_wo_norm2(o_ref,w_ref,x_ref,g_ref,hs_ref,n2_ref):
    L=x_ref.shape[0]; R=128
    def it(i,carry):
        r=pl.ds(pl.multiple_of(i*R,R),R)
        hs=x_ref[r,:].astype(f32)+dot_nn(o_ref[r,:],w_ref[2304:3072,:])
        hs_ref[r,:]=hs
        inv=norm_block(hs,None)
        n2_ref[r,:]=(hs*inv*g_ref[1:2,:]).astype(bf16)
        return carry
    lax.fori_loop(0,L//R,it,0)

def phase_ff(n2_ref,db2_ref,wff_ref,gff_ref,b2_ref,dn2_ref):
    sh=wff_ref.shape[2]; per=256//sh; nt=wff_ref.shape[0]//per
    def tile(t,carry):
        sl=pl.ds(t*per,per)
        wg=wff_ref[sl,0].reshape(256,768); wu=wff_ref[sl,1].reshape(256,768); wd=wff_ref[sl,2].reshape(256,768)
        n2=n2_ref[...]
        g=dot_nt(n2,wg); u=dot_nt(n2,wu)
        da=dot_nt(db2_ref[...],wd)
        sg=1.0/(1.0+jnp.exp2(g*(-LOG2E)))
        silu=g*sg
        a=(silu*u).astype(bf16)
        dg=(da*u*(sg*(1.0+g*(1.0-sg)))).astype(bf16)
        du=(da*silu).astype(bf16)
        b2=dot_nn(a,wd)
        dn=dot_nn(dg,wg)+dot_nn(du,wu)
        @pl.when(t==0)
        def _():
            b2_ref[...]=b2; dn2_ref[...]=dn
        @pl.when(t>0)
        def _():
            b2_ref[...]+=b2; dn2_ref[...]+=dn
        gff_ref[sl,0]=dot_tn(dg,n2).astype(bf16).reshape(per,sh,768)
        gff_ref[sl,1]=dot_tn(du,n2).astype(bf16).reshape(per,sh,768)
        gff_ref[sl,2]=dot_tn(a,db2_ref[...]).astype(bf16).reshape(per,sh,768)
        return carry
    lax.fori_loop(0,nt,tile,0)

def phase_mid(len_ref,c_ref,hs_ref,b2_ref,dn2_ref,g_ref,out_ref,dhs_ref,db1_ref,gg_ref):
    L=hs_ref.shape[0]
    n=len_ref[0]
    gg_ref[...]=jnp.zeros_like(gg_ref)
    def body(r,o):
        row=lax.broadcasted_iota(jnp.int32,(RB,768),0)+o
        hs=hs_ref[r,:]
        out_ref[r,:]=jnp.where(row<n,hs+b2_ref[r,:],0.0).astype(bf16)
        dy=jnp.where(row<n,c_ref[r,:].astype(f32),0.0)
        inv=norm_block(hs,None)
        dn=dn2_ref[r,:]
        q=dn*g_ref[1:2,:]
        gg_ref[1:2,:]+=jnp.sum(hs*inv*dn,axis=0,keepdims=True)
        dh=dy+(inv*q-hs*inv*inv*inv*jnp.mean(hs*q,axis=-1,keepdims=True))
        dhs_ref[r,:]=dh
        db1_ref[r,:]=dh.astype(bf16)
    rows_loop(L,body)

def phase_db2(len_ref,c_ref,db2_ref):
    n=len_ref[0]
    def body(r,o):
        row=lax.broadcasted_iota(jnp.int32,(RB,768),0)+o
        db2_ref[r,:]=jnp.where(row<n,c_ref[r,:].astype(f32),0.0).astype(bf16)
    rows_loop(c_ref.shape[0],body)

def phase_wo_back(db1_ref,o_ref,w_ref,do_ref,gatt_ref):
    def it(n,carry):
        o=pl.multiple_of(n*256,256)
        do_ref[:,pl.ds(o,256)]=dot_nt(db1_ref[...],w_ref[pl.ds(pl.multiple_of(2304+o,256),256),:]).astype(bf16)
        gatt_ref[pl.ds(pl.multiple_of(2304+o,256),256),:]=dot_tn(o_ref[:,pl.ds(o,256)],db1_ref[...]).astype(bf16)
        return carry
    lax.fori_loop(0,3,it,0)

def phase_attn_bwd(qkv_ref,p_ref,do_ref,cos_ref,sin_ref,dp_ref):
    L=qkv_ref.shape[0]; QB=256
    def pair(t,carry):
        oq=pl.multiple_of(t*128,128); ok=pl.multiple_of(768+t*128,128); ov=pl.multiple_of(1536+t*128,128)
        dkt=None; dvt=None
        for i in range(L//QB):
            kl=(i+1)*QB; r=slice(i*QB,(i+1)*QB)
            q=lane_masks(qkv_ref[r,pl.ds(oq,128)])
            k=lane_masks(qkv_ref[0:kl,pl.ds(ok,128)])
            v=qkv_ref[0:kl,pl.ds(ov,128)]
            do=lane_masks(do_ref[r,pl.ds(oq,128)])
            dss=[]; pls=[]
            for h in range(2):
                pb=p_ref[2*t+h,r,0:kl]
                p=pb.astype(f32)
                if i<L//QB:
                    row=lax.broadcasted_iota(jnp.int32,p.shape,0)+i*QB
                dpr=dot_nt(do[h],v)
                pd=p*dpr
                ds=(pd-p*jnp.sum(pd,axis=-1,keepdims=True)).astype(bf16)
                dss.append(ds); pls.append(pb)
            dq=dot_nn(jnp.concatenate(dss,1),jnp.concatenate(k,0))*attn_multiplier
            c=cos_ref[r,:]; s=sin_ref[r,:]
            dp_ref[r,pl.ds(oq,128)]=(dq*c-swap_halves(dq)*s).astype(bf16)
            a=dot_tn(jnp.concatenate(q,0),jnp.concatenate(dss,0))
            b=dot_tn(jnp.concatenate(do,0),jnp.concatenate(pls,0))
            if dkt is None: dkt,dvt=a,b
            else:
                w=dkt.shape[1]
                dkt=jnp.concatenate([dkt+a[:,:w],a[:,w:]],1); dvt=jnp.concatenate([dvt+b[:,:w],b[:,w:]],1)
        dk=dkt.T*attn_multiplier
        dp_ref[:,pl.ds(ok,128)]=(dk*cos_ref[...]-swap_halves(dk)*sin_ref[...]).astype(bf16)
        dp_ref[:,pl.ds(ov,128)]=dvt.T.astype(bf16)
        return carry
    lax.fori_loop(0,H//2,pair,0)

def phase_dn1(dp_ref,w_ref,x_ref,g_ref,dhs_ref,in_ref,gg_ref):
    L=x_ref.shape[0]; R=128
    def it(i,carry):
        r=pl.ds(pl.multiple_of(i*R,R),R)
        dn=dot_nn(dp_ref[r,:],w_ref[0:2304,:])
        xv=x_ref[r,:].astype(f32)
        inv=norm_block(xv,None)
        gg_ref[0:1,:]+=jnp.sum(xv*inv*dn,axis=0,keepdims=True)
        q=dn*g_ref[0:1,:]
        in_ref[r,:]=(dhs_ref[r,:]+(inv*q-xv*inv*inv*inv*jnp.mean(xv*q,axis=-1,keepdims=True))).astype(bf16)
        return carry
    lax.fori_loop(0,L//R,it,0)

def phase_wqkv_grad(dp_ref,n1_ref,gatt_ref):
    def it(n,carry):
        o=pl.multiple_of(n*256,256)
        gatt_ref[pl.ds(o,256),:]=dot_tn(dp_ref[:,pl.ds(o,256)],n1_ref[...]).astype(bf16)
        return carry
    lax.fori_loop(0,9,it,0)

def k2_kernel(len_ref,x_ref,c_ref,watt_ref,wff_ref,g_ref,cos_ref,sin_ref,
              out_ref,in_ref,gatt_ref,gff_ref,gg_ref,
              n1,qkv,pm,o,hs,n2,db2,b2,dn2,dhs,db1,do,dpj):
    phase_norm1(x_ref,g_ref,n1)
    phase_qkv(n1,watt_ref,cos_ref,sin_ref,qkv)
    phase_attn_fwd(qkv,pm,o)
    phase_wo_norm2(o,watt_ref,x_ref,g_ref,hs,n2)
    phase_db2(len_ref,c_ref,db2)
    phase_ff(n2,db2,wff_ref,gff_ref,b2,dn2)
    phase_mid(len_ref,c_ref,hs,b2,dn2,g_ref,out_ref,dhs,db1,gg_ref)
    phase_wo_back(db1,o,watt_ref,do,gatt_ref)
    phase_attn_bwd(qkv,pm,do,cos_ref,sin_ref,dpj)
    phase_dn1(dpj,watt_ref,x_ref,g_ref,dhs,in_ref,gg_ref)
    phase_wqkv_grad(dpj,n1,gatt_ref)

def k2(length,x,c,watt,wff,gains,cos,sin,kern=k2_kernel):
    L,D=x.shape
    V=pl.BlockSpec(memory_space=pltpu.VMEM)
    vm=lambda *s,dt=bf16: pltpu.VMEM(s,dt)
    return pl.pallas_call(kern,
        out_shape=(jax.ShapeDtypeStruct((L,D),bf16),jax.ShapeDtypeStruct((L,D),bf16),jax.ShapeDtypeStruct(watt.shape,bf16),jax.ShapeDtypeStruct(wff.shape,bf16),jax.ShapeDtypeStruct((8,D),f32)),
        in_specs=[pl.BlockSpec(memory_space=pltpu.SMEM)]+[V]*7,out_specs=(V,)*5,
        scratch_shapes=[vm(L,D),vm(L,3*D),vm(H,L,L),vm(L,D),vm(L,D,dt=f32),vm(L,D),vm(L,D),vm(L,D,dt=f32),vm(L,D,dt=f32),vm(L,D,dt=f32),vm(L,D),vm(L,D),vm(L,3*D)],
        compiler_params=pltpu.CompilerParams(vmem_limit_bytes=63*2**20),
        )(length,x,c,watt,wff,gains,cos,sin)
MESH=pl.DeviceIdType.MESH

class Topo:
    def __init__(s, nf, nd):
        assert nd==4 and nf%2==0
        s.Z=nf//2; s.N=nf*nd
        f=lax.axis_index("fsdp"); d=lax.axis_index("dp")
        s.z=f//2; s.y=lax.rem(f,2); s.x=d//2; s.c=lax.rem(d,2)
        s.me=f*4+d
        c=s.c
        s.y1=s.y+c*(1-2*s.y); s.x1=s.x+(1-c)*(1-2*s.x)
        s.y2=s.y+(1-c)*(1-2*s.y); s.x2=s.x+c*(1-2*s.x)
        s.yb=1-s.y; s.xb=1-s.x; s.cb=1-c
    def slot(s,z,y,x,c): return ((z*2+y)*2+x)*2+c
    def dev(s,z,y,x,c): return (z*2+y, x*2+c)
    def flat(s,i): return (i//4, lax.rem(i,4))
    def zk(s,k): return lax.rem(s.z+k,s.Z)
    @property
    def p1(s): return s.dev(s.z,s.y1,s.x1,s.c)
    @property
    def p2(s): return s.dev(s.z,s.y2,s.x2,s.c)
    @property
    def sib(s): return s.dev(s.z,s.y,s.x,s.cb)

def loop(lo,hi,body):
    lax.fori_loop(lo,hi,lambda i,c:(body(i),c)[1],0)

def rcopy(src,dst,ssem,rsem,dev):
    return pltpu.make_async_remote_copy(src_ref=src,dst_ref=dst,send_sem=ssem,recv_sem=rsem,device_id=dev,device_id_type=MESH)

def wait_bytes(ref,sem):
    pltpu.make_async_copy(ref,ref,sem).wait()

def barrier_all(t):
    b=pltpu.get_barrier_semaphore()
    def sig(k): pl.semaphore_signal(b,inc=1,device_id=t.flat(lax.rem(t.me+k,t.N)),device_id_type=MESH)
    loop(1,t.N,sig)
    pl.semaphore_wait(b,t.N-1)

class A2A:
    def __init__(s,t,src,dst,ssem,rsem,lsem): s.t,s.src,s.dst,s.ssem,s.rsem,s.lsem=t,src,dst,ssem,rsem,lsem
    def start(s):
        t=s.t
        pltpu.make_async_copy(s.src.at[t.me],s.dst.at[t.me],s.lsem).start()
        def f(k):
            d=lax.rem(t.me+k,t.N)
            rcopy(s.src.at[d],s.dst.at[t.me],s.ssem,s.rsem,t.flat(d)).start()
        loop(1,t.N,f)
    def wait_recv(s):
        n=s.t.N-1
        pltpu.make_async_copy(s.src.at[s.t.me],s.dst.at[s.t.me],s.lsem).wait()
        wait_bytes(s.dst.at[pl.ds(0,n)],s.rsem)
    def wait_send(s):
        wait_bytes(s.src.at[pl.ds(0,s.t.N-1)],s.ssem)

class Gather:
    def __init__(s,t,src,dst,ssem,rsem,lsem): s.t,s.src,s.dst,s.ssem,s.rsem,s.lsem=t,src,dst,ssem,rsem,lsem
    def send(s,slot,dev,src=None):
        rcopy(s.dst.at[slot] if src is None else src,s.dst.at[slot],s.ssem,s.rsem.at[slot],dev).start()
    def wait(s,slot):
        wait_bytes(s.dst.at[slot],s.rsem.at[slot])
    def start(s):
        t=s.t
        pltpu.make_async_copy(s.src,s.dst.at[t.me],s.lsem).start()
        for dev in (t.p1,t.p2,t.sib): s.send(t.me,dev,s.src)
        loop(1,t.Z,lambda k: s.send(t.me,t.dev(t.zk(k),t.y,t.x,t.c),s.src))
    def phase1(s):
        t=s.t
        def f(k):
            sl=t.slot(t.zk(k),t.y,t.x,t.c); s.wait(sl)
            for dev in (t.p1,t.p2,t.sib): s.send(sl,dev)
        loop(1,t.Z,f)
    def phase2(s):
        t=s.t
        def f(k):
            sl=t.slot(t.zk(k),t.y1,t.x1,t.c); s.wait(sl)
            for dev in (t.p2,t.sib): s.send(sl,dev)
        loop(0,t.Z,f)
    def phase3(s):
        t=s.t
        for y,x in ((t.y2,t.x2),(t.yb,t.xb)):
            def f(k):
                sl=t.slot(t.zk(k),y,x,t.c); s.wait(sl); s.send(sl,t.sib)
            loop(0,t.Z,f)
    def phase4(s):
        t=s.t
        for y,x in ((0,0),(0,1),(1,0),(1,1)):
            loop(0,t.Z,lambda k: s.wait(t.slot(t.zk(k),y,x,t.cb)))
    def finish(s):
        t=s.t
        pltpu.make_async_copy(s.src,s.dst.at[t.me],s.lsem).wait()
        wait_bytes(s.dst.at[pl.ds(0,t.N-1)],s.ssem)

def k1_kernel(nf,nd,perm,tok,cot0,gn,att,ff,xg,cg,gg,wa,wf,cot,ss,rs,ls,ars,frs):
    t=Topo(nf,nd)
    barrier_all(t)
    tk=A2A(t,tok,xg,ss.at[0],rs.at[0],ls.at[0])
    ct=A2A(t,cot,cg,ss.at[1],rs.at[1],ls.at[1])
    A=Gather(t,att,wa,ss.at[3],ars,ls.at[3]); F=Gather(t,ff,wf,ss.at[4],frs,ls.at[4])
    pltpu.make_async_copy(gn,gg.at[t.me],ls.at[2]).start()
    def gs(k): rcopy(gn,gg.at[t.me],ss.at[2],rs.at[2],t.flat(lax.rem(t.me+k,t.N))).start()
    loop(1,t.N,gs)
    A.start()
    tk.start()
    def pm(i): cot[i]=cot0[perm[i]]
    loop(0,t.N,pm)
    A.phase1()
    F.start()
    A.phase2()
    F.phase1()
    A.phase3()
    F.phase2()
    ct.start()
    A.phase4()
    F.phase3(); F.phase4()
    tk.wait_recv(); ct.wait_recv()
    pltpu.make_async_copy(gn,gg.at[t.me],ls.at[2]).wait()
    wait_bytes(gg.at[pl.ds(0,t.N-1)],rs.at[2]); wait_bytes(gg.at[pl.ds(0,t.N-1)],ss.at[2])
    A.finish(); F.finish(); tk.wait_send(); ct.wait_send()

def k1(perm,tok,cot,gn,att,ff):
    nf,nd=lax.axis_size("fsdp"),lax.axis_size("dp"); N=nf*nd
    anyv=pl.BlockSpec(memory_space=pl.ANY); D=pltpu.SemaphoreType.DMA
    sd=jax.ShapeDtypeStruct
    return pl.pallas_call(functools.partial(k1_kernel,nf,nd),
        out_shape=(sd(tok.shape,tok.dtype),sd(cot.shape,cot.dtype),sd((N,)+gn.shape,gn.dtype),sd((N,)+att.shape,att.dtype),sd((N,)+ff.shape,ff.dtype)),
        in_specs=[pl.BlockSpec(memory_space=pltpu.SMEM),anyv,pl.BlockSpec(memory_space=pltpu.VMEM),anyv,anyv,anyv],out_specs=(anyv,)*5,
        scratch_shapes=[pltpu.VMEM(cot.shape,cot.dtype),D((5,)),D((5,)),D((5,)),D((N,)),D((N,))],
        compiler_params=pltpu.CompilerParams(collective_id=0,has_side_effects=True))(perm,tok,cot,gn,att,ff)

class Scatter:
    def __init__(s,t,g,rc,r1,r2,rz,ss,rcs,r1s,r2s,rzs):
        s.t,s.g,s.rc,s.r1,s.r2,s.rz,s.ss,s.rcs,s.r1s,s.r2s,s.rzs=t,g,rc,r1,r2,rz,ss,rcs,r1s,r2s,rzs
        s.Z=t.Z
    def groups(s,sibling):
        t=s.t
        if sibling:
            return ((t.yb,t.xb),(t.y1,t.x1),(t.y2,t.x2),(t.y,t.x))
        return ((t.yb,t.xb),(t.y2,t.x2),(t.y1,t.x1),(t.y,t.x))
    def start(s):
        t=s.t; Z=s.Z
        for gi,(y,x) in enumerate(s.groups(True)):
            def f(k):
                rcopy(s.g.at[t.slot(t.zk(k),y,x,t.cb)],s.rc.at[gi*Z+k],s.ss.at[0],s.rcs.at[gi*Z+k],t.sib).start()
            loop(0,Z,f)
    def stage_c(s):
        t=s.t; Z=s.Z
        for gi,(y,x) in enumerate(s.groups(False)):
            def f(k):
                j=gi*Z+k
                wait_bytes(s.rc.at[j],s.rcs.at[j])
                s.rc[j]=s.rc[j]+s.g[t.slot(t.zk(k),y,x,t.c)]
                if gi<2: rcopy(s.rc.at[j],s.r1.at[j],s.ss.at[1],s.r1s.at[j],t.p2).start()
            loop(0,Z,f)
    def stage_1(s):
        t=s.t; Z=s.Z
        for gi in range(2):
            def f(k):
                j=gi*Z+k
                wait_bytes(s.r1.at[j],s.r1s.at[j])
                s.r1[j]=s.r1[j]+s.rc[2*Z+j]
                if gi==0: rcopy(s.r1.at[j],s.r2.at[k],s.ss.at[2],s.r2s.at[k],t.p1).start()
            loop(0,Z,f)
    def stage_2(s):
        t=s.t; Z=s.Z
        def f(k):
            wait_bytes(s.r2.at[k],s.r2s.at[k])
            s.r2[k]=s.r2[k]+s.r1[Z+k]
            rcopy(s.r2.at[k],s.rz.at[Z-k-1],s.ss.at[3],s.rzs.at[Z-k-1],t.dev(t.zk(k),t.y,t.x,t.c)).start()
        loop(1,Z,f)
        wait_bytes(s.r2.at[0],s.r2s.at[0])
    def final(s,out):
        Z=s.Z
        tot=s.r2[0].astype(f32)+s.r1[Z].astype(f32)
        for k in range(Z-1):
            wait_bytes(s.rz.at[k],s.rzs.at[k])
            tot=tot+s.rz[k].astype(f32)
        out[...]=tot
    def wait_send(s):
        Z=s.Z
        wait_bytes(s.rc,s.ss.at[0])
        wait_bytes(s.r1,s.ss.at[1])
        wait_bytes(s.r2,s.ss.at[2])
        wait_bytes(s.rz,s.ss.at[3])

def k3_kernel(nf,nd,perm,orow,irow,gg,ga,gf,oo0,io,ggo,ao,fo,oo,ggr,arc,ar1,ar2,arz,frc,fr1,fr2,frz,ss,rs,ls,ass,fss,acs,a1s,a2s,azs,fcs,f1s,f2s,fzs):
    t=Topo(nf,nd)
    barrier_all(t)
    A=Scatter(t,ga,arc,ar1,ar2,arz,ass,acs,a1s,a2s,azs)
    F=Scatter(t,gf,frc,fr1,fr2,frz,fss,fcs,f1s,f2s,fzs)
    F.start(); A.start()
    pltpu.make_async_copy(gg.at[t.me],ggr.at[t.me],ls.at[2]).start()
    def gs(k):
        d=lax.rem(t.me+k,t.N)
        rcopy(gg.at[d],ggr.at[t.me],ss.at[2],rs.at[2],t.flat(d)).start()
    loop(1,t.N,gs)
    F.stage_c()
    o=A2A(t,orow,oo,ss.at[0],rs.at[0],ls.at[0])
    i=A2A(t,irow,io,ss.at[1],rs.at[1],ls.at[1])
    o.start()
    A.stage_c()
    i.start()
    F.stage_1(); F.stage_2()
    A.stage_1(); A.stage_2()
    pltpu.make_async_copy(gg.at[t.me],ggr.at[t.me],ls.at[2]).wait()
    wait_bytes(ggr.at[pl.ds(0,t.N-1)],rs.at[2]); wait_bytes(ggr.at[pl.ds(0,t.N-1)],ss.at[2])
    tot=ggr[0]
    for k in range(1,t.N): tot=tot+ggr[k]
    ggo[...]=tot
    F.final(fo); A.final(ao)
    o.wait_recv()
    def pm(j): oo0[j]=oo[perm[j]]
    loop(0,t.N,pm)
    i.wait_recv(); o.wait_send(); i.wait_send()
    F.wait_send(); A.wait_send()

def k3(perm,orow,irow,gg,ga,gf):
    nf,nd=lax.axis_size("fsdp"),lax.axis_size("dp"); N=nf*nd; Z=nf//2
    anyv=pl.BlockSpec(memory_space=pl.ANY); V=pl.BlockSpec(memory_space=pltpu.VMEM); D=pltpu.SemaphoreType.DMA
    sd=jax.ShapeDtypeStruct
    ash,fsh=ga.shape[1:],gf.shape[1:]
    vm=lambda n,sh: pltpu.VMEM((n,)+sh,bf16)
    return pl.pallas_call(functools.partial(k3_kernel,nf,nd),
        out_shape=(sd(orow.shape,bf16),sd(irow.shape,bf16),sd(gg.shape[1:],f32),sd(ash,f32),sd(fsh,f32)),
        in_specs=[pl.BlockSpec(memory_space=pltpu.SMEM),anyv,anyv,V,V,V],out_specs=(V,anyv,V,V,V),
        scratch_shapes=[pltpu.VMEM(orow.shape,bf16),pltpu.VMEM(gg.shape,f32)]+[vm(n,sh) for sh in (ash,fsh) for n in (4*Z,2*Z,Z,Z-1)]+[D((3,)),D((3,)),D((3,)),D((4,)),D((4,))]+[D((n,)) for _ in range(2) for n in (4*Z,2*Z,Z,Z-1)],
        compiler_params=pltpu.CompilerParams(collective_id=1,has_side_effects=True,vmem_limit_bytes=60*2**20))(perm,orow,irow,gg,ga,gf)


from jax.sharding import PartitionSpec as P
AX = ("fsdp", "dp")
beta_first = 0.5
beta_second = 0.5
learning_rate = 0.03
weight_decay = 0.1
adam_epsilon = 1e-08


def adam_update(master, gradient, first_moment, second_moment, decay):
    first_new = beta_first * first_moment + (1.0 - beta_first) * gradient
    second_new = beta_second * second_moment + (1.0 - beta_second) * gradient * gradient
    first_hat = first_new / (1.0 - beta_first**STEP)
    second_hat = second_new / (1.0 - beta_second**STEP)
    master_new = master - learning_rate * (
        first_hat / (jnp.sqrt(second_hat) + adam_epsilon) + decay * master
    )
    return (first_new, second_new, master_new)


def local(tokens, cotangent, lengths, device_sequence, slot_device, attention_master, feedforward_master, gains_master,
          attention_mean, attention_square, feedforward_mean, feedforward_square, gains_mean, gains_square):
    N = lax.axis_size(AX)
    me = lax.axis_index(AX)
    positions, width = tokens.shape[1], tokens.shape[2]
    length = positions * N
    gl = gains_master.shape[1]
    counter = jnp.arange(N, dtype=jnp.int32)
    slot_sequence = jnp.sum(jnp.where(slot_device[:, None] == counter[None, :], device_sequence[None, :], 0), axis=1)
    slot_of_sequence = jnp.sum(jnp.where(slot_sequence[:, None] == counter[None, :], counter[:, None], 0), axis=0)
    att_low = attention_master.astype(bf16)
    ff_low = feedforward_master.transpose(1, 0, 2).astype(bf16)
    gn = jnp.zeros((8, 128), f32).at[:2, :gl].set(gains_master.astype(bf16).astype(f32))
    xg, cg, gg, wa, wf = k1(slot_of_sequence, tokens, cotangent, gn, att_low, ff_low)
    gains = jnp.zeros((8, width), f32).at[:2].set(gg[:, :2, :gl].transpose(1, 0, 2).reshape(2, width))
    C, S = tables(length)
    orow, irow, gatt, gff, ggr = k2(jnp.sum(jnp.where(counter == me, lengths, 0))[None], xg.reshape(length, width), cg.reshape(length, width),
                                    wa.reshape(-1, width), wf, gains, jnp.asarray(C), jnp.asarray(S))
    gblocks = jnp.zeros((N, 8, 128), f32).at[:, :2, :gl].set(ggr[:2].reshape(2, N, gl).transpose(1, 0, 2))
    oo, io, gsum, ag, fg = k3(slot_sequence, orow.reshape(N, positions, width), irow.reshape(N, positions, width), gblocks,
                              gatt.reshape(N, -1, width), gff)
    output = oo
    attention_gradient = ag
    feedforward_gradient = fg.transpose(1, 0, 2)
    gains_gradient = gsum[:2, :gl]
    mean_attention, square_attention, master_attention = adam_update(
        attention_master, attention_gradient, attention_mean, attention_square, weight_decay)
    mean_feedforward, square_feedforward, master_feedforward = adam_update(
        feedforward_master, feedforward_gradient, feedforward_mean, feedforward_square, weight_decay)
    mean_gains, square_gains, master_gains = adam_update(gains_master, gains_gradient, gains_mean, gains_square, 0.0)
    return (output, io, attention_gradient, feedforward_gradient, gains_gradient, mean_attention, square_attention,
            mean_feedforward, square_feedforward, mean_gains, square_gains, master_attention, master_feedforward,
            master_gains - gains_master, master_attention.astype(bf16), master_feedforward.astype(bf16))


class Topo2(Topo):
    def __init__(s, nf, nd):
        super().__init__(nf, nd)
    def flip(s, gi, cc):
        a, b = lax.rem(gi, 2), gi // 2
        fx, fy = (1 - cc) * a + cc * b, (1 - cc) * b + cc * a
        return s.y + fy * (1 - 2 * s.y), s.x + fx * (1 - 2 * s.x)
    def g8(s, gi, cc):
        y, x = s.flip(gi, cc)
        return (y * 2 + x) * 2 + cc


class Gather2:
    def __init__(s, t, at, ssem, rsem): s.t, s.at, s.ssem, s.rsem = t, at, ssem, rsem
    def send(s, z, g, dev):
        rcopy(s.at(z, g), s.at(z, g), s.ssem, s.rsem.at[z, g], dev).start()
    def wait(s, z, g): wait_bytes(s.at(z, g), s.rsem.at[z, g])
    def start(s):
        t = s.t; g = t.g8(0, t.c)
        loop(1, t.Z, lambda k: s.send(t.z, g, t.dev(t.zk(k), t.y, t.x, t.c)))
        for dev in (t.p1, t.p2, t.sib): s.send(t.z, g, dev)
    def take(s, gi, lo=0, hi=None):
        t = s.t; g = t.g8(gi, t.c)
        to = {0: (t.p1, t.p2, t.sib), 1: (t.p2, t.sib)}.get(gi, (t.sib,))
        def f(k):
            z = t.zk(k); s.wait(z, g)
            for dev in to: s.send(z, g, dev)
        loop(lo, t.Z if hi is None else hi, f)
    def take_sib(s, gi):
        t = s.t; g = t.g8(gi, t.cb)
        loop(0, t.Z, lambda k: s.wait(t.zk(k), g))


class Scatter2:
    def __init__(s, t, at, ld, rc, r1, r2, rz, ss, rcs, r1s, r2s, rzs):
        s.t, s.at, s.ld, s.rc, s.r1, s.r2, s.rz, s.ss, s.rcs, s.r1s, s.r2s, s.rzs = t, at, ld, rc, r1, r2, rz, ss, rcs, r1s, r2s, rzs
        s.Z = t.Z
    def start(s, gi):
        t = s.t; Z = s.Z; g = t.g8(gi, t.cb)
        def f(k):
            j = (3 - gi) * Z + k
            rcopy(s.at(t.zk(k), g), s.rc.at[j], s.ss.at[0], s.rcs.at[j], t.sib).start()
        loop(0, Z, f)
    def stage_c(s, gi):
        t = s.t; Z = s.Z; g = t.g8(gi, t.c)
        def f(k):
            j = (3 - gi) * Z + k
            wait_bytes(s.rc.at[j], s.rcs.at[j])
            s.rc[j] = s.rc[j] + s.ld(t.zk(k), g)
            if gi >= 2: rcopy(s.rc.at[j], s.r1.at[j], s.ss.at[1], s.r1s.at[j], t.p2).start()
        loop(0, Z, f)
    def stage_1(s, h):
        t = s.t; Z = s.Z
        def f(k):
            j = h * Z + k
            wait_bytes(s.r1.at[j], s.r1s.at[j])
            s.r1[j] = s.r1[j] + s.rc[2 * Z + j]
            if h == 0: rcopy(s.r1.at[j], s.r2.at[k], s.ss.at[2], s.r2s.at[k], t.p1).start()
        loop(0, Z, f)
    def stage_2(s):
        t = s.t; Z = s.Z
        def f(k):
            wait_bytes(s.r2.at[k], s.r2s.at[k])
            s.r2[k] = s.r2[k] + s.r1[Z + k]
            rcopy(s.r2.at[k], s.rz.at[Z - k - 1], s.ss.at[3], s.rzs.at[Z - k - 1], t.dev(t.zk(k), t.y, t.x, t.c)).start()
        loop(1, Z, f)
        wait_bytes(s.r2.at[0], s.r2s.at[0])
    def final(s, out):
        Z = s.Z
        tot = s.r2[0].astype(f32) + s.r1[Z].astype(f32)
        for k in range(Z - 1):
            wait_bytes(s.rz.at[k], s.rzs.at[k])
            tot = tot + s.rz[k].astype(f32)
        out[...] = tot
    def wait_send(s):
        wait_bytes(s.rc, s.ss.at[0]); wait_bytes(s.r1, s.ss.at[1]); wait_bytes(s.r2, s.ss.at[2]); wait_bytes(s.rz, s.ss.at[3])


class Exchange:
    def __init__(s, t, src, dst, sbulk, dbulk, ssem, rsem, lsem):
        s.t, s.src, s.dst, s.sbulk, s.dbulk, s.ssem, s.rsem, s.lsem = t, src, dst, sbulk, dbulk, ssem, rsem, lsem
    def start(s):
        t = s.t
        pltpu.make_async_copy(s.src(t.me), s.dst(t.me), s.lsem).start()
        def f(k):
            d = lax.rem(t.me + k, t.N)
            rcopy(s.src(d), s.dst(t.me), s.ssem, s.rsem, t.flat(d)).start()
        loop(1, t.N, f)
    def wait_recv(s):
        pltpu.make_async_copy(s.src(s.t.me), s.dst(s.t.me), s.lsem).wait()
        wait_bytes(s.dbulk, s.rsem)
    def wait_send(s): wait_bytes(s.sbulk, s.ssem)


def rows_of(ref, n):
    return lambda d: ref.at[pl.ds(pl.multiple_of(d * n, n), n)]


def attn_fwd2(qkv_ref, ps, o_ref, lo, hi):
    QB = 256
    def pair(t, carry):
        oq = pl.multiple_of(t * 128, 128); ok = pl.multiple_of(768 + t * 128, 128); ov = pl.multiple_of(1536 + t * 128, 128)
        for i in range(len(ps)):
            kl = (i + 1) * QB
            q = lane_masks(qkv_ref[i * QB:kl, pl.ds(oq, 128)])
            k = qkv_ref[0:kl, pl.ds(ok, 128)]
            v = lane_masks(qkv_ref[0:kl, pl.ds(ov, 128)])
            got = []
            for h in range(2):
                s = dot_nt(q[h], k)
                row = lax.broadcasted_iota(jnp.int32, s.shape, 0) + i * QB
                col = lax.broadcasted_iota(jnp.int32, s.shape, 1)
                s = jnp.where(row >= col, s, -1e30)
                m = jnp.max(s, axis=-1, keepdims=True)
                e = jnp.exp2((s - m) * (attn_multiplier * LOG2E))
                pr = (e * (1.0 / jnp.sum(e, axis=-1, keepdims=True))).astype(bf16)
                ps[i][2 * t + h] = pr
                got.append(pr)
            o_ref[i * QB:kl, pl.ds(oq, 128)] = dot_nn(jnp.concatenate(got, 1), jnp.concatenate(v, 0)).astype(bf16)
        return carry
    lax.fori_loop(lo, hi, pair, 0)


def attn_bwd2(qkv_ref, ps, do_ref, cos_ref, sin_ref, lo, hi):
    QB = 256
    def pair(t, carry):
        oq = pl.multiple_of(t * 128, 128); ok = pl.multiple_of(768 + t * 128, 128); ov = pl.multiple_of(1536 + t * 128, 128)
        dkt = None; dvt = None
        for i in range(len(ps)):
            kl = (i + 1) * QB; r = slice(i * QB, kl)
            q = lane_masks(qkv_ref[r, pl.ds(oq, 128)])
            k = lane_masks(qkv_ref[0:kl, pl.ds(ok, 128)])
            v = qkv_ref[0:kl, pl.ds(ov, 128)]
            do = lane_masks(do_ref[r, pl.ds(oq, 128)])
            dss = []; pls = []
            for h in range(2):
                pb = ps[i][2 * t + h]
                p = pb.astype(f32)
                pd = p * dot_nt(do[h], v)
                dss.append((pd - p * jnp.sum(pd, axis=-1, keepdims=True)).astype(bf16)); pls.append(pb)
            dq = dot_nn(jnp.concatenate(dss, 1), jnp.concatenate(k, 0)) * attn_multiplier
            a = dot_tn(jnp.concatenate(q, 0), jnp.concatenate(dss, 0))
            b = dot_tn(jnp.concatenate(do, 0), jnp.concatenate(pls, 0))
            qkv_ref[r, pl.ds(oq, 128)] = (dq * cos_ref[r, :] - swap_halves(dq) * sin_ref[r, :]).astype(bf16)
            if dkt is None: dkt, dvt = a, b
            else:
                w = dkt.shape[1]
                dkt = jnp.concatenate([dkt + a[:, :w], a[:, w:]], 1); dvt = jnp.concatenate([dvt + b[:, :w], b[:, w:]], 1)
        dk = dkt.T * attn_multiplier
        qkv_ref[:, pl.ds(ok, 128)] = (dk * cos_ref[...] - swap_halves(dk) * sin_ref[...]).astype(bf16)
        qkv_ref[:, pl.ds(ov, 128)] = dvt.T.astype(bf16)
        return carry
    lax.fori_loop(lo, hi, pair, 0)


def mid2(n, cg, hs_ref, b2_ref, dn2_ref, g_ref, db1_ref, gg_ref):
    gg_ref[...] = jnp.zeros_like(gg_ref)
    def body(r, o):
        row = lax.broadcasted_iota(jnp.int32, (RB, 768), 0) + o
        hs = hs_ref[r, :]
        dy = cg[r, :].astype(f32)
        cg[r, :] = jnp.where(row < n, hs + b2_ref[r, :], 0.0).astype(bf16)
        inv = norm_block(hs, None)
        dn = dn2_ref[r, :]
        q = dn * g_ref[1:2, :]
        gg_ref[1:2, :] += jnp.sum(hs * inv * dn, axis=0, keepdims=True)
        dh = dy + (inv * q - hs * inv * inv * inv * jnp.mean(hs * q, axis=-1, keepdims=True))
        hs_ref[r, :] = dh
        db1_ref[r, :] = dh.astype(bf16)
    rows_loop(hs_ref.shape[0], body)


def all_kernel(nf, nd, perm, lens, tok, cot0, gm, am, fm, cos_ref, sin_ref,
               oo, io, ggo, ao, fo,
               xg, cg, cst, wa, wf, gt, gg, gains, ggb, gb, ggr,
               n1, qkv, p0, p1, o, hs, n2, b2, dn2, gatt, gff,
               arc, ar1, ar2, arz, frc, fr1, fr2, frz,
               ss, rs, ls, ags, fgs, ass, fss, acs, a1s, a2s, azs, fcs, f1s, f2s, fzs):
    t = Topo2(nf, nd)
    N, Z = t.N, t.Z
    L = xg.shape[0]; pos = L // N; ra = wa.shape[0] // N; gl = gm.shape[1]; R = wf.shape[2]
    ps = (p0, p1)
    row_at = lambda ref: (lambda z, g: ref.at[pl.ds(pl.multiple_of((z * 8 + g) * ra, ra), ra)])
    blk_at = lambda ref: (lambda z, g: ref.at[z * 8 + g])
    most = lambda ref: ref.at[pl.ds(0, L - pos)]
    wa[pl.ds(pl.multiple_of(t.me * ra, ra), ra), :] = am[...].astype(bf16)
    wf[t.me] = fm[...].astype(bf16)
    gt[...] = jnp.zeros_like(gt)
    gt[0:2, 0:gl] = gm[...].astype(bf16).astype(f32)
    gg[t.me] = gt[...]
    barrier_all(t)
    A = Gather2(t, row_at(wa), ss.at[3], ags)
    F = Gather2(t, blk_at(wf), ss.at[4], fgs)
    tk = Exchange(t, lambda d: tok.at[d], rows_of(xg, pos), most(xg), most(xg), ss.at[0], rs.at[0], ls.at[0])
    ct = Exchange(t, rows_of(cst, pos), rows_of(cg, pos), most(cg), most(cg), ss.at[1], rs.at[1], ls.at[1])
    A.start()
    tk.start()
    def gs(k): rcopy(gt, gg.at[t.me], ss.at[2], rs.at[2], t.flat(lax.rem(t.me + k, N))).start()
    loop(1, N, gs)
    def pm(i): cst[pl.ds(pl.multiple_of(i * pos, pos), pos), :] = cot0[perm[i]]
    loop(0, N, pm)
    A.take(0, 1)
    F.start()
    A.take(1)
    A.take(2); A.take(3)
    F.take(0, 1)
    for gi in range(4): A.take_sib(gi)
    tk.wait_recv()
    wait_bytes(gg.at[pl.ds(0, N - 1)], rs.at[2])
    tot = jnp.zeros((8, 768), f32)
    for d in range(N):
        wide = jnp.concatenate([gg[d], jnp.zeros((8, 640), f32)], 1)
        tot = tot + (pltpu.roll(wide, d * gl, 1) if d else wide)
    gains[...] = tot
    phase_norm1(xg, gains, n1)
    phase_qkv(n1, wa, cos_ref, sin_ref, qkv)
    F.take(1)
    ct.start()
    attn_fwd2(qkv, ps, o, 0, 3)
    F.take(2)
    attn_fwd2(qkv, ps, o, 3, 6)
    phase_wo_norm2(o, wa, xg, gains, hs, n2)
    F.take(3)
    ct.wait_recv()
    n = lens[t.me]
    def mask(r, of):
        row = lax.broadcasted_iota(jnp.int32, (RB, 768), 0) + of
        cg[r, :] = jnp.where(row < n, cg[r, :].astype(f32), 0.0).astype(bf16)
    rows_loop(L, mask)
    SA = Scatter2(t, row_at(gatt), lambda z, g: gatt[pl.ds(pl.multiple_of((z * 8 + g) * ra, ra), ra), :], arc, ar1, ar2, arz, ass, acs, a1s, a2s, azs)
    SF = Scatter2(t, blk_at(gff), lambda z, g: gff[z * 8 + g], frc, fr1, fr2, frz, fss, fcs, f1s, f2s, fzs)
    def tile(i):
        gi = i // 2
        par = lax.rem(lax.rem(i, 2) + i // 6, 2)
        cc = t.c + par * (1 - 2 * t.c)
        g = t.g8(gi, cc)
        @pl.when(par == 1)
        def _(): F.take_sib(gi)
        wg, wu, wd = (jnp.concatenate([wf[z * 8 + g, j] for z in range(Z)], 0) for j in range(3))
        nv = n2[...]
        ga = dot_nt(nv, wg); u = dot_nt(nv, wu)
        da = dot_nt(cg[...], wd)
        sg = 1.0 / (1.0 + jnp.exp2(ga * (-LOG2E)))
        silu = ga * sg
        a = (silu * u).astype(bf16)
        dg = (da * u * (sg * (1.0 + ga * (1.0 - sg)))).astype(bf16)
        du = (da * silu).astype(bf16)
        bb = dot_nn(a, wd)
        dn = dot_nn(dg, wg) + dot_nn(du, wu)
        @pl.when(i == 0)
        def _():
            b2[...] = bb; dn2[...] = dn
        @pl.when(i > 0)
        def _():
            b2[...] += bb; dn2[...] += dn
        for j, (lhs, rhs) in enumerate(((dg, nv), (du, nv), (a, cg[...]))):
            w = dot_tn(lhs, rhs).astype(bf16)
            for z in range(Z): gff[z * 8 + g, j] = w[z * R:(z + 1) * R]
        @pl.when(par == 1)
        def _(): SF.start(gi)
    loop(0, 8, tile)
    mid2(n, cg, hs, b2, dn2, gains, n2, ggb)
    ox = Exchange(t, rows_of(cg, pos), lambda d: oo.at[d], most(cg), oo.at[pl.ds(0, N - 1)], ss.at[5], rs.at[3], ls.at[3])
    ix = Exchange(t, rows_of(n1, pos), lambda d: io.at[d], most(n1), io.at[pl.ds(0, N - 1)], ss.at[6], rs.at[4], ls.at[4])
    SF.stage_c(3); SF.stage_c(2)
    ox.start()
    ct.wait_send()
    phase_wo_back(n2, o, wa, cst, gatt)
    SF.stage_c(1); SF.stage_c(0)
    attn_bwd2(qkv, ps, cst, cos_ref, sin_ref, 0, 3)
    SF.stage_1(0)
    attn_bwd2(qkv, ps, cst, cos_ref, sin_ref, 3, 6)
    phase_wqkv_grad(qkv, n1, gatt)
    for gi in (3, 2, 1, 0): SA.start(gi)
    SF.stage_1(1)
    SF.stage_2()
    SA.stage_c(3); SA.stage_c(2)
    phase_dn1(qkv, wa, xg, gains, hs, n1, ggb)
    ix.start()
    for d in range(N):
        v = ggb[...]
        gb[d] = (pltpu.roll(v, 768 - d * gl, 1) if d else v)[:, 0:128]
    ggr[t.me] = gb[t.me]
    def gsend(k):
        d = lax.rem(t.me + k, N)
        rcopy(gb.at[d], ggr.at[t.me], ss.at[7], rs.at[5], t.flat(d)).start()
    loop(1, N, gsend)
    SA.stage_c(1); SA.stage_c(0)
    SA.stage_1(0); SA.stage_1(1); SA.stage_2()
    SF.final(fo)
    wait_bytes(ggr.at[pl.ds(0, N - 1)], rs.at[5])
    tot = ggr[0]
    for d in range(1, N): tot = tot + ggr[d]
    ggo[...] = tot
    SA.final(ao)
    ox.wait_recv(); ix.wait_recv()
    tk.wait_send(); ox.wait_send(); ix.wait_send()
    wait_bytes(gg.at[pl.ds(0, N - 1)], ss.at[2]); wait_bytes(ggr.at[pl.ds(0, N - 1)], ss.at[7])
    wait_bytes(wa.at[pl.ds(0, (N - 1) * ra)], ss.at[3])
    wait_bytes(wf.at[pl.ds(0, N - 1)], ss.at[4])
    SF.wait_send(); SA.wait_send()


def all_call(perm, lens, tok, cot, gm, am, fm, C, S):
    nf, nd = lax.axis_size("fsdp"), lax.axis_size("dp"); N = nf * nd; Z = nf // 2
    pos, D = tok.shape[1:]; L = pos * N; ra = am.shape[0]; R = fm.shape[1]
    anyv = pl.BlockSpec(memory_space=pl.ANY); V = pl.BlockSpec(memory_space=pltpu.VMEM); SM = pl.BlockSpec(memory_space=pltpu.SMEM)
    sd = jax.ShapeDtypeStruct; Q = pltpu.SemaphoreType.DMA
    vm = lambda *s, dt=bf16: pltpu.VMEM(s, dt)
    return pl.pallas_call(functools.partial(all_kernel, nf, nd),
        out_shape=(sd(tok.shape, bf16), sd(tok.shape, bf16), sd((8, 128), f32), sd((ra, D), f32), sd((3, R, D), f32)),
        in_specs=[SM, SM, anyv, V, V, V, V, V, V], out_specs=(anyv, anyv, V, V, V),
        scratch_shapes=[vm(L, D), vm(L, D), vm(L, D), vm(N * ra, D), vm(N, 3, R, D), vm(8, 128, dt=f32), vm(N, 8, 128, dt=f32), vm(8, D, dt=f32),
                        vm(8, D, dt=f32), vm(N, 8, 128, dt=f32), vm(N, 8, 128, dt=f32),
                        vm(L, D), vm(L, 3 * D), vm(H, 256, 256), vm(H, 256, 512), vm(L, D), vm(L, D, dt=f32), vm(L, D), vm(L, D, dt=f32), vm(L, D, dt=f32),
                        vm(N * ra, D), vm(N, 3, R, D)]
                       + [vm(n, *sh) for sh in ((ra, D), (3, R, D)) for n in (4 * Z, 2 * Z, Z, Z - 1)]
                       + [Q((8,)), Q((6,)), Q((5,)), Q((Z, 8)), Q((Z, 8)), Q((4,)), Q((4,))] + [Q((n,)) for _ in range(2) for n in (4 * Z, 2 * Z, Z, Z - 1)],
        compiler_params=pltpu.CompilerParams(collective_id=2, has_side_effects=True, vmem_limit_bytes=64 * 2**20))(perm, lens, tok, cot, gm, am, fm, C, S)


def update(w, q, m, v, decay, mo, vo, wo):
    m2 = beta_first * m + (1.0 - beta_first) * q
    v2 = beta_second * v + (1.0 - beta_second) * q * q
    mo[...] = m2
    vo[...] = v2
    new = w - learning_rate * ((m2 / (1.0 - beta_first**STEP)) / (jnp.sqrt(v2 / (1.0 - beta_second**STEP)) + adam_epsilon) + decay * w)
    wo[...] = new
    return new


def last_kernel(slot, oo, io, gs, ag, fg, am, amm, amv, fm, fmm, fmv, gm, gmm, gmv,
                out, iout, ago, fgo, ggo, amo, avo, fmo, fvo, gmo, gvo, awo, fwo, gup, ac, fc):
    N = oo.shape[0]; gl = gm.shape[1]
    def pm(j): out[j] = oo[slot[j]]
    loop(0, N, pm)
    iout[...] = io[...]
    ago[...] = ag[...]
    fgo[...] = fg[...]
    q = gs[0:2, 0:gl]
    ggo[...] = q
    ac[...] = update(am[...], ag[...], amm[...], amv[...], weight_decay, amo, avo, awo).astype(bf16)
    fc[...] = update(fm[...], fg[...], fmm[...], fmv[...], weight_decay, fmo, fvo, fwo).astype(bf16)
    w = gm[...]
    gup[...] = update(w, q, gmm[...], gmv[...], 0.0, gmo, gvo, gup) - w


def last_call(slot, oo, io, gs, ag, fg, am, amm, amv, fm, fmm, fmv, gm, gmm, gmv):
    V = pl.BlockSpec(memory_space=pltpu.VMEM); SM = pl.BlockSpec(memory_space=pltpu.SMEM)
    sd = lambda a, dt=None: jax.ShapeDtypeStruct(a.shape, dt or a.dtype)
    return pl.pallas_call(last_kernel, in_specs=[SM] + [V] * 14, out_specs=(V,) * 16,
        out_shape=(sd(oo), sd(io), sd(am), sd(fm), sd(gm), sd(am), sd(am), sd(fm), sd(fm), sd(gm), sd(gm), sd(am), sd(fm), sd(gm), sd(am, bf16), sd(fm, bf16)),
        compiler_params=pltpu.CompilerParams(vmem_limit_bytes=48 * 2**20))(slot, oo, io, gs, ag, fg, am, amm, amv, fm, fmm, fmv, gm, gmm, gmv)


def local_one(tokens, cotangent, lengths, device_sequence, slot_device, attention_master, feedforward_master, gains_master,
              attention_mean, attention_square, feedforward_mean, feedforward_square, gains_mean, gains_square):
    N = lax.axis_size(AX)
    counter = jnp.arange(N, dtype=jnp.int32)
    slot_sequence = jnp.sum(jnp.where(slot_device[:, None] == counter[None, :], device_sequence[None, :], 0), axis=1)
    slot_of_sequence = jnp.sum(jnp.where(slot_sequence[:, None] == counter[None, :], counter[:, None], 0), axis=0)
    tr = lambda a: a.transpose(1, 0, 2)
    C, S = tables(tokens.shape[1] * N)
    oo, io, gs, ag, fg = all_call(slot_of_sequence, lengths, tokens, cotangent, gains_master, attention_master, tr(feedforward_master), jnp.asarray(C), jnp.asarray(S))
    r = list(last_call(slot_sequence, oo, io, gs, ag, fg, attention_master, attention_mean, attention_square,
                       tr(feedforward_master), tr(feedforward_mean), tr(feedforward_square), gains_master, gains_mean, gains_square))
    for i in (3, 7, 8, 12, 15): r[i] = tr(r[i])
    return tuple(r)


def solution(mesh):
    t, r, f, g = P(None, AX, None), P(AX, None), P(AX, None, None), P(None, AX)
    in_specs = (t, t, P(), P(), P(), r, f, g, r, r, f, f, g, g)
    out_specs = (t, t, r, f, g, r, r, f, f, g, g, r, f, g, r, f)
    n = mesh.shape["fsdp"] * mesh.shape["dp"]
    body = local_one if 512 // n % 16 == 0 and 3072 // n % 16 == 0 else local
    return jax.shard_map(body, mesh=mesh, in_specs=in_specs, out_specs=out_specs, check_vma=False)
```

```python
import functools
import jax, jax.numpy as jnp, numpy as np
from jax import lax
from jax.experimental import pallas as pl
from jax.experimental.pallas import tpu as pltpu
H=12; KVH=12; HD=64; STEP=4
norm_epsilon=1e-05; attn_multiplier=0.125; rope_theta=10000.0
f32=jnp.float32; bf16=jnp.bfloat16
LOG2E=1.4426950408889634

def dot_nt(a,b):
    return lax.dot_general(a,b,(((1,),(1,)),((),())),preferred_element_type=f32)
def dot_nn(a,b):
    return lax.dot_general(a,b,(((1,),(0,)),((),())),preferred_element_type=f32)
def dot_tn(a,b):
    return lax.dot_general(a,b,(((0,),(0,)),((),())),preferred_element_type=f32)

def tables(length):
    half=HD//2
    freq=(np.float32(rope_theta)**(-(np.arange(half,dtype=np.float32)*np.float32(2.0))/np.float32(HD))).astype(np.float32)
    ang=(np.arange(length,dtype=np.float32)[:,None]*freq[None,:]).astype(np.float32)
    c=np.cos(ang.astype(np.float64)).astype(np.float32); s=np.sin(ang.astype(np.float64)).astype(np.float32)
    C=np.concatenate([c,c,c,c],1); S=np.concatenate([-s,s,-s,s],1)
    return C,S

RB=64
def rows_loop(length, body):
    def it(i,carry):
        body(pl.ds(pl.multiple_of(i*RB,RB),RB), i*RB)
        return carry
    lax.fori_loop(0,length//RB,it,0)

def norm_block(xv, gain):
    inv=lax.rsqrt(jnp.mean(xv*xv,axis=-1,keepdims=True)+norm_epsilon)
    return inv

def swap_halves(x):
    lane=lax.broadcasted_iota(jnp.int32,x.shape,1)
    return jnp.where(lax.rem(lane,64)<32, pltpu.roll(x,96,1), pltpu.roll(x,32,1))

def phase_norm1(x_ref,g_ref,n1_ref):
    L=x_ref.shape[0]
    def body(r,_):
        xv=x_ref[r,:].astype(f32)
        inv=norm_block(xv,None)
        n1_ref[r,:]=(xv*inv*g_ref[0:1,:]).astype(bf16)
    rows_loop(L,body)

def phase_qkv(n1_ref,w_ref,cos_ref,sin_ref,qkv_ref):
    def rt(n,carry):
        o=pl.multiple_of(n*256,256)
        p=dot_nt(n1_ref[...],w_ref[pl.ds(o,256),:])
        for j in range(2):
            x=p[:,128*j:128*j+128]
            qkv_ref[:,pl.ds(pl.multiple_of(o+128*j,128),128)]=(x*cos_ref[...]+swap_halves(x)*sin_ref[...]).astype(bf16)
        return carry
    lax.fori_loop(0,6,rt,0)
    def vt(n,carry):
        o=pl.multiple_of(n*256,256)
        qkv_ref[:,pl.ds(o,256)]=dot_nt(n1_ref[...],w_ref[pl.ds(o,256),:]).astype(bf16)
        return carry
    lax.fori_loop(6,9,vt,0)

def lane_masks(a):
    lane=lax.broadcasted_iota(jnp.int32,a.shape,1)
    z=jnp.zeros_like(a)
    return jnp.where(lane<64,a,z), jnp.where(lane<64,z,a)

def phase_attn_fwd(qkv_ref,p_ref,o_ref):
    L=qkv_ref.shape[0]; QB=256
    def pair(t,carry):
        oq=pl.multiple_of(t*128,128); ok=pl.multiple_of(768+t*128,128); ov=pl.multiple_of(1536+t*128,128)
        for i in range(L//QB):
            kl=(i+1)*QB
            q=lane_masks(qkv_ref[i*QB:(i+1)*QB,pl.ds(oq,128)])
            k=qkv_ref[0:kl,pl.ds(ok,128)]
            v=lane_masks(qkv_ref[0:kl,pl.ds(ov,128)])
            ps=[]
            for h in range(2):
                s=dot_nt(q[h],k)
                row=lax.broadcasted_iota(jnp.int32,s.shape,0)+i*QB
                col=lax.broadcasted_iota(jnp.int32,s.shape,1)
                s=jnp.where(row>=col,s,-1e30)
                m=jnp.max(s,axis=-1,keepdims=True)
                e=jnp.exp2((s-m)*(attn_multiplier*LOG2E))
                pr=(e*(1.0/jnp.sum(e,axis=-1,keepdims=True))).astype(bf16)
                p_ref[2*t+h,i*QB:(i+1)*QB,0:kl]=pr
                ps.append(pr)
            o_ref[i*QB:(i+1)*QB,pl.ds(oq,128)]=dot_nn(jnp.concatenate(ps,1),jnp.concatenate(v,0)).astype(bf16)
        return carry
    lax.fori_loop(0,H//2,pair,0)

def phase_wo_norm2(o_ref,w_ref,x_ref,g_ref,hs_ref,n2_ref):
    L=x_ref.shape[0]; R=128
    def it(i,carry):
        r=pl.ds(pl.multiple_of(i*R,R),R)
        hs=x_ref[r,:].astype(f32)+dot_nn(o_ref[r,:],w_ref[2304:3072,:])
        hs_ref[r,:]=hs
        inv=norm_block(hs,None)
        n2_ref[r,:]=(hs*inv*g_ref[1:2,:]).astype(bf16)
        return carry
    lax.fori_loop(0,L//R,it,0)

def phase_ff(n2_ref,db2_ref,wff_ref,gff_ref,b2_ref,dn2_ref):
    sh=wff_ref.shape[2]; per=256//sh; nt=wff_ref.shape[0]//per
    def tile(t,carry):
        sl=pl.ds(t*per,per)
        wg=wff_ref[sl,0].reshape(256,768); wu=wff_ref[sl,1].reshape(256,768); wd=wff_ref[sl,2].reshape(256,768)
        n2=n2_ref[...]
        g=dot_nt(n2,wg); u=dot_nt(n2,wu)
        da=dot_nt(db2_ref[...],wd)
        sg=1.0/(1.0+jnp.exp2(g*(-LOG2E)))
        silu=g*sg
        a=(silu*u).astype(bf16)
        dg=(da*u*(sg*(1.0+g*(1.0-sg)))).astype(bf16)
        du=(da*silu).astype(bf16)
        b2=dot_nn(a,wd)
        dn=dot_nn(dg,wg)+dot_nn(du,wu)
        @pl.when(t==0)
        def _():
            b2_ref[...]=b2; dn2_ref[...]=dn
        @pl.when(t>0)
        def _():
            b2_ref[...]+=b2; dn2_ref[...]+=dn
        gff_ref[sl,0]=dot_tn(dg,n2).astype(bf16).reshape(per,sh,768)
        gff_ref[sl,1]=dot_tn(du,n2).astype(bf16).reshape(per,sh,768)
        gff_ref[sl,2]=dot_tn(a,db2_ref[...]).astype(bf16).reshape(per,sh,768)
        return carry
    lax.fori_loop(0,nt,tile,0)

def phase_mid(len_ref,c_ref,hs_ref,b2_ref,dn2_ref,g_ref,out_ref,dhs_ref,db1_ref,gg_ref):
    L=hs_ref.shape[0]
    n=len_ref[0]
    gg_ref[...]=jnp.zeros_like(gg_ref)
    def body(r,o):
        row=lax.broadcasted_iota(jnp.int32,(RB,768),0)+o
        hs=hs_ref[r,:]
        out_ref[r,:]=jnp.where(row<n,hs+b2_ref[r,:],0.0).astype(bf16)
        dy=jnp.where(row<n,c_ref[r,:].astype(f32),0.0)
        inv=norm_block(hs,None)
        dn=dn2_ref[r,:]
        q=dn*g_ref[1:2,:]
        gg_ref[1:2,:]+=jnp.sum(hs*inv*dn,axis=0,keepdims=True)
        dh=dy+(inv*q-hs*inv*inv*inv*jnp.mean(hs*q,axis=-1,keepdims=True))
        dhs_ref[r,:]=dh
        db1_ref[r,:]=dh.astype(bf16)
    rows_loop(L,body)

def phase_db2(len_ref,c_ref,db2_ref):
    n=len_ref[0]
    def body(r,o):
        row=lax.broadcasted_iota(jnp.int32,(RB,768),0)+o
        db2_ref[r,:]=jnp.where(row<n,c_ref[r,:].astype(f32),0.0).astype(bf16)
    rows_loop(c_ref.shape[0],body)

def phase_wo_back(db1_ref,o_ref,w_ref,do_ref,gatt_ref):
    def it(n,carry):
        o=pl.multiple_of(n*256,256)
        do_ref[:,pl.ds(o,256)]=dot_nt(db1_ref[...],w_ref[pl.ds(pl.multiple_of(2304+o,256),256),:]).astype(bf16)
        gatt_ref[pl.ds(pl.multiple_of(2304+o,256),256),:]=dot_tn(o_ref[:,pl.ds(o,256)],db1_ref[...]).astype(bf16)
        return carry
    lax.fori_loop(0,3,it,0)

def phase_attn_bwd(qkv_ref,p_ref,do_ref,cos_ref,sin_ref,dp_ref):
    L=qkv_ref.shape[0]; QB=256
    def pair(t,carry):
        oq=pl.multiple_of(t*128,128); ok=pl.multiple_of(768+t*128,128); ov=pl.multiple_of(1536+t*128,128)
        dkt=None; dvt=None
        for i in range(L//QB):
            kl=(i+1)*QB; r=slice(i*QB,(i+1)*QB)
            q=lane_masks(qkv_ref[r,pl.ds(oq,128)])
            k=lane_masks(qkv_ref[0:kl,pl.ds(ok,128)])
            v=qkv_ref[0:kl,pl.ds(ov,128)]
            do=lane_masks(do_ref[r,pl.ds(oq,128)])
            dss=[]; pls=[]
            for h in range(2):
                pb=p_ref[2*t+h,r,0:kl]
                p=pb.astype(f32)
                if i<L//QB:
                    row=lax.broadcasted_iota(jnp.int32,p.shape,0)+i*QB
                dpr=dot_nt(do[h],v)
                pd=p*dpr
                ds=(pd-p*jnp.sum(pd,axis=-1,keepdims=True)).astype(bf16)
                dss.append(ds); pls.append(pb)
            dq=dot_nn(jnp.concatenate(dss,1),jnp.concatenate(k,0))*attn_multiplier
            c=cos_ref[r,:]; s=sin_ref[r,:]
            dp_ref[r,pl.ds(oq,128)]=(dq*c-swap_halves(dq)*s).astype(bf16)
            a=dot_tn(jnp.concatenate(q,0),jnp.concatenate(dss,0))
            b=dot_tn(jnp.concatenate(do,0),jnp.concatenate(pls,0))
            if dkt is None: dkt,dvt=a,b
            else:
                w=dkt.shape[1]
                dkt=jnp.concatenate([dkt+a[:,:w],a[:,w:]],1); dvt=jnp.concatenate([dvt+b[:,:w],b[:,w:]],1)
        dk=dkt.T*attn_multiplier
        dp_ref[:,pl.ds(ok,128)]=(dk*cos_ref[...]-swap_halves(dk)*sin_ref[...]).astype(bf16)
        dp_ref[:,pl.ds(ov,128)]=dvt.T.astype(bf16)
        return carry
    lax.fori_loop(0,H//2,pair,0)

def phase_dn1(dp_ref,w_ref,x_ref,g_ref,dhs_ref,in_ref,gg_ref):
    L=x_ref.shape[0]; R=128
    def it(i,carry):
        r=pl.ds(pl.multiple_of(i*R,R),R)
        dn=dot_nn(dp_ref[r,:],w_ref[0:2304,:])
        xv=x_ref[r,:].astype(f32)
        inv=norm_block(xv,None)
        gg_ref[0:1,:]+=jnp.sum(xv*inv*dn,axis=0,keepdims=True)
        q=dn*g_ref[0:1,:]
        in_ref[r,:]=(dhs_ref[r,:]+(inv*q-xv*inv*inv*inv*jnp.mean(xv*q,axis=-1,keepdims=True))).astype(bf16)
        return carry
    lax.fori_loop(0,L//R,it,0)

def phase_wqkv_grad(dp_ref,n1_ref,gatt_ref):
    def it(n,carry):
        o=pl.multiple_of(n*256,256)
        gatt_ref[pl.ds(o,256),:]=dot_tn(dp_ref[:,pl.ds(o,256)],n1_ref[...]).astype(bf16)
        return carry
    lax.fori_loop(0,9,it,0)

def k2_kernel(len_ref,x_ref,c_ref,watt_ref,wff_ref,g_ref,cos_ref,sin_ref,
              out_ref,in_ref,gatt_ref,gff_ref,gg_ref,
              n1,qkv,pm,o,hs,n2,db2,b2,dn2,dhs,db1,do,dpj):
    phase_norm1(x_ref,g_ref,n1)
    phase_qkv(n1,watt_ref,cos_ref,sin_ref,qkv)
    phase_attn_fwd(qkv,pm,o)
    phase_wo_norm2(o,watt_ref,x_ref,g_ref,hs,n2)
    phase_db2(len_ref,c_ref,db2)
    phase_ff(n2,db2,wff_ref,gff_ref,b2,dn2)
    phase_mid(len_ref,c_ref,hs,b2,dn2,g_ref,out_ref,dhs,db1,gg_ref)
    phase_wo_back(db1,o,watt_ref,do,gatt_ref)
    phase_attn_bwd(qkv,pm,do,cos_ref,sin_ref,dpj)
    phase_dn1(dpj,watt_ref,x_ref,g_ref,dhs,in_ref,gg_ref)
    phase_wqkv_grad(dpj,n1,gatt_ref)

def k2(length,x,c,watt,wff,gains,cos,sin,kern=k2_kernel):
    L,D=x.shape
    V=pl.BlockSpec(memory_space=pltpu.VMEM)
    vm=lambda *s,dt=bf16: pltpu.VMEM(s,dt)
    return pl.pallas_call(kern,
        out_shape=(jax.ShapeDtypeStruct((L,D),bf16),jax.ShapeDtypeStruct((L,D),bf16),jax.ShapeDtypeStruct(watt.shape,bf16),jax.ShapeDtypeStruct(wff.shape,bf16),jax.ShapeDtypeStruct((8,D),f32)),
        in_specs=[pl.BlockSpec(memory_space=pltpu.SMEM)]+[V]*7,out_specs=(V,)*5,
        scratch_shapes=[vm(L,D),vm(L,3*D),vm(H,L,L),vm(L,D),vm(L,D,dt=f32),vm(L,D),vm(L,D),vm(L,D,dt=f32),vm(L,D,dt=f32),vm(L,D,dt=f32),vm(L,D),vm(L,D),vm(L,3*D)],
        compiler_params=pltpu.CompilerParams(vmem_limit_bytes=63*2**20),
        )(length,x,c,watt,wff,gains,cos,sin)
MESH=pl.DeviceIdType.MESH

class Topo:
    def __init__(s, nf, nd):
        assert nd==4 and nf%2==0
        s.Z=nf//2; s.N=nf*nd
        f=lax.axis_index("fsdp"); d=lax.axis_index("dp")
        s.z=f//2; s.y=lax.rem(f,2); s.x=d//2; s.c=lax.rem(d,2)
        s.me=f*4+d
        c=s.c
        s.y1=s.y+c*(1-2*s.y); s.x1=s.x+(1-c)*(1-2*s.x)
        s.y2=s.y+(1-c)*(1-2*s.y); s.x2=s.x+c*(1-2*s.x)
        s.yb=1-s.y; s.xb=1-s.x; s.cb=1-c
    def slot(s,z,y,x,c): return ((z*2+y)*2+x)*2+c
    def dev(s,z,y,x,c): return (z*2+y, x*2+c)
    def flat(s,i): return (i//4, lax.rem(i,4))
    def zk(s,k): return lax.rem(s.z+k,s.Z)
    @property
    def p1(s): return s.dev(s.z,s.y1,s.x1,s.c)
    @property
    def p2(s): return s.dev(s.z,s.y2,s.x2,s.c)
    @property
    def sib(s): return s.dev(s.z,s.y,s.x,s.cb)

def loop(lo,hi,body):
    lax.fori_loop(lo,hi,lambda i,c:(body(i),c)[1],0)

def rcopy(src,dst,ssem,rsem,dev):
    return pltpu.make_async_remote_copy(src_ref=src,dst_ref=dst,send_sem=ssem,recv_sem=rsem,device_id=dev,device_id_type=MESH)

def wait_bytes(ref,sem):
    pltpu.make_async_copy(ref,ref,sem).wait()

def barrier_all(t):
    b=pltpu.get_barrier_semaphore()
    def sig(k): pl.semaphore_signal(b,inc=1,device_id=t.flat(lax.rem(t.me+k,t.N)),device_id_type=MESH)
    loop(1,t.N,sig)
    pl.semaphore_wait(b,t.N-1)

class A2A:
    def __init__(s,t,src,dst,ssem,rsem,lsem): s.t,s.src,s.dst,s.ssem,s.rsem,s.lsem=t,src,dst,ssem,rsem,lsem
    def start(s):
        t=s.t
        pltpu.make_async_copy(s.src.at[t.me],s.dst.at[t.me],s.lsem).start()
        def f(k):
            d=lax.rem(t.me+k,t.N)
            rcopy(s.src.at[d],s.dst.at[t.me],s.ssem,s.rsem,t.flat(d)).start()
        loop(1,t.N,f)
    def wait_recv(s):
        n=s.t.N-1
        pltpu.make_async_copy(s.src.at[s.t.me],s.dst.at[s.t.me],s.lsem).wait()
        wait_bytes(s.dst.at[pl.ds(0,n)],s.rsem)
    def wait_send(s):
        wait_bytes(s.src.at[pl.ds(0,s.t.N-1)],s.ssem)

class Gather:
    def __init__(s,t,src,dst,ssem,rsem,lsem): s.t,s.src,s.dst,s.ssem,s.rsem,s.lsem=t,src,dst,ssem,rsem,lsem
    def send(s,slot,dev,src=None):
        rcopy(s.dst.at[slot] if src is None else src,s.dst.at[slot],s.ssem,s.rsem.at[slot],dev).start()
    def wait(s,slot):
        wait_bytes(s.dst.at[slot],s.rsem.at[slot])
    def start(s):
        t=s.t
        pltpu.make_async_copy(s.src,s.dst.at[t.me],s.lsem).start()
        for dev in (t.p1,t.p2,t.sib): s.send(t.me,dev,s.src)
        loop(1,t.Z,lambda k: s.send(t.me,t.dev(t.zk(k),t.y,t.x,t.c),s.src))
    def phase1(s):
        t=s.t
        def f(k):
            sl=t.slot(t.zk(k),t.y,t.x,t.c); s.wait(sl)
            for dev in (t.p1,t.p2,t.sib): s.send(sl,dev)
        loop(1,t.Z,f)
    def phase2(s):
        t=s.t
        def f(k):
            sl=t.slot(t.zk(k),t.y1,t.x1,t.c); s.wait(sl)
            for dev in (t.p2,t.sib): s.send(sl,dev)
        loop(0,t.Z,f)
    def phase3(s):
        t=s.t
        for y,x in ((t.y2,t.x2),(t.yb,t.xb)):
            def f(k):
                sl=t.slot(t.zk(k),y,x,t.c); s.wait(sl); s.send(sl,t.sib)
            loop(0,t.Z,f)
    def phase4(s):
        t=s.t
        for y,x in ((0,0),(0,1),(1,0),(1,1)):
            loop(0,t.Z,lambda k: s.wait(t.slot(t.zk(k),y,x,t.cb)))
    def finish(s):
        t=s.t
        pltpu.make_async_copy(s.src,s.dst.at[t.me],s.lsem).wait()
        wait_bytes(s.dst.at[pl.ds(0,t.N-1)],s.ssem)

def k1_kernel(nf,nd,perm,tok,cot0,gn,att,ff,xg,cg,gg,wa,wf,cot,ss,rs,ls,ars,frs):
    t=Topo(nf,nd)
    barrier_all(t)
    tk=A2A(t,tok,xg,ss.at[0],rs.at[0],ls.at[0])
    ct=A2A(t,cot,cg,ss.at[1],rs.at[1],ls.at[1])
    A=Gather(t,att,wa,ss.at[3],ars,ls.at[3]); F=Gather(t,ff,wf,ss.at[4],frs,ls.at[4])
    pltpu.make_async_copy(gn,gg.at[t.me],ls.at[2]).start()
    def gs(k): rcopy(gn,gg.at[t.me],ss.at[2],rs.at[2],t.flat(lax.rem(t.me+k,t.N))).start()
    loop(1,t.N,gs)
    A.start()
    tk.start()
    def pm(i): cot[i]=cot0[perm[i]]
    loop(0,t.N,pm)
    A.phase1()
    F.start()
    A.phase2()
    F.phase1()
    A.phase3()
    F.phase2()
    ct.start()
    A.phase4()
    F.phase3(); F.phase4()
    tk.wait_recv(); ct.wait_recv()
    pltpu.make_async_copy(gn,gg.at[t.me],ls.at[2]).wait()
    wait_bytes(gg.at[pl.ds(0,t.N-1)],rs.at[2]); wait_bytes(gg.at[pl.ds(0,t.N-1)],ss.at[2])
    A.finish(); F.finish(); tk.wait_send(); ct.wait_send()

def k1(perm,tok,cot,gn,att,ff):
    nf,nd=lax.axis_size("fsdp"),lax.axis_size("dp"); N=nf*nd
    anyv=pl.BlockSpec(memory_space=pl.ANY); D=pltpu.SemaphoreType.DMA
    sd=jax.ShapeDtypeStruct
    return pl.pallas_call(functools.partial(k1_kernel,nf,nd),
        out_shape=(sd(tok.shape,tok.dtype),sd(cot.shape,cot.dtype),sd((N,)+gn.shape,gn.dtype),sd((N,)+att.shape,att.dtype),sd((N,)+ff.shape,ff.dtype)),
        in_specs=[pl.BlockSpec(memory_space=pltpu.SMEM),anyv,pl.BlockSpec(memory_space=pltpu.VMEM),anyv,anyv,anyv],out_specs=(anyv,)*5,
        scratch_shapes=[pltpu.VMEM(cot.shape,cot.dtype),D((5,)),D((5,)),D((5,)),D((N,)),D((N,))],
        compiler_params=pltpu.CompilerParams(collective_id=0,has_side_effects=True))(perm,tok,cot,gn,att,ff)

class Scatter:
    def __init__(s,t,g,rc,r1,r2,rz,ss,rcs,r1s,r2s,rzs):
        s.t,s.g,s.rc,s.r1,s.r2,s.rz,s.ss,s.rcs,s.r1s,s.r2s,s.rzs=t,g,rc,r1,r2,rz,ss,rcs,r1s,r2s,rzs
        s.Z=t.Z
    def groups(s,sibling):
        t=s.t
        if sibling:
            return ((t.yb,t.xb),(t.y1,t.x1),(t.y2,t.x2),(t.y,t.x))
        return ((t.yb,t.xb),(t.y2,t.x2),(t.y1,t.x1),(t.y,t.x))
    def start(s):
        t=s.t; Z=s.Z
        for gi,(y,x) in enumerate(s.groups(True)):
            def f(k):
                rcopy(s.g.at[t.slot(t.zk(k),y,x,t.cb)],s.rc.at[gi*Z+k],s.ss.at[0],s.rcs.at[gi*Z+k],t.sib).start()
            loop(0,Z,f)
    def stage_c(s):
        t=s.t; Z=s.Z
        for gi,(y,x) in enumerate(s.groups(False)):
            def f(k):
                j=gi*Z+k
                wait_bytes(s.rc.at[j],s.rcs.at[j])
                s.rc[j]=s.rc[j]+s.g[t.slot(t.zk(k),y,x,t.c)]
                if gi<2: rcopy(s.rc.at[j],s.r1.at[j],s.ss.at[1],s.r1s.at[j],t.p2).start()
            loop(0,Z,f)
    def stage_1(s):
        t=s.t; Z=s.Z
        for gi in range(2):
            def f(k):
                j=gi*Z+k
                wait_bytes(s.r1.at[j],s.r1s.at[j])
                s.r1[j]=s.r1[j]+s.rc[2*Z+j]
                if gi==0: rcopy(s.r1.at[j],s.r2.at[k],s.ss.at[2],s.r2s.at[k],t.p1).start()
            loop(0,Z,f)
    def stage_2(s):
        t=s.t; Z=s.Z
        def f(k):
            wait_bytes(s.r2.at[k],s.r2s.at[k])
            s.r2[k]=s.r2[k]+s.r1[Z+k]
            rcopy(s.r2.at[k],s.rz.at[Z-k-1],s.ss.at[3],s.rzs.at[Z-k-1],t.dev(t.zk(k),t.y,t.x,t.c)).start()
        loop(1,Z,f)
        wait_bytes(s.r2.at[0],s.r2s.at[0])
    def final(s,out):
        Z=s.Z
        tot=s.r2[0].astype(f32)+s.r1[Z].astype(f32)
        for k in range(Z-1):
            wait_bytes(s.rz.at[k],s.rzs.at[k])
            tot=tot+s.rz[k].astype(f32)
        out[...]=tot
    def wait_send(s):
        Z=s.Z
        wait_bytes(s.rc,s.ss.at[0])
        wait_bytes(s.r1,s.ss.at[1])
        wait_bytes(s.r2,s.ss.at[2])
        wait_bytes(s.rz,s.ss.at[3])

def k3_kernel(nf,nd,perm,orow,irow,gg,ga,gf,oo0,io,ggo,ao,fo,oo,ggr,arc,ar1,ar2,arz,frc,fr1,fr2,frz,ss,rs,ls,ass,fss,acs,a1s,a2s,azs,fcs,f1s,f2s,fzs):
    t=Topo(nf,nd)
    barrier_all(t)
    A=Scatter(t,ga,arc,ar1,ar2,arz,ass,acs,a1s,a2s,azs)
    F=Scatter(t,gf,frc,fr1,fr2,frz,fss,fcs,f1s,f2s,fzs)
    F.start(); A.start()
    pltpu.make_async_copy(gg.at[t.me],ggr.at[t.me],ls.at[2]).start()
    def gs(k):
        d=lax.rem(t.me+k,t.N)
        rcopy(gg.at[d],ggr.at[t.me],ss.at[2],rs.at[2],t.flat(d)).start()
    loop(1,t.N,gs)
    F.stage_c()
    o=A2A(t,orow,oo,ss.at[0],rs.at[0],ls.at[0])
    i=A2A(t,irow,io,ss.at[1],rs.at[1],ls.at[1])
    o.start()
    A.stage_c()
    i.start()
    F.stage_1(); F.stage_2()
    A.stage_1(); A.stage_2()
    pltpu.make_async_copy(gg.at[t.me],ggr.at[t.me],ls.at[2]).wait()
    wait_bytes(ggr.at[pl.ds(0,t.N-1)],rs.at[2]); wait_bytes(ggr.at[pl.ds(0,t.N-1)],ss.at[2])
    tot=ggr[0]
    for k in range(1,t.N): tot=tot+ggr[k]
    ggo[...]=tot
    F.final(fo); A.final(ao)
    o.wait_recv()
    def pm(j): oo0[j]=oo[perm[j]]
    loop(0,t.N,pm)
    i.wait_recv(); o.wait_send(); i.wait_send()
    F.wait_send(); A.wait_send()

def k3(perm,orow,irow,gg,ga,gf):
    nf,nd=lax.axis_size("fsdp"),lax.axis_size("dp"); N=nf*nd; Z=nf//2
    anyv=pl.BlockSpec(memory_space=pl.ANY); V=pl.BlockSpec(memory_space=pltpu.VMEM); D=pltpu.SemaphoreType.DMA
    sd=jax.ShapeDtypeStruct
    ash,fsh=ga.shape[1:],gf.shape[1:]
    vm=lambda n,sh: pltpu.VMEM((n,)+sh,bf16)
    return pl.pallas_call(functools.partial(k3_kernel,nf,nd),
        out_shape=(sd(orow.shape,bf16),sd(irow.shape,bf16),sd(gg.shape[1:],f32),sd(ash,f32),sd(fsh,f32)),
        in_specs=[pl.BlockSpec(memory_space=pltpu.SMEM),anyv,anyv,V,V,V],out_specs=(V,anyv,V,V,V),
        scratch_shapes=[pltpu.VMEM(orow.shape,bf16),pltpu.VMEM(gg.shape,f32)]+[vm(n,sh) for sh in (ash,fsh) for n in (4*Z,2*Z,Z,Z-1)]+[D((3,)),D((3,)),D((3,)),D((4,)),D((4,))]+[D((n,)) for _ in range(2) for n in (4*Z,2*Z,Z,Z-1)],
        compiler_params=pltpu.CompilerParams(collective_id=1,has_side_effects=True,vmem_limit_bytes=60*2**20))(perm,orow,irow,gg,ga,gf)


from jax.sharding import PartitionSpec as P
AX = ("fsdp", "dp")
beta_first = 0.5
beta_second = 0.5
learning_rate = 0.03
weight_decay = 0.1
adam_epsilon = 1e-08


def adam_update(master, gradient, first_moment, second_moment, decay):
    first_new = beta_first * first_moment + (1.0 - beta_first) * gradient
    second_new = beta_second * second_moment + (1.0 - beta_second) * gradient * gradient
    first_hat = first_new / (1.0 - beta_first**STEP)
    second_hat = second_new / (1.0 - beta_second**STEP)
    master_new = master - learning_rate * (
        first_hat / (jnp.sqrt(second_hat) + adam_epsilon) + decay * master
    )
    return (first_new, second_new, master_new)


def local(tokens, cotangent, lengths, device_sequence, slot_device, attention_master, feedforward_master, gains_master,
          attention_mean, attention_square, feedforward_mean, feedforward_square, gains_mean, gains_square):
    N = lax.axis_size(AX)
    me = lax.axis_index(AX)
    positions, width = tokens.shape[1], tokens.shape[2]
    length = positions * N
    gl = gains_master.shape[1]
    counter = jnp.arange(N, dtype=jnp.int32)
    slot_sequence = jnp.sum(jnp.where(slot_device[:, None] == counter[None, :], device_sequence[None, :], 0), axis=1)
    slot_of_sequence = jnp.sum(jnp.where(slot_sequence[:, None] == counter[None, :], counter[:, None], 0), axis=0)
    att_low = attention_master.astype(bf16)
    ff_low = feedforward_master.transpose(1, 0, 2).astype(bf16)
    gn = jnp.zeros((8, 128), f32).at[:2, :gl].set(gains_master.astype(bf16).astype(f32))
    xg, cg, gg, wa, wf = k1(slot_of_sequence, tokens, cotangent, gn, att_low, ff_low)
    gains = jnp.zeros((8, width), f32).at[:2].set(gg[:, :2, :gl].transpose(1, 0, 2).reshape(2, width))
    C, S = tables(length)
    orow, irow, gatt, gff, ggr = k2(jnp.sum(jnp.where(counter == me, lengths, 0))[None], xg.reshape(length, width), cg.reshape(length, width),
                                    wa.reshape(-1, width), wf, gains, jnp.asarray(C), jnp.asarray(S))
    gblocks = jnp.zeros((N, 8, 128), f32).at[:, :2, :gl].set(ggr[:2].reshape(2, N, gl).transpose(1, 0, 2))
    oo, io, gsum, ag, fg = k3(slot_sequence, orow.reshape(N, positions, width), irow.reshape(N, positions, width), gblocks,
                              gatt.reshape(N, -1, width), gff)
    output = oo
    attention_gradient = ag
    feedforward_gradient = fg.transpose(1, 0, 2)
    gains_gradient = gsum[:2, :gl]
    mean_attention, square_attention, master_attention = adam_update(
        attention_master, attention_gradient, attention_mean, attention_square, weight_decay)
    mean_feedforward, square_feedforward, master_feedforward = adam_update(
        feedforward_master, feedforward_gradient, feedforward_mean, feedforward_square, weight_decay)
    mean_gains, square_gains, master_gains = adam_update(gains_master, gains_gradient, gains_mean, gains_square, 0.0)
    return (output, io, attention_gradient, feedforward_gradient, gains_gradient, mean_attention, square_attention,
            mean_feedforward, square_feedforward, mean_gains, square_gains, master_attention, master_feedforward,
            master_gains - gains_master, master_attention.astype(bf16), master_feedforward.astype(bf16))


class Topo2(Topo):
    def __init__(s, nf, nd):
        super().__init__(nf, nd)
    def flip(s, gi, cc):
        a, b = lax.rem(gi, 2), gi // 2
        fx, fy = (1 - cc) * a + cc * b, (1 - cc) * b + cc * a
        return s.y + fy * (1 - 2 * s.y), s.x + fx * (1 - 2 * s.x)
    def g8(s, gi, cc):
        y, x = s.flip(gi, cc)
        return (y * 2 + x) * 2 + cc


class Gather2:
    def __init__(s, t, at, ssem, zsem, rsem): s.t, s.at, s.ssem, s.zsem, s.rsem = t, at, ssem, zsem, rsem
    def send(s, z, g, dev):
        rcopy(s.at(z, g), s.at(z, g), s.ssem, s.rsem.at[z, g], dev).start()
    def wait(s, z, g): wait_bytes(s.at(z, g), s.rsem.at[z, g])
    def along(s, z, g, side, f):
        t = s.t
        @pl.when((t.z + side >= 0) & (t.z + side < t.Z))
        def _(): f(rcopy(s.at(z, g), s.at(z, g), s.zsem.at[z, (side + 1) // 2], s.rsem.at[z, g], t.dev(t.z + side, t.y, t.x, t.c)))
    def start(s):
        t = s.t; g = t.g8(0, t.c)
        for side in (-1, 1): s.along(t.z, g, side, lambda c: c.start())
        for dev in (t.p1, t.p2, t.sib): s.send(t.z, g, dev)
    def sweep(s, lo, hi, f):
        t = s.t
        def step(j):
            @pl.when(t.z - j >= 0)
            def _(): f(t.z - j, -1)
            @pl.when(t.z + j < t.Z)
            def _(): f(t.z + j, 1)
        if lo == 0: f(t.z, 0)
        loop(max(lo, 1), hi, step)
    def take(s, gi, lo=0, hi=None):
        t = s.t; g = t.g8(gi, t.c)
        to = {0: (t.p1, t.p2, t.sib), 1: (t.p2, t.sib)}.get(gi, (t.sib,))
        def f(z, side):
            s.wait(z, g)
            if gi == 0: s.along(z, g, -side, lambda c: c.start())
            for dev in to: s.send(z, g, dev)
        s.sweep(lo, t.Z if hi is None else hi, f)
    def take_sib(s, gi, lo=0, hi=None):
        t = s.t; g = t.g8(gi, t.cb)
        s.sweep(lo, t.Z if hi is None else hi, lambda z, side: s.wait(z, g))
    def finish(s, bulk):
        t = s.t; g = t.g8(0, t.c)
        wait_bytes(bulk, s.ssem)
        for side in (-1, 1): s.along(t.z, g, side, lambda c: c.wait_send())
        s.sweep(1, t.Z, lambda z, side: s.along(z, g, -side, lambda c: c.wait_send()))


SEQ = ((0, 1), (1, 0), (0, 2), (1, 1), (2, 0), (0, 3), (1, 2), (2, 1), (3, 0), (1, 3), (2, 2), (3, 1), (2, 3), (3, 2), (3, 3))


class Scatter3:
    def __init__(s, t, at, ld, rc, r1, r2, rz, ss, rcs, r1s, r2s, rzs, zss):
        s.t, s.at, s.ld, s.rc, s.r1, s.r2, s.rz, s.ss, s.rcs, s.r1s, s.r2s, s.rzs, s.zss = t, at, ld, rc, r1, r2, rz, ss, rcs, r1s, r2s, rzs, zss
        s.Z = Z = t.Z
        s.order = [sorted(range(Z), key=lambda q: (-abs(q - z), (q > z) == (z < Z // 2))) for z in range(Z)]
    def zof(s, i):
        r = 0
        for z in range(s.Z): r = r + jnp.where(s.t.z == z, s.order[z][i], 0)
        return r
    def start(s, gi):
        t = s.t; Z = s.Z; g = t.g8(gi, t.cb)
        for i in range(Z):
            z = s.zof(i); j = (3 - gi) * Z + z
            rcopy(s.at(z, g), s.rc.at[j], s.ss.at[0], s.rcs.at[j], t.sib).start()
    def chip(s, z, gs):
        t = s.t; Z = s.Z
        for gi in gs:
            j = (3 - gi) * Z + z
            wait_bytes(s.rc.at[j], s.rcs.at[j])
            s.rc[j] = s.rc[j] + s.ld(z, t.g8(gi, t.c))
            if gi >= 2: rcopy(s.rc.at[j], s.r1.at[j], s.ss.at[1], s.r1s.at[j], t.p2).start()
    def first(s, z):
        t = s.t; Z = s.Z
        for h in range(2):
            j = h * Z + z
            wait_bytes(s.r1.at[j], s.r1s.at[j])
            s.r1[j] = s.r1[j] + s.rc[2 * Z + j]
            if h == 0: rcopy(s.r1.at[z], s.r2.at[z], s.ss.at[2], s.r2s.at[z], t.p1).start()
    def hop(s, z, side):
        t = s.t
        j = jnp.where((z == t.z + side) & (side < 0), s.Z, z)
        return rcopy(s.r2.at[z], s.rz.at[j], s.zss.at[z], s.rzs.at[j], t.dev(t.z + side, t.y, t.x, t.c))
    def second(s, z):
        t = s.t; Z = s.Z
        wait_bytes(s.r2.at[z], s.r2s.at[z])
        s.r2[z] = s.r2[z] + s.r1[Z + z]
    def line(s, z):
        t = s.t; Z = s.Z
        for side in (-1, 1):
            @pl.when((z - t.z) * side > 0)
            def _():
                @pl.when((t.z - side >= 0) & (t.z - side < Z))
                def _():
                    wait_bytes(s.rz.at[z], s.rzs.at[z])
                    s.r2[z] = s.r2[z] + s.rz[z]
                s.hop(z, side).start()
    def C(s, *ii):
        for i in ii: s.chip(s.zof(i), (3, 2, 1, 0))
    def F(s, *ii):
        for i in ii: s.first(s.zof(i))
    def S(s, *ii):
        for i in ii: s.second(s.zof(i)); s.line(s.zof(i))
    def total(s):
        t = s.t; Z = s.Z
        tot = s.r2[t.z].astype(f32)
        below = jnp.where(t.z > 0, 1.0, 0.0); above = jnp.where(t.z < Z - 1, 1.0, 0.0)
        @pl.when(t.z > 0)
        def _(): wait_bytes(s.rz.at[t.z], s.rzs.at[t.z])
        @pl.when(t.z == 0)
        def _(): s.rz[t.z] = jnp.zeros(s.rz.shape[1:], bf16)
        @pl.when(t.z < Z - 1)
        def _(): wait_bytes(s.rz.at[Z], s.rzs.at[Z])
        @pl.when(t.z == Z - 1)
        def _(): s.rz[Z] = jnp.zeros(s.rz.shape[1:], bf16)
        return tot + (s.rz[t.z].astype(f32) + s.rz[Z].astype(f32))
    def wait_send(s):
        t = s.t; Z = s.Z
        wait_bytes(s.rc, s.ss.at[0]); wait_bytes(s.r1, s.ss.at[1]); wait_bytes(s.r2, s.ss.at[2])
        def f(z):
            for side in (-1, 1):
                @pl.when((z - t.z) * side > 0)
                def _(): s.hop(z, side).wait_send()
        loop(0, Z, f)


class Exchange:
    def __init__(s, t, src, dst, sbulk, dbulk, ssem, rsem, lsem):
        s.t, s.src, s.dst, s.sbulk, s.dbulk, s.ssem, s.rsem, s.lsem = t, src, dst, sbulk, dbulk, ssem, rsem, lsem
        s.sent = 1
    def start(s): pltpu.make_async_copy(s.src(s.t.me), s.dst(s.t.me), s.lsem).start()
    def more(s, n):
        t = s.t
        def f(k):
            d = lax.rem(t.me + k, t.N)
            rcopy(s.src(d), s.dst(t.me), s.ssem, s.rsem, t.flat(d)).start()
        to = min(t.N, s.sent + n)
        if to > s.sent: loop(s.sent, to, f)
        s.sent = to
    def wait_recv(s):
        pltpu.make_async_copy(s.src(s.t.me), s.dst(s.t.me), s.lsem).wait()
        wait_bytes(s.dbulk, s.rsem)
    def wait_send(s): wait_bytes(s.sbulk, s.ssem)


def rows_of(ref, n):
    return lambda d: ref.at[pl.ds(pl.multiple_of(d * n, n), n)]


def attn_fwd2(qkv_ref, ps, o_ref, lo, hi):
    QB = 256
    def pair(t, carry):
        oq = pl.multiple_of(t * 128, 128); ok = pl.multiple_of(768 + t * 128, 128); ov = pl.multiple_of(1536 + t * 128, 128)
        for i in range(len(ps)):
            kl = (i + 1) * QB
            q = lane_masks(qkv_ref[i * QB:kl, pl.ds(oq, 128)])
            k = qkv_ref[0:kl, pl.ds(ok, 128)]
            v = lane_masks(qkv_ref[0:kl, pl.ds(ov, 128)])
            got = []
            for h in range(2):
                s = dot_nt(q[h], k)
                row = lax.broadcasted_iota(jnp.int32, s.shape, 0) + i * QB
                col = lax.broadcasted_iota(jnp.int32, s.shape, 1)
                s = jnp.where(row >= col, s, -1e30)
                m = jnp.max(s, axis=-1, keepdims=True)
                e = jnp.exp2((s - m) * (attn_multiplier * LOG2E))
                pr = (e * (1.0 / jnp.sum(e, axis=-1, keepdims=True))).astype(bf16)
                ps[i][2 * t + h] = pr
                got.append(pr)
            n = o_ref.shape[1]
            o_ref[i * QB // n:kl // n, :, pl.ds(oq, 128)] = dot_nn(jnp.concatenate(got, 1), jnp.concatenate(v, 0)).astype(bf16).reshape(QB // n, n, 128)
        return carry
    lax.fori_loop(lo, hi, pair, 0)


def attn_bwd2(qkv_ref, ps, do_ref, cos_ref, sin_ref, lo, hi):
    QB = 256
    def pair(t, carry):
        oq = pl.multiple_of(t * 128, 128); ok = pl.multiple_of(768 + t * 128, 128); ov = pl.multiple_of(1536 + t * 128, 128)
        dkt = None; dvt = None
        for i in range(len(ps)):
            kl = (i + 1) * QB; r = slice(i * QB, kl)
            q = lane_masks(qkv_ref[r, pl.ds(oq, 128)])
            k = lane_masks(qkv_ref[0:kl, pl.ds(ok, 128)])
            v = qkv_ref[0:kl, pl.ds(ov, 128)]
            do = lane_masks(do_ref[r, pl.ds(oq, 128)])
            dss = []; pls = []
            for h in range(2):
                pb = ps[i][2 * t + h]
                p = pb.astype(f32)
                pd = p * dot_nt(do[h], v)
                dss.append((pd - p * jnp.sum(pd, axis=-1, keepdims=True)).astype(bf16)); pls.append(pb)
            dq = dot_nn(jnp.concatenate(dss, 1), jnp.concatenate(k, 0)) * attn_multiplier
            a = dot_tn(jnp.concatenate(q, 0), jnp.concatenate(dss, 0))
            b = dot_tn(jnp.concatenate(do, 0), jnp.concatenate(pls, 0))
            qkv_ref[r, pl.ds(oq, 128)] = (dq * cos_ref[r, :] - swap_halves(dq) * sin_ref[r, :]).astype(bf16)
            if dkt is None: dkt, dvt = a, b
            else:
                w = dkt.shape[1]
                dkt = jnp.concatenate([dkt + a[:, :w], a[:, w:]], 1); dvt = jnp.concatenate([dvt + b[:, :w], b[:, w:]], 1)
        dk = dkt.T * attn_multiplier
        qkv_ref[:, pl.ds(ok, 128)] = (dk * cos_ref[...] - swap_halves(dk) * sin_ref[...]).astype(bf16)
        qkv_ref[:, pl.ds(ov, 128)] = dvt.T.astype(bf16)
        return carry
    lax.fori_loop(lo, hi, pair, 0)


def wo_norm2(o_ref, w_ref, x_ref, g_ref, hs_ref, n2_ref):
    L = x_ref.shape[0]; R = 128; n = o_ref.shape[1]
    def it(i, carry):
        r = pl.ds(pl.multiple_of(i * R, R), R)
        hs = x_ref[r, :].astype(f32) + dot_nn(o_ref[pl.ds(i * (R // n), R // n)].reshape(R, 768), w_ref[2304:3072, :])
        hs_ref[r, :] = hs
        n2_ref[r, :] = (hs * norm_block(hs, None) * g_ref[1:2, :]).astype(bf16)
        return carry
    lax.fori_loop(0, L // R, it, 0)


def wo_back2(db1_ref, o_ref, w_ref, do_ref, gatt_ref):
    def it(n, carry):
        o = pl.multiple_of(n * 256, 256); w = pl.ds(pl.multiple_of(2304 + o, 256), 256)
        do_ref[:, pl.ds(o, 256)] = dot_nt(db1_ref[...], w_ref[w, :]).astype(bf16)
        gatt_ref[w, :] = dot_tn(o_ref[:, :, pl.ds(o, 256)].reshape(-1, 256), db1_ref[...]).astype(bf16)
        return carry
    lax.fori_loop(0, 3, it, 0)


def mid2(n, cg, hs_ref, b2_ref, dn2_ref, g_ref, db1_ref, gg_ref):
    gg_ref[...] = jnp.zeros_like(gg_ref)
    def body(r, o):
        row = lax.broadcasted_iota(jnp.int32, (RB, 768), 0) + o
        hs = hs_ref[r, :]
        dy = cg[r, :].astype(f32)
        cg[r, :] = jnp.where(row < n, hs + b2_ref[r, :], 0.0).astype(bf16)
        inv = norm_block(hs, None)
        dn = dn2_ref[r, :]
        q = dn * g_ref[1:2, :]
        gg_ref[1:2, :] += jnp.sum(hs * inv * dn, axis=0, keepdims=True)
        dh = dy + (inv * q - hs * inv * inv * inv * jnp.mean(hs * q, axis=-1, keepdims=True))
        hs_ref[r, :] = dh
        db1_ref[r, :] = dh.astype(bf16)
    rows_loop(hs_ref.shape[0], body)


def all_kernel(nf, nd, perm, lens, tok, cot0, gm, am, fm, cos_ref, sin_ref,
               oo, io, ggo, ao, fo,
               xg, cg, cst, wa, wf, gt, gg, gains, ggb, gb, ggr,
               n1, qkv, p0, p1, o, hs, n2, b2, dn2, gatt, gff, cs, sn,
               arc, ar1, ar2, arz, frc, fr1, fr2, frz,
               ss, rs, ls, azs2, fzs2, ags, fgs, ass, fss, acs, a1s, a2s, azs, azq, fcs, f1s, f2s, fzs, fzq):
    t = Topo2(nf, nd)
    N, Z = t.N, t.Z
    L = xg.shape[0]; pos = L // N; ra = wa.shape[0] // N; gl = gm.shape[1]; R = wf.shape[2]
    ps = (p0, p1)
    row_at = lambda ref: (lambda z, g: ref.at[pl.ds(pl.multiple_of((z * 8 + g) * ra, ra), ra)])
    blk_at = lambda ref: (lambda z, g: ref.at[z * 8 + g])
    most = lambda ref: ref.at[pl.ds(0, L - pos)]
    f0 = b2.at[pl.ds(0, ra)], dn2.at[pl.ds(0, 3 * R)]
    near = [pltpu.make_async_copy(a, d, ls.at[5 + i]) for i, (a, d) in enumerate(((am, f0[0]), (fm, f0[1]), (cot0, o), (cos_ref, cs), (sin_ref, sn)))]
    for c in near: c.start()
    near[0].wait()
    wa[pl.ds(pl.multiple_of(t.me * ra, ra), ra), :] = f0[0][...].astype(bf16)
    near[1].wait()
    wf[t.me] = f0[1][...].astype(bf16).reshape(3, R, 768)
    gt[...] = jnp.zeros_like(gt)
    gt[0:2, 0:gl] = gm[...].astype(bf16).astype(f32)
    gg[t.me] = gt[...]
    barrier_all(t)
    A = Gather2(t, row_at(wa), ss.at[3], azs2, ags)
    F = Gather2(t, blk_at(wf), ss.at[4], fzs2, fgs)
    tk = Exchange(t, lambda d: tok.at[d], rows_of(xg, pos), most(xg), most(xg), ss.at[0], rs.at[0], ls.at[0])
    ct = Exchange(t, rows_of(cst, pos), rows_of(cg, pos), most(cg), most(cg), ss.at[1], rs.at[1], ls.at[1])
    def takes(X, lo, hi, *more):
        for g, d in SEQ[lo:hi]:
            X.take(g, d, d + 1)
            for e, k in more: e.more(k)
    tk.start()
    A.start()
    tk.more(8)
    takes(A, 0, 3, (tk, 3))
    F.start()
    near[2].wait()
    def pm(i): cst[pl.ds(pl.multiple_of(i * pos, pos), pos), :] = o[perm[i]]
    loop(0, N, pm)
    ct.start()
    def gs(k): rcopy(gt, gg.at[t.me], ss.at[2], rs.at[2], t.flat(lax.rem(t.me + k, N))).start()
    loop(1, N, gs)
    takes(A, 3, 15, (tk, 3))
    tk.more(N)
    for gi in range(4): A.take_sib(gi)
    tk.wait_recv()
    wait_bytes(gg.at[pl.ds(0, N - 1)], rs.at[2])
    tot = jnp.zeros((8, 768), f32)
    for d in range(N):
        wide = jnp.concatenate([gg[d], jnp.zeros((8, 640), f32)], 1)
        tot = tot + (pltpu.roll(wide, d * gl, 1) if d else wide)
    gains[...] = tot
    takes(F, 0, 2, (ct, 3))
    phase_norm1(xg, gains, n1)
    takes(F, 2, 4, (ct, 3))
    near[3].wait(); near[4].wait()
    phase_qkv(n1, wa, cs, sn, qkv)
    takes(F, 4, 6, (ct, 4))
    def fwd(i):
        attn_fwd2(qkv, ps, o, i, i + 1)
    loop(0, 2, fwd)
    takes(F, 6, 8, (ct, 4))
    loop(2, 4, fwd)
    takes(F, 8, 10, (ct, 4))
    loop(4, 6, fwd)
    ct.more(N)
    wo_norm2(o, wa, xg, gains, hs, n2)
    takes(F, 10, 11)
    ct.wait_recv()
    n = lens[t.me]
    def mask(r, of):
        row = lax.broadcasted_iota(jnp.int32, (RB, 768), 0) + of
        cg[r, :] = jnp.where(row < n, cg[r, :].astype(f32), 0.0).astype(bf16)
    rows_loop(L, mask)
    SA = Scatter3(t, row_at(gatt), lambda z, g: gatt[pl.ds(pl.multiple_of((z * 8 + g) * ra, ra), ra), :], arc, ar1, ar2, arz, ass, acs, a1s, a2s, azs, azq)
    SF = Scatter3(t, blk_at(gff), lambda z, g: gff[z * 8 + g], frc, fr1, fr2, frz, fss, fcs, f1s, f2s, fzs, fzq)
    def tile(i):
        gi = i // 2
        par = lax.rem(lax.rem(i, 2) + i // 6, 2)
        cc = t.c + par * (1 - 2 * t.c)
        g = t.g8(gi, cc)
        for k, lo, hi in ((1, 11, 12), (2, 12, 13), (3, 13, 14), (4, 14, 15)):
            @pl.when(i == k)
            def _(): takes(F, lo, hi)
        @pl.when(par == 1)
        def _(): F.take_sib(gi)
        wg, wu, wd = (jnp.concatenate([wf[z * 8 + g, j] for z in range(Z)], 0) for j in range(3))
        nv = n2[...]
        ga = dot_nt(nv, wg); u = dot_nt(nv, wu)
        da = dot_nt(cg[...], wd)
        sg = 1.0 / (1.0 + jnp.exp2(ga * (-LOG2E)))
        silu = ga * sg
        a = (silu * u).astype(bf16)
        dg = (da * u * (sg * (1.0 + ga * (1.0 - sg)))).astype(bf16)
        du = (da * silu).astype(bf16)
        bb = dot_nn(a, wd)
        dn = dot_nn(dg, wg) + dot_nn(du, wu)
        @pl.when(i == 0)
        def _():
            b2[...] = bb; dn2[...] = dn
        @pl.when(i > 0)
        def _():
            b2[...] += bb; dn2[...] += dn
        for j, (lhs, rhs) in enumerate(((dg, nv), (du, nv), (a, cg[...]))):
            w = dot_tn(lhs, rhs).astype(bf16)
            for z in range(Z): gff[z * 8 + g, j] = w[z * R:(z + 1) * R]
        @pl.when(par == 1)
        def _(): SF.start(gi)
    loop(0, 8, tile)
    ox = Exchange(t, rows_of(cg, pos), lambda d: oo.at[d], most(cg), oo.at[pl.ds(0, N - 1)], ss.at[5], rs.at[3], ls.at[3])
    ix = Exchange(t, rows_of(n1, pos), lambda d: io.at[d], most(n1), io.at[pl.ds(0, N - 1)], ss.at[6], rs.at[4], ls.at[4])
    SF.C(0, 1)
    mid2(n, cg, hs, b2, dn2, gains, n2, ggb)
    ox.start(); ox.more(8)
    ct.wait_send()
    wo_back2(n2, o, wa, cst, gatt)
    ox.more(8)
    def back(i):
        attn_bwd2(qkv, ps, cst, cs, sn, i, i + 1)
    loop(0, 1, back)
    SF.F(0); SF.C(2); ox.more(8)
    loop(1, 4, back)
    SF.F(1); SF.S(0); SF.C(3); ox.more(N)
    loop(4, 6, back)
    phase_wqkv_grad(qkv, n1, gatt)
    for gi in (3, 2, 1, 0): SA.start(gi)
    SF.F(2); SF.S(1)
    phase_dn1(qkv, wa, xg, gains, hs, n1, ggb)
    SA.C(0, 1)
    ix.start(); ix.more(8)
    for d in range(N):
        v = ggb[...]
        gb[d] = (pltpu.roll(v, 768 - d * gl, 1) if d else v)[:, 0:128]
    ggr[t.me] = gb[t.me]
    def gsend(k):
        d = lax.rem(t.me + k, N)
        rcopy(gb.at[d], ggr.at[t.me], ss.at[7], rs.at[5], t.flat(d)).start()
    loop(1, N, gsend)
    SF.F(3); SF.S(2)
    SA.F(0); SA.C(2); ix.more(8)
    SF.S(3)
    SA.F(1); SA.S(0); SA.C(3); ix.more(N)
    SA.F(2); SA.S(1)
    f0[1][...] = SF.total().reshape(3 * R, 768)
    far = [pltpu.make_async_copy(f0[1], fo, ls.at[6]), pltpu.make_async_copy(f0[0], ao, ls.at[5])]
    far[0].start()
    SA.F(3); SA.S(2); SA.S(3)
    wait_bytes(ggr.at[pl.ds(0, N - 1)], rs.at[5])
    tot = ggr[0]
    for d in range(1, N): tot = tot + ggr[d]
    ggo[...] = tot
    f0[0][...] = SA.total()
    far[1].start()
    ox.wait_recv(); ix.wait_recv()
    for c in far: c.wait()
    tk.wait_send(); ox.wait_send(); ix.wait_send()
    wait_bytes(gg.at[pl.ds(0, N - 1)], ss.at[2]); wait_bytes(ggr.at[pl.ds(0, N - 1)], ss.at[7])
    A.finish(wa.at[pl.ds(0, 7 * Z * ra)])
    F.finish(wf.at[pl.ds(0, 7 * Z)])
    SF.wait_send(); SA.wait_send()


def all_call(perm, lens, tok, cot, gm, am, fm, C, S):
    nf, nd = lax.axis_size("fsdp"), lax.axis_size("dp"); N = nf * nd; Z = nf // 2
    pos, D = tok.shape[1:]; L = pos * N; ra = am.shape[0]; R = fm.shape[0] // 3
    hbm = pl.BlockSpec(memory_space=pltpu.HBM); V = pl.BlockSpec(memory_space=pltpu.VMEM); SM = pl.BlockSpec(memory_space=pltpu.SMEM)
    sd = jax.ShapeDtypeStruct; Q = pltpu.SemaphoreType.DMA
    vm = lambda *s, dt=bf16: pltpu.VMEM(s, dt)
    return pl.pallas_call(functools.partial(all_kernel, nf, nd),
        out_shape=(sd(tok.shape, bf16), sd(tok.shape, bf16), sd((8, 128), f32), sd((ra, D), f32), sd((3 * R, D), f32)),
        in_specs=[SM, SM, hbm, hbm, V, hbm, hbm, hbm, hbm], out_specs=(hbm, hbm, V, hbm, hbm),
        scratch_shapes=[vm(L, D), vm(L, D), vm(L, D), vm(N * ra, D), vm(N, 3, R, D), vm(8, 128, dt=f32), vm(N, 8, 128, dt=f32), vm(8, D, dt=f32),
                        vm(8, D, dt=f32), vm(N, 8, 128, dt=f32), vm(N, 8, 128, dt=f32),
                        vm(L, D), vm(L, 3 * D), vm(H, 256, 256), vm(H, 256, 512), vm(N, pos, D), vm(L, D, dt=f32), vm(L, D), vm(L, D, dt=f32), vm(L, D, dt=f32),
                        vm(N * ra, D), vm(N, 3, R, D), vm(L, 128, dt=f32), vm(L, 128, dt=f32)]
                       + [vm(n, *sh) for sh in ((ra, D), (3, R, D)) for n in (4 * Z, 2 * Z, Z, Z + 1)]
                       + [Q((8,)), Q((6,)), Q((10,)), Q((Z, 2)), Q((Z, 2)), Q((Z, 8)), Q((Z, 8)), Q((4,)), Q((4,))] + [Q((n,)) for _ in range(2) for n in (4 * Z, 2 * Z, Z, Z + 1, Z)],
        compiler_params=pltpu.CompilerParams(collective_id=2, has_side_effects=True, vmem_limit_bytes=64 * 2**20))(perm, lens, tok, cot, gm, am, fm, C, S)


def update(w, q, m, v, decay, mo, vo, wo):
    m2 = beta_first * m + (1.0 - beta_first) * q
    v2 = beta_second * v + (1.0 - beta_second) * q * q
    mo[...] = m2
    vo[...] = v2
    new = w - learning_rate * ((m2 / (1.0 - beta_first**STEP)) / (jnp.sqrt(v2 / (1.0 - beta_second**STEP)) + adam_epsilon) + decay * w)
    wo[...] = new
    return new


def last_kernel(slot, *refs):
    ins, outs, iv, ov, isem, osem = refs[:14], refs[14:30], refs[30:44], refs[44:57], refs[57], refs[58]
    oo, io, gs, ag, fg = ins[:5]
    N = oo.shape[0]; gl = ins[11].shape[1]
    order = [8, 9, 10, 4, 5, 6, 7, 3, 1, 11, 12, 13, 2, 0]
    src = {k: pltpu.make_async_copy(ins[k], iv[i], isem.at[i]) for i, k in enumerate(order)}
    val = {k: iv[i] for i, k in enumerate(order)}
    for k in order: src[k].start()
    done = []
    def copy(a, b, i):
        c = pltpu.make_async_copy(a, b, osem.at[i]); c.start(); done.append(c)
    put = {k: i for i, k in enumerate((0, 4, 5, 6, 7, 8, 9, 10, 11, 12, 13, 14, 15))}
    def out(k): copy(ov[put[k]], outs[k], k)
    at = lambda k: ov[put[k]]
    for w, q, m, v, ks in ((8, 4, 9, 10, (7, 8, 12, 15)), (5, 3, 6, 7, (5, 6, 11, 14))):
        for k in (w, q, m, v): src[k].wait()
        new = update(val[w][...], val[q][...], val[m][...], val[v][...], weight_decay, at(ks[0]), at(ks[1]), at(ks[2]))
        at(ks[3])[...] = new.astype(bf16)
        for k in ks: out(k)
        copy(val[q], outs[q - 1], q - 1)
    src[1].wait()
    copy(val[1], outs[1], 1)
    for k in (11, 12, 13, 2): src[k].wait()
    q = val[2][0:2, 0:gl]
    w = val[11][...]
    at(4)[...] = q
    at(13)[...] = update(w, q, val[12][...], val[13][...], 0.0, at(9), at(10), at(13)) - w
    for k in (4, 9, 10, 13): out(k)
    src[0].wait()
    def pm(j): at(0)[j] = val[0][slot[j]]
    loop(0, N, pm)
    out(0)
    for c in done: c.wait()


def last_call(slot, oo, io, gs, ag, fg, am, amm, amv, fm, fmm, fmv, gm, gmm, gmv):
    A = pl.BlockSpec(memory_space=pltpu.HBM); SM = pl.BlockSpec(memory_space=pltpu.SMEM)
    sd = lambda a, dt=None: jax.ShapeDtypeStruct(a.shape, dt or a.dtype)
    args = (oo, io, gs, ag, fg, am, amm, amv, fm, fmm, fmv, gm, gmm, gmv)
    res = (sd(oo), sd(io), sd(am), sd(fm), sd(gm), sd(am), sd(am), sd(fm), sd(fm), sd(gm), sd(gm), sd(am), sd(fm), sd(gm), sd(am, bf16), sd(fm, bf16))
    vm = lambda a: pltpu.VMEM(a.shape, a.dtype)
    return pl.pallas_call(last_kernel, in_specs=[SM] + [A] * 14, out_specs=(A,) * 16, out_shape=res,
        scratch_shapes=[vm(args[k]) for k in (8, 9, 10, 4, 5, 6, 7, 3, 1, 11, 12, 13, 2, 0)] + [vm(res[k]) for k in (0, 4, 5, 6, 7, 8, 9, 10, 11, 12, 13, 14, 15)]
                       + [pltpu.SemaphoreType.DMA((14,)), pltpu.SemaphoreType.DMA((16,))],
        compiler_params=pltpu.CompilerParams(vmem_limit_bytes=64 * 2**20))(slot, *args)


def local_one(tokens, cotangent, lengths, device_sequence, slot_device, attention_master, feedforward_master, gains_master,
              attention_mean, attention_square, feedforward_mean, feedforward_square, gains_mean, gains_square):
    N = lax.axis_size(AX)
    counter = jnp.arange(N, dtype=jnp.int32)
    slot_sequence = jnp.sum(jnp.where(slot_device[:, None] == counter[None, :], device_sequence[None, :], 0), axis=1)
    slot_of_sequence = jnp.sum(jnp.where(slot_sequence[:, None] == counter[None, :], counter[:, None], 0), axis=0)
    tr = lambda a: a.transpose(1, 0, 2)
    C, S = tables(tokens.shape[1] * N)
    width = tokens.shape[2]
    oo, io, gs, ag, fg = all_call(slot_of_sequence, lengths, tokens, cotangent, gains_master, attention_master,
                                  tr(feedforward_master).reshape(-1, width), jnp.asarray(C), jnp.asarray(S))
    fg = fg.reshape(3, -1, width)
    r = list(last_call(slot_sequence, oo, io, gs, ag, fg, attention_master, attention_mean, attention_square,
                       tr(feedforward_master), tr(feedforward_mean), tr(feedforward_square), gains_master, gains_mean, gains_square))
    for i in (3, 7, 8, 12, 15): r[i] = tr(r[i])
    return tuple(r)


def solution(mesh):
    t, r, f, g = P(None, AX, None), P(AX, None), P(AX, None, None), P(None, AX)
    in_specs = (t, t, P(), P(), P(), r, f, g, r, r, f, f, g, g)
    out_specs = (t, t, r, f, g, r, r, f, f, g, g, r, f, g, r, f)
    n = mesh.shape["fsdp"] * mesh.shape["dp"]
    body = local_one if 512 // n % 16 == 0 and 3072 // n % 16 == 0 else local
    return jax.shard_map(body, mesh=mesh, in_specs=in_specs, out_specs=out_specs, check_vma=False)
```

```python
import functools
import jax, jax.numpy as jnp, numpy as np
from jax import lax
from jax.experimental import pallas as pl
from jax.experimental.pallas import tpu as pltpu
H=12; KVH=12; HD=64; STEP=4
norm_epsilon=1e-05; attn_multiplier=0.125; rope_theta=10000.0
f32=jnp.float32; bf16=jnp.bfloat16
LOG2E=1.4426950408889634

def dot_nt(a,b):
    return lax.dot_general(a,b,(((1,),(1,)),((),())),preferred_element_type=f32)
def dot_nn(a,b):
    return lax.dot_general(a,b,(((1,),(0,)),((),())),preferred_element_type=f32)
def dot_tn(a,b):
    return lax.dot_general(a,b,(((0,),(0,)),((),())),preferred_element_type=f32)

def tables(length):
    half=HD//2
    freq=(np.float32(rope_theta)**(-(np.arange(half,dtype=np.float32)*np.float32(2.0))/np.float32(HD))).astype(np.float32)
    ang=(np.arange(length,dtype=np.float32)[:,None]*freq[None,:]).astype(np.float32)
    c=np.cos(ang.astype(np.float64)).astype(np.float32); s=np.sin(ang.astype(np.float64)).astype(np.float32)
    C=np.concatenate([c,c,c,c],1); S=np.concatenate([-s,s,-s,s],1)
    return C,S

RB=64
def rows_loop(length, body):
    def it(i,carry):
        body(pl.ds(pl.multiple_of(i*RB,RB),RB), i*RB)
        return carry
    lax.fori_loop(0,length//RB,it,0)

def norm_block(xv, gain):
    inv=lax.rsqrt(jnp.mean(xv*xv,axis=-1,keepdims=True)+norm_epsilon)
    return inv

def swap_halves(x):
    lane=lax.broadcasted_iota(jnp.int32,x.shape,1)
    return jnp.where(lax.rem(lane,64)<32, pltpu.roll(x,96,1), pltpu.roll(x,32,1))

def phase_norm1(x_ref,g_ref,n1_ref):
    L=x_ref.shape[0]
    def body(r,_):
        xv=x_ref[r,:].astype(f32)
        inv=norm_block(xv,None)
        n1_ref[r,:]=(xv*inv*g_ref[0:1,:]).astype(bf16)
    rows_loop(L,body)

def phase_qkv(n1_ref,w_ref,cos_ref,sin_ref,qkv_ref):
    def rt(n,carry):
        o=pl.multiple_of(n*256,256)
        p=dot_nt(n1_ref[...],w_ref[pl.ds(o,256),:])
        for j in range(2):
            x=p[:,128*j:128*j+128]
            qkv_ref[:,pl.ds(pl.multiple_of(o+128*j,128),128)]=(x*cos_ref[...]+swap_halves(x)*sin_ref[...]).astype(bf16)
        return carry
    lax.fori_loop(0,6,rt,0)
    def vt(n,carry):
        o=pl.multiple_of(n*256,256)
        qkv_ref[:,pl.ds(o,256)]=dot_nt(n1_ref[...],w_ref[pl.ds(o,256),:]).astype(bf16)
        return carry
    lax.fori_loop(6,9,vt,0)

def lane_masks(a):
    lane=lax.broadcasted_iota(jnp.int32,a.shape,1)
    z=jnp.zeros_like(a)
    return jnp.where(lane<64,a,z), jnp.where(lane<64,z,a)

def phase_attn_fwd(qkv_ref,p_ref,o_ref):
    L=qkv_ref.shape[0]; QB=256
    def pair(t,carry):
        oq=pl.multiple_of(t*128,128); ok=pl.multiple_of(768+t*128,128); ov=pl.multiple_of(1536+t*128,128)
        for i in range(L//QB):
            kl=(i+1)*QB
            q=lane_masks(qkv_ref[i*QB:(i+1)*QB,pl.ds(oq,128)])
            k=qkv_ref[0:kl,pl.ds(ok,128)]
            v=lane_masks(qkv_ref[0:kl,pl.ds(ov,128)])
            ps=[]
            for h in range(2):
                s=dot_nt(q[h],k)
                row=lax.broadcasted_iota(jnp.int32,s.shape,0)+i*QB
                col=lax.broadcasted_iota(jnp.int32,s.shape,1)
                s=jnp.where(row>=col,s,-1e30)
                m=jnp.max(s,axis=-1,keepdims=True)
                e=jnp.exp2((s-m)*(attn_multiplier*LOG2E))
                pr=(e*(1.0/jnp.sum(e,axis=-1,keepdims=True))).astype(bf16)
                p_ref[2*t+h,i*QB:(i+1)*QB,0:kl]=pr
                ps.append(pr)
            o_ref[i*QB:(i+1)*QB,pl.ds(oq,128)]=dot_nn(jnp.concatenate(ps,1),jnp.concatenate(v,0)).astype(bf16)
        return carry
    lax.fori_loop(0,H//2,pair,0)

def phase_wo_norm2(o_ref,w_ref,x_ref,g_ref,hs_ref,n2_ref):
    L=x_ref.shape[0]; R=128
    def it(i,carry):
        r=pl.ds(pl.multiple_of(i*R,R),R)
        hs=x_ref[r,:].astype(f32)+dot_nn(o_ref[r,:],w_ref[2304:3072,:])
        hs_ref[r,:]=hs
        inv=norm_block(hs,None)
        n2_ref[r,:]=(hs*inv*g_ref[1:2,:]).astype(bf16)
        return carry
    lax.fori_loop(0,L//R,it,0)

def phase_ff(n2_ref,db2_ref,wff_ref,gff_ref,b2_ref,dn2_ref):
    sh=wff_ref.shape[2]; per=256//sh; nt=wff_ref.shape[0]//per
    def tile(t,carry):
        sl=pl.ds(t*per,per)
        wg=wff_ref[sl,0].reshape(256,768); wu=wff_ref[sl,1].reshape(256,768); wd=wff_ref[sl,2].reshape(256,768)
        n2=n2_ref[...]
        g=dot_nt(n2,wg); u=dot_nt(n2,wu)
        da=dot_nt(db2_ref[...],wd)
        sg=1.0/(1.0+jnp.exp2(g*(-LOG2E)))
        silu=g*sg
        a=(silu*u).astype(bf16)
        dg=(da*u*(sg*(1.0+g*(1.0-sg)))).astype(bf16)
        du=(da*silu).astype(bf16)
        b2=dot_nn(a,wd)
        dn=dot_nn(dg,wg)+dot_nn(du,wu)
        @pl.when(t==0)
        def _():
            b2_ref[...]=b2; dn2_ref[...]=dn
        @pl.when(t>0)
        def _():
            b2_ref[...]+=b2; dn2_ref[...]+=dn
        gff_ref[sl,0]=dot_tn(dg,n2).astype(bf16).reshape(per,sh,768)
        gff_ref[sl,1]=dot_tn(du,n2).astype(bf16).reshape(per,sh,768)
        gff_ref[sl,2]=dot_tn(a,db2_ref[...]).astype(bf16).reshape(per,sh,768)
        return carry
    lax.fori_loop(0,nt,tile,0)

def phase_mid(len_ref,c_ref,hs_ref,b2_ref,dn2_ref,g_ref,out_ref,dhs_ref,db1_ref,gg_ref):
    L=hs_ref.shape[0]
    n=len_ref[0]
    gg_ref[...]=jnp.zeros_like(gg_ref)
    def body(r,o):
        row=lax.broadcasted_iota(jnp.int32,(RB,768),0)+o
        hs=hs_ref[r,:]
        out_ref[r,:]=jnp.where(row<n,hs+b2_ref[r,:],0.0).astype(bf16)
        dy=jnp.where(row<n,c_ref[r,:].astype(f32),0.0)
        inv=norm_block(hs,None)
        dn=dn2_ref[r,:]
        q=dn*g_ref[1:2,:]
        gg_ref[1:2,:]+=jnp.sum(hs*inv*dn,axis=0,keepdims=True)
        dh=dy+(inv*q-hs*inv*inv*inv*jnp.mean(hs*q,axis=-1,keepdims=True))
        dhs_ref[r,:]=dh
        db1_ref[r,:]=dh.astype(bf16)
    rows_loop(L,body)

def phase_db2(len_ref,c_ref,db2_ref):
    n=len_ref[0]
    def body(r,o):
        row=lax.broadcasted_iota(jnp.int32,(RB,768),0)+o
        db2_ref[r,:]=jnp.where(row<n,c_ref[r,:].astype(f32),0.0).astype(bf16)
    rows_loop(c_ref.shape[0],body)

def phase_wo_back(db1_ref,o_ref,w_ref,do_ref,gatt_ref):
    def it(n,carry):
        o=pl.multiple_of(n*256,256)
        do_ref[:,pl.ds(o,256)]=dot_nt(db1_ref[...],w_ref[pl.ds(pl.multiple_of(2304+o,256),256),:]).astype(bf16)
        gatt_ref[pl.ds(pl.multiple_of(2304+o,256),256),:]=dot_tn(o_ref[:,pl.ds(o,256)],db1_ref[...]).astype(bf16)
        return carry
    lax.fori_loop(0,3,it,0)

def phase_attn_bwd(qkv_ref,p_ref,do_ref,cos_ref,sin_ref,dp_ref):
    L=qkv_ref.shape[0]; QB=256
    def pair(t,carry):
        oq=pl.multiple_of(t*128,128); ok=pl.multiple_of(768+t*128,128); ov=pl.multiple_of(1536+t*128,128)
        dkt=None; dvt=None
        for i in range(L//QB):
            kl=(i+1)*QB; r=slice(i*QB,(i+1)*QB)
            q=lane_masks(qkv_ref[r,pl.ds(oq,128)])
            k=lane_masks(qkv_ref[0:kl,pl.ds(ok,128)])
            v=qkv_ref[0:kl,pl.ds(ov,128)]
            do=lane_masks(do_ref[r,pl.ds(oq,128)])
            dss=[]; pls=[]
            for h in range(2):
                pb=p_ref[2*t+h,r,0:kl]
                p=pb.astype(f32)
                if i<L//QB:
                    row=lax.broadcasted_iota(jnp.int32,p.shape,0)+i*QB
                dpr=dot_nt(do[h],v)
                pd=p*dpr
                ds=(pd-p*jnp.sum(pd,axis=-1,keepdims=True)).astype(bf16)
                dss.append(ds); pls.append(pb)
            dq=dot_nn(jnp.concatenate(dss,1),jnp.concatenate(k,0))*attn_multiplier
            c=cos_ref[r,:]; s=sin_ref[r,:]
            dp_ref[r,pl.ds(oq,128)]=(dq*c-swap_halves(dq)*s).astype(bf16)
            a=dot_tn(jnp.concatenate(q,0),jnp.concatenate(dss,0))
            b=dot_tn(jnp.concatenate(do,0),jnp.concatenate(pls,0))
            if dkt is None: dkt,dvt=a,b
            else:
                w=dkt.shape[1]
                dkt=jnp.concatenate([dkt+a[:,:w],a[:,w:]],1); dvt=jnp.concatenate([dvt+b[:,:w],b[:,w:]],1)
        dk=dkt.T*attn_multiplier
        dp_ref[:,pl.ds(ok,128)]=(dk*cos_ref[...]-swap_halves(dk)*sin_ref[...]).astype(bf16)
        dp_ref[:,pl.ds(ov,128)]=dvt.T.astype(bf16)
        return carry
    lax.fori_loop(0,H//2,pair,0)

def phase_dn1(dp_ref,w_ref,x_ref,g_ref,dhs_ref,in_ref,gg_ref):
    L=x_ref.shape[0]; R=128
    def it(i,carry):
        r=pl.ds(pl.multiple_of(i*R,R),R)
        dn=dot_nn(dp_ref[r,:],w_ref[0:2304,:])
        xv=x_ref[r,:].astype(f32)
        inv=norm_block(xv,None)
        gg_ref[0:1,:]+=jnp.sum(xv*inv*dn,axis=0,keepdims=True)
        q=dn*g_ref[0:1,:]
        in_ref[r,:]=(dhs_ref[r,:]+(inv*q-xv*inv*inv*inv*jnp.mean(xv*q,axis=-1,keepdims=True))).astype(bf16)
        return carry
    lax.fori_loop(0,L//R,it,0)

def phase_wqkv_grad(dp_ref,n1_ref,gatt_ref):
    def it(n,carry):
        o=pl.multiple_of(n*256,256)
        gatt_ref[pl.ds(o,256),:]=dot_tn(dp_ref[:,pl.ds(o,256)],n1_ref[...]).astype(bf16)
        return carry
    lax.fori_loop(0,9,it,0)

def k2_kernel(len_ref,x_ref,c_ref,watt_ref,wff_ref,g_ref,cos_ref,sin_ref,
              out_ref,in_ref,gatt_ref,gff_ref,gg_ref,
              n1,qkv,pm,o,hs,n2,db2,b2,dn2,dhs,db1,do,dpj):
    phase_norm1(x_ref,g_ref,n1)
    phase_qkv(n1,watt_ref,cos_ref,sin_ref,qkv)
    phase_attn_fwd(qkv,pm,o)
    phase_wo_norm2(o,watt_ref,x_ref,g_ref,hs,n2)
    phase_db2(len_ref,c_ref,db2)
    phase_ff(n2,db2,wff_ref,gff_ref,b2,dn2)
    phase_mid(len_ref,c_ref,hs,b2,dn2,g_ref,out_ref,dhs,db1,gg_ref)
    phase_wo_back(db1,o,watt_ref,do,gatt_ref)
    phase_attn_bwd(qkv,pm,do,cos_ref,sin_ref,dpj)
    phase_dn1(dpj,watt_ref,x_ref,g_ref,dhs,in_ref,gg_ref)
    phase_wqkv_grad(dpj,n1,gatt_ref)

def k2(length,x,c,watt,wff,gains,cos,sin,kern=k2_kernel):
    L,D=x.shape
    V=pl.BlockSpec(memory_space=pltpu.VMEM)
    vm=lambda *s,dt=bf16: pltpu.VMEM(s,dt)
    return pl.pallas_call(kern,
        out_shape=(jax.ShapeDtypeStruct((L,D),bf16),jax.ShapeDtypeStruct((L,D),bf16),jax.ShapeDtypeStruct(watt.shape,bf16),jax.ShapeDtypeStruct(wff.shape,bf16),jax.ShapeDtypeStruct((8,D),f32)),
        in_specs=[pl.BlockSpec(memory_space=pltpu.SMEM)]+[V]*7,out_specs=(V,)*5,
        scratch_shapes=[vm(L,D),vm(L,3*D),vm(H,L,L),vm(L,D),vm(L,D,dt=f32),vm(L,D),vm(L,D),vm(L,D,dt=f32),vm(L,D,dt=f32),vm(L,D,dt=f32),vm(L,D),vm(L,D),vm(L,3*D)],
        compiler_params=pltpu.CompilerParams(vmem_limit_bytes=63*2**20),
        )(length,x,c,watt,wff,gains,cos,sin)
MESH=pl.DeviceIdType.MESH

class Topo:
    def __init__(s, nf, nd):
        assert nd==4 and nf%2==0
        s.Z=nf//2; s.N=nf*nd
        f=lax.axis_index("fsdp"); d=lax.axis_index("dp")
        s.z=f//2; s.y=lax.rem(f,2); s.x=d//2; s.c=lax.rem(d,2)
        s.me=f*4+d
        c=s.c
        s.y1=s.y+c*(1-2*s.y); s.x1=s.x+(1-c)*(1-2*s.x)
        s.y2=s.y+(1-c)*(1-2*s.y); s.x2=s.x+c*(1-2*s.x)
        s.yb=1-s.y; s.xb=1-s.x; s.cb=1-c
    def slot(s,z,y,x,c): return ((z*2+y)*2+x)*2+c
    def dev(s,z,y,x,c): return (z*2+y, x*2+c)
    def flat(s,i): return (i//4, lax.rem(i,4))
    def zk(s,k): return lax.rem(s.z+k,s.Z)
    @property
    def p1(s): return s.dev(s.z,s.y1,s.x1,s.c)
    @property
    def p2(s): return s.dev(s.z,s.y2,s.x2,s.c)
    @property
    def sib(s): return s.dev(s.z,s.y,s.x,s.cb)

def loop(lo,hi,body):
    lax.fori_loop(lo,hi,lambda i,c:(body(i),c)[1],0)

def rcopy(src,dst,ssem,rsem,dev):
    return pltpu.make_async_remote_copy(src_ref=src,dst_ref=dst,send_sem=ssem,recv_sem=rsem,device_id=dev,device_id_type=MESH)

def wait_bytes(ref,sem):
    pltpu.make_async_copy(ref,ref,sem).wait()

def barrier_all(t):
    b=pltpu.get_barrier_semaphore()
    def sig(k): pl.semaphore_signal(b,inc=1,device_id=t.flat(lax.rem(t.me+k,t.N)),device_id_type=MESH)
    loop(1,t.N,sig)
    pl.semaphore_wait(b,t.N-1)

class A2A:
    def __init__(s,t,src,dst,ssem,rsem,lsem): s.t,s.src,s.dst,s.ssem,s.rsem,s.lsem=t,src,dst,ssem,rsem,lsem
    def start(s):
        t=s.t
        pltpu.make_async_copy(s.src.at[t.me],s.dst.at[t.me],s.lsem).start()
        def f(k):
            d=lax.rem(t.me+k,t.N)
            rcopy(s.src.at[d],s.dst.at[t.me],s.ssem,s.rsem,t.flat(d)).start()
        loop(1,t.N,f)
    def wait_recv(s):
        n=s.t.N-1
        pltpu.make_async_copy(s.src.at[s.t.me],s.dst.at[s.t.me],s.lsem).wait()
        wait_bytes(s.dst.at[pl.ds(0,n)],s.rsem)
    def wait_send(s):
        wait_bytes(s.src.at[pl.ds(0,s.t.N-1)],s.ssem)

class Gather:
    def __init__(s,t,src,dst,ssem,rsem,lsem): s.t,s.src,s.dst,s.ssem,s.rsem,s.lsem=t,src,dst,ssem,rsem,lsem
    def send(s,slot,dev,src=None):
        rcopy(s.dst.at[slot] if src is None else src,s.dst.at[slot],s.ssem,s.rsem.at[slot],dev).start()
    def wait(s,slot):
        wait_bytes(s.dst.at[slot],s.rsem.at[slot])
    def start(s):
        t=s.t
        pltpu.make_async_copy(s.src,s.dst.at[t.me],s.lsem).start()
        for dev in (t.p1,t.p2,t.sib): s.send(t.me,dev,s.src)
        loop(1,t.Z,lambda k: s.send(t.me,t.dev(t.zk(k),t.y,t.x,t.c),s.src))
    def phase1(s):
        t=s.t
        def f(k):
            sl=t.slot(t.zk(k),t.y,t.x,t.c); s.wait(sl)
            for dev in (t.p1,t.p2,t.sib): s.send(sl,dev)
        loop(1,t.Z,f)
    def phase2(s):
        t=s.t
        def f(k):
            sl=t.slot(t.zk(k),t.y1,t.x1,t.c); s.wait(sl)
            for dev in (t.p2,t.sib): s.send(sl,dev)
        loop(0,t.Z,f)
    def phase3(s):
        t=s.t
        for y,x in ((t.y2,t.x2),(t.yb,t.xb)):
            def f(k):
                sl=t.slot(t.zk(k),y,x,t.c); s.wait(sl); s.send(sl,t.sib)
            loop(0,t.Z,f)
    def phase4(s):
        t=s.t
        for y,x in ((0,0),(0,1),(1,0),(1,1)):
            loop(0,t.Z,lambda k: s.wait(t.slot(t.zk(k),y,x,t.cb)))
    def finish(s):
        t=s.t
        pltpu.make_async_copy(s.src,s.dst.at[t.me],s.lsem).wait()
        wait_bytes(s.dst.at[pl.ds(0,t.N-1)],s.ssem)

def k1_kernel(nf,nd,perm,tok,cot0,gn,att,ff,xg,cg,gg,wa,wf,cot,ss,rs,ls,ars,frs):
    t=Topo(nf,nd)
    barrier_all(t)
    tk=A2A(t,tok,xg,ss.at[0],rs.at[0],ls.at[0])
    ct=A2A(t,cot,cg,ss.at[1],rs.at[1],ls.at[1])
    A=Gather(t,att,wa,ss.at[3],ars,ls.at[3]); F=Gather(t,ff,wf,ss.at[4],frs,ls.at[4])
    pltpu.make_async_copy(gn,gg.at[t.me],ls.at[2]).start()
    def gs(k): rcopy(gn,gg.at[t.me],ss.at[2],rs.at[2],t.flat(lax.rem(t.me+k,t.N))).start()
    loop(1,t.N,gs)
    A.start()
    tk.start()
    def pm(i): cot[i]=cot0[perm[i]]
    loop(0,t.N,pm)
    A.phase1()
    F.start()
    A.phase2()
    F.phase1()
    A.phase3()
    F.phase2()
    ct.start()
    A.phase4()
    F.phase3(); F.phase4()
    tk.wait_recv(); ct.wait_recv()
    pltpu.make_async_copy(gn,gg.at[t.me],ls.at[2]).wait()
    wait_bytes(gg.at[pl.ds(0,t.N-1)],rs.at[2]); wait_bytes(gg.at[pl.ds(0,t.N-1)],ss.at[2])
    A.finish(); F.finish(); tk.wait_send(); ct.wait_send()

def k1(perm,tok,cot,gn,att,ff):
    nf,nd=lax.axis_size("fsdp"),lax.axis_size("dp"); N=nf*nd
    anyv=pl.BlockSpec(memory_space=pl.ANY); D=pltpu.SemaphoreType.DMA
    sd=jax.ShapeDtypeStruct
    return pl.pallas_call(functools.partial(k1_kernel,nf,nd),
        out_shape=(sd(tok.shape,tok.dtype),sd(cot.shape,cot.dtype),sd((N,)+gn.shape,gn.dtype),sd((N,)+att.shape,att.dtype),sd((N,)+ff.shape,ff.dtype)),
        in_specs=[pl.BlockSpec(memory_space=pltpu.SMEM),anyv,pl.BlockSpec(memory_space=pltpu.VMEM),anyv,anyv,anyv],out_specs=(anyv,)*5,
        scratch_shapes=[pltpu.VMEM(cot.shape,cot.dtype),D((5,)),D((5,)),D((5,)),D((N,)),D((N,))],
        compiler_params=pltpu.CompilerParams(collective_id=0,has_side_effects=True))(perm,tok,cot,gn,att,ff)

class Scatter:
    def __init__(s,t,g,rc,r1,r2,rz,ss,rcs,r1s,r2s,rzs):
        s.t,s.g,s.rc,s.r1,s.r2,s.rz,s.ss,s.rcs,s.r1s,s.r2s,s.rzs=t,g,rc,r1,r2,rz,ss,rcs,r1s,r2s,rzs
        s.Z=t.Z
    def groups(s,sibling):
        t=s.t
        if sibling:
            return ((t.yb,t.xb),(t.y1,t.x1),(t.y2,t.x2),(t.y,t.x))
        return ((t.yb,t.xb),(t.y2,t.x2),(t.y1,t.x1),(t.y,t.x))
    def start(s):
        t=s.t; Z=s.Z
        for gi,(y,x) in enumerate(s.groups(True)):
            def f(k):
                rcopy(s.g.at[t.slot(t.zk(k),y,x,t.cb)],s.rc.at[gi*Z+k],s.ss.at[0],s.rcs.at[gi*Z+k],t.sib).start()
            loop(0,Z,f)
    def stage_c(s):
        t=s.t; Z=s.Z
        for gi,(y,x) in enumerate(s.groups(False)):
            def f(k):
                j=gi*Z+k
                wait_bytes(s.rc.at[j],s.rcs.at[j])
                s.rc[j]=s.rc[j]+s.g[t.slot(t.zk(k),y,x,t.c)]
                if gi<2: rcopy(s.rc.at[j],s.r1.at[j],s.ss.at[1],s.r1s.at[j],t.p2).start()
            loop(0,Z,f)
    def stage_1(s):
        t=s.t; Z=s.Z
        for gi in range(2):
            def f(k):
                j=gi*Z+k
                wait_bytes(s.r1.at[j],s.r1s.at[j])
                s.r1[j]=s.r1[j]+s.rc[2*Z+j]
                if gi==0: rcopy(s.r1.at[j],s.r2.at[k],s.ss.at[2],s.r2s.at[k],t.p1).start()
            loop(0,Z,f)
    def stage_2(s):
        t=s.t; Z=s.Z
        def f(k):
            wait_bytes(s.r2.at[k],s.r2s.at[k])
            s.r2[k]=s.r2[k]+s.r1[Z+k]
            rcopy(s.r2.at[k],s.rz.at[Z-k-1],s.ss.at[3],s.rzs.at[Z-k-1],t.dev(t.zk(k),t.y,t.x,t.c)).start()
        loop(1,Z,f)
        wait_bytes(s.r2.at[0],s.r2s.at[0])
    def final(s,out):
        Z=s.Z
        tot=s.r2[0].astype(f32)+s.r1[Z].astype(f32)
        for k in range(Z-1):
            wait_bytes(s.rz.at[k],s.rzs.at[k])
            tot=tot+s.rz[k].astype(f32)
        out[...]=tot
    def wait_send(s):
        Z=s.Z
        wait_bytes(s.rc,s.ss.at[0])
        wait_bytes(s.r1,s.ss.at[1])
        wait_bytes(s.r2,s.ss.at[2])
        wait_bytes(s.rz,s.ss.at[3])

def k3_kernel(nf,nd,perm,orow,irow,gg,ga,gf,oo0,io,ggo,ao,fo,oo,ggr,arc,ar1,ar2,arz,frc,fr1,fr2,frz,ss,rs,ls,ass,fss,acs,a1s,a2s,azs,fcs,f1s,f2s,fzs):
    t=Topo(nf,nd)
    barrier_all(t)
    A=Scatter(t,ga,arc,ar1,ar2,arz,ass,acs,a1s,a2s,azs)
    F=Scatter(t,gf,frc,fr1,fr2,frz,fss,fcs,f1s,f2s,fzs)
    F.start(); A.start()
    pltpu.make_async_copy(gg.at[t.me],ggr.at[t.me],ls.at[2]).start()
    def gs(k):
        d=lax.rem(t.me+k,t.N)
        rcopy(gg.at[d],ggr.at[t.me],ss.at[2],rs.at[2],t.flat(d)).start()
    loop(1,t.N,gs)
    F.stage_c()
    o=A2A(t,orow,oo,ss.at[0],rs.at[0],ls.at[0])
    i=A2A(t,irow,io,ss.at[1],rs.at[1],ls.at[1])
    o.start()
    A.stage_c()
    i.start()
    F.stage_1(); F.stage_2()
    A.stage_1(); A.stage_2()
    pltpu.make_async_copy(gg.at[t.me],ggr.at[t.me],ls.at[2]).wait()
    wait_bytes(ggr.at[pl.ds(0,t.N-1)],rs.at[2]); wait_bytes(ggr.at[pl.ds(0,t.N-1)],ss.at[2])
    tot=ggr[0]
    for k in range(1,t.N): tot=tot+ggr[k]
    ggo[...]=tot
    F.final(fo); A.final(ao)
    o.wait_recv()
    def pm(j): oo0[j]=oo[perm[j]]
    loop(0,t.N,pm)
    i.wait_recv(); o.wait_send(); i.wait_send()
    F.wait_send(); A.wait_send()

def k3(perm,orow,irow,gg,ga,gf):
    nf,nd=lax.axis_size("fsdp"),lax.axis_size("dp"); N=nf*nd; Z=nf//2
    anyv=pl.BlockSpec(memory_space=pl.ANY); V=pl.BlockSpec(memory_space=pltpu.VMEM); D=pltpu.SemaphoreType.DMA
    sd=jax.ShapeDtypeStruct
    ash,fsh=ga.shape[1:],gf.shape[1:]
    vm=lambda n,sh: pltpu.VMEM((n,)+sh,bf16)
    return pl.pallas_call(functools.partial(k3_kernel,nf,nd),
        out_shape=(sd(orow.shape,bf16),sd(irow.shape,bf16),sd(gg.shape[1:],f32),sd(ash,f32),sd(fsh,f32)),
        in_specs=[pl.BlockSpec(memory_space=pltpu.SMEM),anyv,anyv,V,V,V],out_specs=(V,anyv,V,V,V),
        scratch_shapes=[pltpu.VMEM(orow.shape,bf16),pltpu.VMEM(gg.shape,f32)]+[vm(n,sh) for sh in (ash,fsh) for n in (4*Z,2*Z,Z,Z-1)]+[D((3,)),D((3,)),D((3,)),D((4,)),D((4,))]+[D((n,)) for _ in range(2) for n in (4*Z,2*Z,Z,Z-1)],
        compiler_params=pltpu.CompilerParams(collective_id=1,has_side_effects=True,vmem_limit_bytes=60*2**20))(perm,orow,irow,gg,ga,gf)


from jax.sharding import PartitionSpec as P
AX = ("fsdp", "dp")
beta_first = 0.5
beta_second = 0.5
learning_rate = 0.03
weight_decay = 0.1
adam_epsilon = 1e-08


def adam_update(master, gradient, first_moment, second_moment, decay):
    first_new = beta_first * first_moment + (1.0 - beta_first) * gradient
    second_new = beta_second * second_moment + (1.0 - beta_second) * gradient * gradient
    first_hat = first_new / (1.0 - beta_first**STEP)
    second_hat = second_new / (1.0 - beta_second**STEP)
    master_new = master - learning_rate * (
        first_hat / (jnp.sqrt(second_hat) + adam_epsilon) + decay * master
    )
    return (first_new, second_new, master_new)


def local(tokens, cotangent, lengths, device_sequence, slot_device, attention_master, feedforward_master, gains_master,
          attention_mean, attention_square, feedforward_mean, feedforward_square, gains_mean, gains_square):
    N = lax.axis_size(AX)
    me = lax.axis_index(AX)
    positions, width = tokens.shape[1], tokens.shape[2]
    length = positions * N
    gl = gains_master.shape[1]
    counter = jnp.arange(N, dtype=jnp.int32)
    slot_sequence = jnp.sum(jnp.where(slot_device[:, None] == counter[None, :], device_sequence[None, :], 0), axis=1)
    slot_of_sequence = jnp.sum(jnp.where(slot_sequence[:, None] == counter[None, :], counter[:, None], 0), axis=0)
    att_low = attention_master.astype(bf16)
    ff_low = feedforward_master.transpose(1, 0, 2).astype(bf16)
    gn = jnp.zeros((8, 128), f32).at[:2, :gl].set(gains_master.astype(bf16).astype(f32))
    xg, cg, gg, wa, wf = k1(slot_of_sequence, tokens, cotangent, gn, att_low, ff_low)
    gains = jnp.zeros((8, width), f32).at[:2].set(gg[:, :2, :gl].transpose(1, 0, 2).reshape(2, width))
    C, S = tables(length)
    orow, irow, gatt, gff, ggr = k2(jnp.sum(jnp.where(counter == me, lengths, 0))[None], xg.reshape(length, width), cg.reshape(length, width),
                                    wa.reshape(-1, width), wf, gains, jnp.asarray(C), jnp.asarray(S))
    gblocks = jnp.zeros((N, 8, 128), f32).at[:, :2, :gl].set(ggr[:2].reshape(2, N, gl).transpose(1, 0, 2))
    oo, io, gsum, ag, fg = k3(slot_sequence, orow.reshape(N, positions, width), irow.reshape(N, positions, width), gblocks,
                              gatt.reshape(N, -1, width), gff)
    output = oo
    attention_gradient = ag
    feedforward_gradient = fg.transpose(1, 0, 2)
    gains_gradient = gsum[:2, :gl]
    mean_attention, square_attention, master_attention = adam_update(
        attention_master, attention_gradient, attention_mean, attention_square, weight_decay)
    mean_feedforward, square_feedforward, master_feedforward = adam_update(
        feedforward_master, feedforward_gradient, feedforward_mean, feedforward_square, weight_decay)
    mean_gains, square_gains, master_gains = adam_update(gains_master, gains_gradient, gains_mean, gains_square, 0.0)
    return (output, io, attention_gradient, feedforward_gradient, gains_gradient, mean_attention, square_attention,
            mean_feedforward, square_feedforward, mean_gains, square_gains, master_attention, master_feedforward,
            master_gains - gains_master, master_attention.astype(bf16), master_feedforward.astype(bf16))


class Topo2(Topo):
    def __init__(s, nf, nd):
        super().__init__(nf, nd)
    def flip(s, gi, cc):
        a, b = lax.rem(gi, 2), gi // 2
        fx, fy = (1 - cc) * a + cc * b, (1 - cc) * b + cc * a
        return s.y + fy * (1 - 2 * s.y), s.x + fx * (1 - 2 * s.x)
    def g8(s, gi, cc):
        y, x = s.flip(gi, cc)
        return (y * 2 + x) * 2 + cc


def near(t, i):
    r = 0
    for z in range(t.Z):
        by = sorted(range(t.Z), key=lambda q: (abs(q - z), q))
        for k in range(t.Z): r = r + jnp.where((t.z == z) & (i == k), by[k], 0)
    return r


class Gather2:
    def __init__(s, t, at, ssem, zsem, rsem): s.t, s.at, s.ssem, s.zsem, s.rsem = t, at, ssem, zsem, rsem
    def send(s, z, g, dev):
        rcopy(s.at(z, g), s.at(z, g), s.ssem, s.rsem.at[z, g], dev).start()
    def wait(s, z, g): wait_bytes(s.at(z, g), s.rsem.at[z, g])
    def along(s, z, g, side, f):
        t = s.t
        @pl.when((t.z + side >= 0) & (t.z + side < t.Z))
        def _(): f(rcopy(s.at(z, g), s.at(z, g), s.zsem.at[z, (side + 1) // 2], s.rsem.at[z, g], t.dev(t.z + side, t.y, t.x, t.c)))
    def start(s):
        t = s.t; g = t.g8(0, t.c)
        for side in (-1, 1): s.along(t.z, g, side, lambda c: c.start())
        for dev in (t.p1, t.p2, t.sib): s.send(t.z, g, dev)
    def sweep(s, lo, hi, f):
        t = s.t
        def step(j):
            @pl.when(t.z - j >= 0)
            def _(): f(t.z - j, -1)
            @pl.when(t.z + j < t.Z)
            def _(): f(t.z + j, 1)
        if lo == 0: f(t.z, 0)
        loop(max(lo, 1), hi, step)
    def take(s, gi, lo=0, hi=None):
        t = s.t; g = t.g8(gi, t.c)
        to = {0: (t.p1, t.p2, t.sib), 1: (t.p2, t.sib)}.get(gi, (t.sib,))
        def f(z, side):
            s.wait(z, g)
            if gi == 0: s.along(z, g, -side, lambda c: c.start())
            for dev in to: s.send(z, g, dev)
        s.sweep(lo, t.Z if hi is None else hi, f)
    def take_sib(s, gi, lo=0, hi=None):
        t = s.t; g = t.g8(gi, t.cb)
        s.sweep(lo, t.Z if hi is None else hi, lambda z, side: s.wait(z, g))
    def finish(s, bulk):
        t = s.t; g = t.g8(0, t.c)
        wait_bytes(bulk, s.ssem)
        for side in (-1, 1): s.along(t.z, g, side, lambda c: c.wait_send())
        s.sweep(1, t.Z, lambda z, side: s.along(z, g, -side, lambda c: c.wait_send()))


SEQ = ((0, 1), (1, 0), (0, 2), (1, 1), (2, 0), (0, 3), (1, 2), (2, 1), (3, 0), (1, 3), (2, 2), (3, 1), (2, 3), (3, 2), (3, 3))


class Scatter3:
    def __init__(s, t, at, ld, rc, r1, r2, rz, ss, rcs, r1s, r2s, rzs, zss, far=True):
        s.far = far
        s.t, s.at, s.ld, s.rc, s.r1, s.r2, s.rz, s.ss, s.rcs, s.r1s, s.r2s, s.rzs, s.zss = t, at, ld, rc, r1, r2, rz, ss, rcs, r1s, r2s, rzs, zss
        s.Z = Z = t.Z
        far_order = [sorted(range(Z), key=lambda q: (-abs(q - z), (q > z) == (z < Z // 2))) for z in range(Z)]
        s.order = far_order if far else [sorted(range(Z), key=lambda q: (abs(q - z), q)) for z in range(Z)]
    def zof(s, i):
        r = 0
        for z in range(s.Z): r = r + jnp.where(s.t.z == z, s.order[z][i], 0)
        return r
    def start(s, z):
        t = s.t
        for gi in range(4):
            j = (3 - gi) * s.Z + z
            rcopy(s.at(z, t.g8(gi, t.cb)), s.rc.at[j], s.ss.at[0], s.rcs.at[j], t.sib).start()
    def chip(s, z, gs):
        t = s.t; Z = s.Z
        for gi in gs:
            j = (3 - gi) * Z + z
            wait_bytes(s.rc.at[j], s.rcs.at[j])
            s.rc[j] = s.rc[j] + s.ld(z, t.g8(gi, t.c))
            if gi >= 2: rcopy(s.rc.at[j], s.r1.at[j], s.ss.at[1], s.r1s.at[j], t.p2).start()
    def first(s, z):
        t = s.t; Z = s.Z
        for h in range(2):
            j = h * Z + z
            wait_bytes(s.r1.at[j], s.r1s.at[j])
            s.r1[j] = s.r1[j] + s.rc[2 * Z + j]
            if h == 0: rcopy(s.r1.at[z], s.r2.at[z], s.ss.at[2], s.r2s.at[z], t.p1).start()
    def hop(s, z, side):
        t = s.t
        j = jnp.where((z == t.z + side) & (side < 0), s.Z, z)
        return rcopy(s.r2.at[z], s.rz.at[j], s.zss.at[z], s.rzs.at[j], t.dev(t.z + side, t.y, t.x, t.c))
    def second(s, z):
        t = s.t; Z = s.Z
        wait_bytes(s.r2.at[z], s.r2s.at[z])
        s.r2[z] = s.r2[z] + s.r1[Z + z]
    def line(s, z):
        t = s.t; Z = s.Z
        for side in (-1, 1):
            @pl.when((z - t.z) * side > 0)
            def _():
                @pl.when((t.z - side >= 0) & (t.z - side < Z))
                def _():
                    wait_bytes(s.rz.at[z], s.rzs.at[z])
                    s.r2[z] = s.r2[z] + s.rz[z]
                s.hop(z, side).start()
    def C(s, *ii):
        for i in ii: s.chip(s.zof(i), (3, 2, 1, 0))
    def F(s, *ii):
        for i in ii: s.first(s.zof(i))
    def straight(s, z):
        t = s.t
        return rcopy(s.r2.at[z], s.rz.at[t.z], s.zss.at[z], s.rzs.at[t.z], t.dev(z, t.y, t.x, t.c))
    def D(s, *ii):
        for i in ii:
            z = s.zof(i)
            s.second(z)
            @pl.when(z != s.t.z)
            def _(): s.straight(z).start()
    def S(s, *ii):
        for i in ii: s.second(s.zof(i)); s.line(s.zof(i))
    def total(s):
        t = s.t; Z = s.Z
        tot = s.r2[t.z].astype(f32)
        if not s.far:
            for q in range(Z):
                @pl.when(t.z != q)
                def _(): wait_bytes(s.rz.at[q], s.rzs.at[q])
                @pl.when(t.z == q)
                def _(): s.rz[q] = jnp.zeros(s.rz.shape[1:], bf16)
                tot = tot + s.rz[q].astype(f32)
            return tot
        below = jnp.where(t.z > 0, 1.0, 0.0); above = jnp.where(t.z < Z - 1, 1.0, 0.0)
        @pl.when(t.z > 0)
        def _(): wait_bytes(s.rz.at[t.z], s.rzs.at[t.z])
        @pl.when(t.z == 0)
        def _(): s.rz[t.z] = jnp.zeros(s.rz.shape[1:], bf16)
        @pl.when(t.z < Z - 1)
        def _(): wait_bytes(s.rz.at[Z], s.rzs.at[Z])
        @pl.when(t.z == Z - 1)
        def _(): s.rz[Z] = jnp.zeros(s.rz.shape[1:], bf16)
        return tot + (s.rz[t.z].astype(f32) + s.rz[Z].astype(f32))
    def wait_send(s):
        t = s.t; Z = s.Z
        wait_bytes(s.rc, s.ss.at[0]); wait_bytes(s.r1, s.ss.at[1]); wait_bytes(s.r2, s.ss.at[2])
        def f(z):
            if not s.far:
                @pl.when(z != t.z)
                def _(): s.straight(z).wait_send()
                return
            for side in (-1, 1):
                @pl.when((z - t.z) * side > 0)
                def _(): s.hop(z, side).wait_send()
        loop(0, Z, f)


class Exchange:
    def __init__(s, t, src, dst, sbulk, dbulk, ssem, rsem, lsem):
        s.t, s.src, s.dst, s.sbulk, s.dbulk, s.ssem, s.rsem, s.lsem = t, src, dst, sbulk, dbulk, ssem, rsem, lsem
        s.sent = 1
    def start(s): pltpu.make_async_copy(s.src(s.t.me), s.dst(s.t.me), s.lsem).start()
    def more(s, n):
        t = s.t
        def f(k):
            d = lax.rem(t.me + k, t.N)
            rcopy(s.src(d), s.dst(t.me), s.ssem, s.rsem, t.flat(d)).start()
        to = min(t.N, s.sent + n)
        if to > s.sent: loop(s.sent, to, f)
        s.sent = to
    def wait_recv(s):
        pltpu.make_async_copy(s.src(s.t.me), s.dst(s.t.me), s.lsem).wait()
        wait_bytes(s.dbulk, s.rsem)
    def wait_send(s): wait_bytes(s.sbulk, s.ssem)


def rows_of(ref, n):
    return lambda d: ref.at[pl.ds(pl.multiple_of(d * n, n), n)]


def attn_fwd2(qkv_ref, ps, o_ref, lo, hi):
    QB = 256
    def pair(t, carry):
        oq = pl.multiple_of(t * 128, 128); ok = pl.multiple_of(768 + t * 128, 128); ov = pl.multiple_of(1536 + t * 128, 128)
        for i in range(len(ps)):
            kl = (i + 1) * QB
            q = lane_masks(qkv_ref[i * QB:kl, pl.ds(oq, 128)])
            k = qkv_ref[0:kl, pl.ds(ok, 128)]
            v = lane_masks(qkv_ref[0:kl, pl.ds(ov, 128)])
            got = []
            for h in range(2):
                s = dot_nt(q[h], k)
                row = lax.broadcasted_iota(jnp.int32, s.shape, 0) + i * QB
                col = lax.broadcasted_iota(jnp.int32, s.shape, 1)
                s = jnp.where(row >= col, s, -1e30)
                m = jnp.max(s, axis=-1, keepdims=True)
                e = jnp.exp2((s - m) * (attn_multiplier * LOG2E))
                pr = (e * (1.0 / jnp.sum(e, axis=-1, keepdims=True))).astype(bf16)
                ps[i][2 * t + h] = pr
                got.append(pr)
            n = o_ref.shape[1]
            o_ref[i * QB // n:kl // n, :, pl.ds(oq, 128)] = dot_nn(jnp.concatenate(got, 1), jnp.concatenate(v, 0)).astype(bf16).reshape(QB // n, n, 128)
        return carry
    lax.fori_loop(lo, hi, pair, 0)


def attn_bwd2(qkv_ref, ps, do_ref, cos_ref, sin_ref, lo, hi):
    QB = 256
    def pair(t, carry):
        oq = pl.multiple_of(t * 128, 128); ok = pl.multiple_of(768 + t * 128, 128); ov = pl.multiple_of(1536 + t * 128, 128)
        dkt = None; dvt = None
        for i in range(len(ps)):
            kl = (i + 1) * QB; r = slice(i * QB, kl)
            q = lane_masks(qkv_ref[r, pl.ds(oq, 128)])
            k = lane_masks(qkv_ref[0:kl, pl.ds(ok, 128)])
            v = qkv_ref[0:kl, pl.ds(ov, 128)]
            do = lane_masks(do_ref[r, pl.ds(oq, 128)])
            dss = []; pls = []
            for h in range(2):
                pb = ps[i][2 * t + h]
                p = pb.astype(f32)
                pd = p * dot_nt(do[h], v)
                dss.append((pd - p * jnp.sum(pd, axis=-1, keepdims=True)).astype(bf16)); pls.append(pb)
            dq = dot_nn(jnp.concatenate(dss, 1), jnp.concatenate(k, 0)) * attn_multiplier
            a = dot_tn(jnp.concatenate(q, 0), jnp.concatenate(dss, 0))
            b = dot_tn(jnp.concatenate(do, 0), jnp.concatenate(pls, 0))
            qkv_ref[r, pl.ds(oq, 128)] = (dq * cos_ref[r, :] - swap_halves(dq) * sin_ref[r, :]).astype(bf16)
            if dkt is None: dkt, dvt = a, b
            else:
                w = dkt.shape[1]
                dkt = jnp.concatenate([dkt + a[:, :w], a[:, w:]], 1); dvt = jnp.concatenate([dvt + b[:, :w], b[:, w:]], 1)
        dk = dkt.T * attn_multiplier
        qkv_ref[:, pl.ds(ok, 128)] = (dk * cos_ref[...] - swap_halves(dk) * sin_ref[...]).astype(bf16)
        qkv_ref[:, pl.ds(ov, 128)] = dvt.T.astype(bf16)
        return carry
    lax.fori_loop(lo, hi, pair, 0)


def wo_norm2(o_ref, w_ref, x_ref, g_ref, hs_ref, n2_ref):
    L = x_ref.shape[0]; R = 128; n = o_ref.shape[1]
    def it(i, carry):
        r = pl.ds(pl.multiple_of(i * R, R), R)
        hs = x_ref[r, :].astype(f32) + dot_nn(o_ref[pl.ds(i * (R // n), R // n)].reshape(R, 768), w_ref[2304:3072, :])
        hs_ref[r, :] = hs
        n2_ref[r, :] = (hs * norm_block(hs, None) * g_ref[1:2, :]).astype(bf16)
        return carry
    lax.fori_loop(0, L // R, it, 0)


def wo_back2(db1_ref, o_ref, w_ref, do_ref, gatt_ref):
    def it(n, carry):
        o = pl.multiple_of(n * 256, 256); w = pl.ds(pl.multiple_of(2304 + o, 256), 256)
        do_ref[:, pl.ds(o, 256)] = dot_nt(db1_ref[...], w_ref[w, :]).astype(bf16)
        gatt_ref[w, :] = dot_tn(o_ref[:, :, pl.ds(o, 256)].reshape(-1, 256), db1_ref[...]).astype(bf16)
        return carry
    lax.fori_loop(0, 3, it, 0)


def mid2(n, cg, hs_ref, b2_ref, dn2_ref, g_ref, db1_ref, gg_ref):
    gg_ref[...] = jnp.zeros_like(gg_ref)
    def body(r, o):
        row = lax.broadcasted_iota(jnp.int32, (RB, 768), 0) + o
        hs = hs_ref[r, :]
        dy = cg[r, :].astype(f32)
        cg[r, :] = jnp.where(row < n, hs + b2_ref[r, :], 0.0).astype(bf16)
        inv = norm_block(hs, None)
        dn = dn2_ref[r, :]
        q = dn * g_ref[1:2, :]
        gg_ref[1:2, :] += jnp.sum(hs * inv * dn, axis=0, keepdims=True)
        dh = dy + (inv * q - hs * inv * inv * inv * jnp.mean(hs * q, axis=-1, keepdims=True))
        hs_ref[r, :] = dh
        db1_ref[r, :] = dh.astype(bf16)
    rows_loop(hs_ref.shape[0], body)


def all_kernel(nf, nd, perm, lens, tok, cot0, gm, am, fm, cos_ref, sin_ref,
               oo, io, ggo, ao, fo,
               xg, cg, cst, wa, wf, gt, gg, gains, ggb, gb, ggr,
               n1, qkv, p0, p1, o, hs, n2, b2, dn2, gatt, gff, cs, sn,
               arc, ar1, ar2, arz, frc, fr1, fr2, frz,
               ss, rs, ls, azs2, fzs2, ags, fgs, ass, fss, acs, a1s, a2s, azs, azq, fcs, f1s, f2s, fzs, fzq):
    t = Topo2(nf, nd)
    N, Z = t.N, t.Z
    L = xg.shape[0]; pos = L // N; ra = wa.shape[0] // N; gl = gm.shape[1]; R = wf.shape[2]
    ps = (p0, p1)
    row_at = lambda ref: (lambda z, g: ref.at[pl.ds(pl.multiple_of((z * 8 + g) * ra, ra), ra)])
    blk_at = lambda ref: (lambda z, g: ref.at[z * 8 + g])
    most = lambda ref: ref.at[pl.ds(0, L - pos)]
    f0 = b2.at[pl.ds(0, ra)], dn2.at[pl.ds(0, 3 * R)]
    near_w = [pltpu.make_async_copy(a, d, ls.at[5 + i]) for i, (a, d) in enumerate(((am, f0[0]), (fm, f0[1]), (cot0, o), (cos_ref, cs), (sin_ref, sn)))]
    for c in near_w: c.start()
    near_w[0].wait()
    wa[pl.ds(pl.multiple_of(t.me * ra, ra), ra), :] = f0[0][...].astype(bf16)
    near_w[1].wait()
    wf[t.me] = f0[1][...].astype(bf16).reshape(3, R, 768)
    gt[...] = jnp.zeros_like(gt)
    gt[0:2, 0:gl] = gm[...].astype(bf16).astype(f32)
    gg[t.me] = gt[...]
    barrier_all(t)
    A = Gather2(t, row_at(wa), ss.at[3], azs2, ags)
    F = Gather2(t, blk_at(wf), ss.at[4], fzs2, fgs)
    tk = Exchange(t, lambda d: tok.at[d], rows_of(xg, pos), most(xg), most(xg), ss.at[0], rs.at[0], ls.at[0])
    ct = Exchange(t, rows_of(cst, pos), rows_of(cg, pos), most(cg), most(cg), ss.at[1], rs.at[1], ls.at[1])
    def takes(X, lo, hi, *more):
        for g, d in SEQ[lo:hi]:
            X.take(g, d, d + 1)
            for e, k in more: e.more(k)
    tk.start()
    A.start()
    tk.more(8)
    takes(A, 0, 3, (tk, 3))
    F.start()
    near_w[2].wait()
    def pm(i): cst[pl.ds(pl.multiple_of(i * pos, pos), pos), :] = o[perm[i]]
    loop(0, N, pm)
    ct.start()
    def gs(k): rcopy(gt, gg.at[t.me], ss.at[2], rs.at[2], t.flat(lax.rem(t.me + k, N))).start()
    loop(1, N, gs)
    takes(A, 3, 8, (tk, 3))
    takes(A, 8, 15, (tk, 8), (ct, 4))

    tk.more(N)
    for gi in range(4): A.take_sib(gi)
    tk.wait_recv()
    wait_bytes(gg.at[pl.ds(0, N - 1)], rs.at[2])
    tot = jnp.zeros((8, 768), f32)
    for d in range(N):
        wide = jnp.concatenate([gg[d], jnp.zeros((8, 640), f32)], 1)
        tot = tot + (pltpu.roll(wide, d * gl, 1) if d else wide)
    gains[...] = tot
    takes(F, 0, 2, (ct, 8))

    phase_norm1(xg, gains, n1)
    takes(F, 2, 3)

    near_w[3].wait(); near_w[4].wait()
    phase_qkv(n1, wa, cs, sn, qkv)
    takes(F, 3, 5)
    def fwd(i):
        attn_fwd2(qkv, ps, o, i, i + 1)
    loop(0, 2, fwd)
    takes(F, 5, 6)
    loop(2, 4, fwd)
    takes(F, 6, 7)
    loop(4, 6, fwd)
    takes(F, 7, 8)

    ct.more(N)
    wo_norm2(o, wa, xg, gains, hs, n2)
    takes(F, 8, 9)

    ct.wait_recv()
    n = lens[t.me]
    def mask(r, of):
        row = lax.broadcasted_iota(jnp.int32, (RB, 768), 0) + of
        cg[r, :] = jnp.where(row < n, cg[r, :].astype(f32), 0.0).astype(bf16)
    rows_loop(L, mask)
    SA = Scatter3(t, row_at(gatt), lambda z, g: gatt[pl.ds(pl.multiple_of((z * 8 + g) * ra, ra), ra), :], arc, ar1, ar2, arz, ass, acs, a1s, a2s, azs, azq)
    SF = Scatter3(t, blk_at(gff), lambda z, g: gff[z * 8 + g], frc, fr1, fr2, frz, fss, fcs, f1s, f2s, fzs, fzq, far=False)
    def tile(i):
        z = near(t, i // 2)
        par = lax.rem(i, 2)
        cc = t.c + par * (1 - 2 * t.c)
        slots = [z * 8 + q * 2 + cc for q in range(4)]
        for k, lo, hi in ((1, 9, 11), (2, 11, 12), (3, 12, 13), (4, 13, 14), (6, 14, 15)):
            @pl.when(i == k)
            def _(): takes(F, lo, hi)
        for k in range(Z - 1):
            @pl.when(i == 2 * k + 3)
            def _(): SF.C(k)
        @pl.when(par == 1)
        def _():
            for q in range(4): F.wait(z, q * 2 + cc)
        wg, wu, wd = (jnp.concatenate([wf[sl, j] for sl in slots], 0) for j in range(3))
        nv = n2[...]
        ga = dot_nt(nv, wg); u = dot_nt(nv, wu)
        da = dot_nt(cg[...], wd)
        sg = 1.0 / (1.0 + jnp.exp2(ga * (-LOG2E)))
        silu = ga * sg
        a = (silu * u).astype(bf16)
        dg = (da * u * (sg * (1.0 + ga * (1.0 - sg)))).astype(bf16)
        du = (da * silu).astype(bf16)
        bb = dot_nn(a, wd)
        dn = dot_nn(dg, wg) + dot_nn(du, wu)
        @pl.when(i == 0)
        def _():
            b2[...] = bb; dn2[...] = dn
        @pl.when(i > 0)
        def _():
            b2[...] += bb; dn2[...] += dn
        for j, (lhs, rhs) in enumerate(((dg, nv), (du, nv), (a, cg[...]))):
            w = dot_tn(lhs, rhs).astype(bf16)
            for q, sl in enumerate(slots): gff[sl, j] = w[q * R:(q + 1) * R]
        @pl.when(par == 1)
        def _(): SF.start(z)
    loop(0, 8, tile)
    ox = Exchange(t, rows_of(cg, pos), lambda d: oo.at[d], most(cg), oo.at[pl.ds(0, N - 1)], ss.at[5], rs.at[3], ls.at[3])
    ix = Exchange(t, rows_of(n1, pos), lambda d: io.at[d], most(n1), io.at[pl.ds(0, N - 1)], ss.at[6], rs.at[4], ls.at[4])
    mid2(n, cg, hs, b2, dn2, gains, n2, ggb)
    SF.C(3)
    ox.start(); ox.more(8)
    ct.wait_send()
    wo_back2(n2, o, wa, cst, gatt)
    SF.F(0, 1); SF.D(0); ox.more(8)
    def back(i):
        attn_bwd2(qkv, ps, cst, cs, sn, i, i + 1)
    loop(0, 2, back)
    ox.more(8)
    loop(2, 4, back)
    SF.F(2); SF.D(1); ox.more(N)
    loop(4, 6, back)
    phase_wqkv_grad(qkv, n1, gatt)
    for i in range(Z): SA.start(SA.zof(i))
    SF.F(3); SF.D(2)
    SA.C(0, 1)
    phase_dn1(qkv, wa, xg, gains, hs, n1, ggb)
    ix.start(); ix.more(8)
    SF.D(3)
    for d in range(N):
        v = ggb[...]
        gb[d] = (pltpu.roll(v, 768 - d * gl, 1) if d else v)[:, 0:128]
    ggr[t.me] = gb[t.me]
    def gsend(k):
        d = lax.rem(t.me + k, N)
        rcopy(gb.at[d], ggr.at[t.me], ss.at[7], rs.at[5], t.flat(d)).start()
    loop(1, N, gsend)
    SA.F(0); SA.C(2); ix.more(8)
    SA.F(1); SA.S(0); SA.C(3); ix.more(N)
    SA.F(2); SA.S(1)
    f0[1][...] = SF.total().reshape(3 * R, 768)
    far = [pltpu.make_async_copy(f0[1], fo, ls.at[6]), pltpu.make_async_copy(f0[0], ao, ls.at[5])]
    far[0].start()
    SA.F(3); SA.S(2); SA.S(3)
    wait_bytes(ggr.at[pl.ds(0, N - 1)], rs.at[5])
    tot = ggr[0]
    for d in range(1, N): tot = tot + ggr[d]
    ggo[...] = tot
    f0[0][...] = SA.total()
    far[1].start()
    ox.wait_recv(); ix.wait_recv()
    for c in far: c.wait()
    tk.wait_send(); ox.wait_send(); ix.wait_send()
    wait_bytes(gg.at[pl.ds(0, N - 1)], ss.at[2]); wait_bytes(ggr.at[pl.ds(0, N - 1)], ss.at[7])
    A.finish(wa.at[pl.ds(0, 7 * Z * ra)])
    F.finish(wf.at[pl.ds(0, 7 * Z)])
    SF.wait_send(); SA.wait_send()


def all_call(perm, lens, tok, cot, gm, am, fm, C, S):
    nf, nd = lax.axis_size("fsdp"), lax.axis_size("dp"); N = nf * nd; Z = nf // 2
    pos, D = tok.shape[1:]; L = pos * N; ra = am.shape[0]; R = fm.shape[0] // 3
    hbm = pl.BlockSpec(memory_space=pltpu.HBM); V = pl.BlockSpec(memory_space=pltpu.VMEM); SM = pl.BlockSpec(memory_space=pltpu.SMEM)
    sd = jax.ShapeDtypeStruct; Q = pltpu.SemaphoreType.DMA
    vm = lambda *s, dt=bf16: pltpu.VMEM(s, dt)
    return pl.pallas_call(functools.partial(all_kernel, nf, nd),
        out_shape=(sd(tok.shape, bf16), sd(tok.shape, bf16), sd((8, 128), f32), sd((ra, D), f32), sd((3 * R, D), f32)),
        in_specs=[SM, SM, hbm, hbm, V, hbm, hbm, hbm, hbm], out_specs=(hbm, hbm, V, hbm, hbm),
        scratch_shapes=[vm(L, D), vm(L, D), vm(L, D), vm(N * ra, D), vm(N, 3, R, D), vm(8, 128, dt=f32), vm(N, 8, 128, dt=f32), vm(8, D, dt=f32),
                        vm(8, D, dt=f32), vm(N, 8, 128, dt=f32), vm(N, 8, 128, dt=f32),
                        vm(L, D), vm(L, 3 * D), vm(H, 256, 256), vm(H, 256, 512), vm(N, pos, D), vm(L, D, dt=f32), vm(L, D), vm(L, D, dt=f32), vm(L, D, dt=f32),
                        vm(N * ra, D), vm(N, 3, R, D), vm(L, 128, dt=f32), vm(L, 128, dt=f32)]
                       + [vm(n, *sh) for sh in ((ra, D), (3, R, D)) for n in (4 * Z, 2 * Z, Z, Z + 1)]
                       + [Q((8,)), Q((6,)), Q((10,)), Q((Z, 2)), Q((Z, 2)), Q((Z, 8)), Q((Z, 8)), Q((4,)), Q((4,))] + [Q((n,)) for _ in range(2) for n in (4 * Z, 2 * Z, Z, Z + 1, Z)],
        compiler_params=pltpu.CompilerParams(collective_id=2, has_side_effects=True, vmem_limit_bytes=64 * 2**20))(perm, lens, tok, cot, gm, am, fm, C, S)


def update(w, q, m, v, decay, mo, vo, wo):
    m2 = beta_first * m + (1.0 - beta_first) * q
    v2 = beta_second * v + (1.0 - beta_second) * q * q
    mo[...] = m2
    vo[...] = v2
    new = w - learning_rate * ((m2 / (1.0 - beta_first**STEP)) / (jnp.sqrt(v2 / (1.0 - beta_second**STEP)) + adam_epsilon) + decay * w)
    wo[...] = new
    return new


def last_kernel(slot, *refs):
    ins, outs, iv, ov, isem, osem = refs[:14], refs[14:30], refs[30:44], refs[44:57], refs[57], refs[58]
    oo, io, gs, ag, fg = ins[:5]
    N = oo.shape[0]; gl = ins[11].shape[1]
    order = [8, 9, 10, 4, 5, 6, 7, 3, 1, 11, 12, 13, 2, 0]
    src = {k: pltpu.make_async_copy(ins[k], iv[i], isem.at[i]) for i, k in enumerate(order)}
    val = {k: iv[i] for i, k in enumerate(order)}
    for k in order: src[k].start()
    done = []
    def copy(a, b, i):
        c = pltpu.make_async_copy(a, b, osem.at[i]); c.start(); done.append(c)
    put = {k: i for i, k in enumerate((0, 4, 5, 6, 7, 8, 9, 10, 11, 12, 13, 14, 15))}
    def out(k): copy(ov[put[k]], outs[k], k)
    at = lambda k: ov[put[k]]
    for w, q, m, v, ks in ((8, 4, 9, 10, (7, 8, 12, 15)), (5, 3, 6, 7, (5, 6, 11, 14))):
        for k in (w, q, m, v): src[k].wait()
        new = update(val[w][...], val[q][...], val[m][...], val[v][...], weight_decay, at(ks[0]), at(ks[1]), at(ks[2]))
        at(ks[3])[...] = new.astype(bf16)
        for k in ks: out(k)
        copy(val[q], outs[q - 1], q - 1)
    src[1].wait()
    copy(val[1], outs[1], 1)
    for k in (11, 12, 13, 2): src[k].wait()
    q = val[2][0:2, 0:gl]
    w = val[11][...]
    at(4)[...] = q
    at(13)[...] = update(w, q, val[12][...], val[13][...], 0.0, at(9), at(10), at(13)) - w
    for k in (4, 9, 10, 13): out(k)
    src[0].wait()
    def pm(j): at(0)[j] = val[0][slot[j]]
    loop(0, N, pm)
    out(0)
    for c in done: c.wait()


def last_call(slot, oo, io, gs, ag, fg, am, amm, amv, fm, fmm, fmv, gm, gmm, gmv):
    A = pl.BlockSpec(memory_space=pltpu.HBM); SM = pl.BlockSpec(memory_space=pltpu.SMEM)
    sd = lambda a, dt=None: jax.ShapeDtypeStruct(a.shape, dt or a.dtype)
    args = (oo, io, gs, ag, fg, am, amm, amv, fm, fmm, fmv, gm, gmm, gmv)
    res = (sd(oo), sd(io), sd(am), sd(fm), sd(gm), sd(am), sd(am), sd(fm), sd(fm), sd(gm), sd(gm), sd(am), sd(fm), sd(gm), sd(am, bf16), sd(fm, bf16))
    vm = lambda a: pltpu.VMEM(a.shape, a.dtype)
    return pl.pallas_call(last_kernel, in_specs=[SM] + [A] * 14, out_specs=(A,) * 16, out_shape=res,
        scratch_shapes=[vm(args[k]) for k in (8, 9, 10, 4, 5, 6, 7, 3, 1, 11, 12, 13, 2, 0)] + [vm(res[k]) for k in (0, 4, 5, 6, 7, 8, 9, 10, 11, 12, 13, 14, 15)]
                       + [pltpu.SemaphoreType.DMA((14,)), pltpu.SemaphoreType.DMA((16,))],
        compiler_params=pltpu.CompilerParams(vmem_limit_bytes=64 * 2**20))(slot, *args)


def local_one(tokens, cotangent, lengths, device_sequence, slot_device, attention_master, feedforward_master, gains_master,
              attention_mean, attention_square, feedforward_mean, feedforward_square, gains_mean, gains_square):
    N = lax.axis_size(AX)
    counter = jnp.arange(N, dtype=jnp.int32)
    slot_sequence = jnp.sum(jnp.where(slot_device[:, None] == counter[None, :], device_sequence[None, :], 0), axis=1)
    slot_of_sequence = jnp.sum(jnp.where(slot_sequence[:, None] == counter[None, :], counter[:, None], 0), axis=0)
    tr = lambda a: a.transpose(1, 0, 2)
    C, S = tables(tokens.shape[1] * N)
    width = tokens.shape[2]
    oo, io, gs, ag, fg = all_call(slot_of_sequence, lengths, tokens, cotangent, gains_master, attention_master,
                                  tr(feedforward_master).reshape(-1, width), jnp.asarray(C), jnp.asarray(S))
    fg = fg.reshape(3, -1, width)
    r = list(last_call(slot_sequence, oo, io, gs, ag, fg, attention_master, attention_mean, attention_square,
                       tr(feedforward_master), tr(feedforward_mean), tr(feedforward_square), gains_master, gains_mean, gains_square))
    for i in (3, 7, 8, 12, 15): r[i] = tr(r[i])
    return tuple(r)


def solution(mesh):
    t, r, f, g = P(None, AX, None), P(AX, None), P(AX, None, None), P(None, AX)
    in_specs = (t, t, P(), P(), P(), r, f, g, r, r, f, f, g, g)
    out_specs = (t, t, r, f, g, r, r, f, f, g, g, r, f, g, r, f)
    n = mesh.shape["fsdp"] * mesh.shape["dp"]
    body = local_one if 512 // n % 16 == 0 and 3072 // n % 16 == 0 else local
    return jax.shard_map(body, mesh=mesh, in_specs=in_specs, out_specs=out_specs, check_vma=False)
```

```python
import functools
import jax, jax.numpy as jnp, numpy as np
from jax import lax
from jax.experimental import pallas as pl
from jax.experimental.pallas import tpu as pltpu
H=12; KVH=12; HD=64; STEP=4
norm_epsilon=1e-05; attn_multiplier=0.125; rope_theta=10000.0
f32=jnp.float32; bf16=jnp.bfloat16
LOG2E=1.4426950408889634

def dot_nt(a,b):
    return lax.dot_general(a,b,(((1,),(1,)),((),())),preferred_element_type=f32)
def dot_nn(a,b):
    return lax.dot_general(a,b,(((1,),(0,)),((),())),preferred_element_type=f32)
def dot_tn(a,b):
    return lax.dot_general(a,b,(((0,),(0,)),((),())),preferred_element_type=f32)

def tables(length):
    half=HD//2
    freq=(np.float32(rope_theta)**(-(np.arange(half,dtype=np.float32)*np.float32(2.0))/np.float32(HD))).astype(np.float32)
    ang=(np.arange(length,dtype=np.float32)[:,None]*freq[None,:]).astype(np.float32)
    c=np.cos(ang.astype(np.float64)).astype(np.float32); s=np.sin(ang.astype(np.float64)).astype(np.float32)
    C=np.concatenate([c,c,c,c],1); S=np.concatenate([-s,s,-s,s],1)
    return C,S

RB=64
def rows_loop(length, body):
    def it(i,carry):
        body(pl.ds(pl.multiple_of(i*RB,RB),RB), i*RB)
        return carry
    lax.fori_loop(0,length//RB,it,0)

def norm_block(xv, gain):
    inv=lax.rsqrt(jnp.mean(xv*xv,axis=-1,keepdims=True)+norm_epsilon)
    return inv

def swap_halves(x):
    lane=lax.broadcasted_iota(jnp.int32,x.shape,1)
    return jnp.where(lax.rem(lane,64)<32, pltpu.roll(x,96,1), pltpu.roll(x,32,1))

def phase_norm1(x_ref,g_ref,n1_ref):
    L=x_ref.shape[0]
    def body(r,_):
        xv=x_ref[r,:].astype(f32)
        inv=norm_block(xv,None)
        n1_ref[r,:]=(xv*inv*g_ref[0:1,:]).astype(bf16)
    rows_loop(L,body)

def phase_qkv(n1_ref,w_ref,cos_ref,sin_ref,qkv_ref):
    def rt(n,carry):
        o=pl.multiple_of(n*256,256)
        p=dot_nt(n1_ref[...],w_ref[pl.ds(o,256),:])
        for j in range(2):
            x=p[:,128*j:128*j+128]
            qkv_ref[:,pl.ds(pl.multiple_of(o+128*j,128),128)]=(x*cos_ref[...]+swap_halves(x)*sin_ref[...]).astype(bf16)
        return carry
    lax.fori_loop(0,6,rt,0)
    def vt(n,carry):
        o=pl.multiple_of(n*256,256)
        qkv_ref[:,pl.ds(o,256)]=dot_nt(n1_ref[...],w_ref[pl.ds(o,256),:]).astype(bf16)
        return carry
    lax.fori_loop(6,9,vt,0)

def lane_masks(a):
    lane=lax.broadcasted_iota(jnp.int32,a.shape,1)
    z=jnp.zeros_like(a)
    return jnp.where(lane<64,a,z), jnp.where(lane<64,z,a)

def phase_attn_fwd(qkv_ref,p_ref,o_ref):
    L=qkv_ref.shape[0]; QB=256
    def pair(t,carry):
        oq=pl.multiple_of(t*128,128); ok=pl.multiple_of(768+t*128,128); ov=pl.multiple_of(1536+t*128,128)
        for i in range(L//QB):
            kl=(i+1)*QB
            q=lane_masks(qkv_ref[i*QB:(i+1)*QB,pl.ds(oq,128)])
            k=qkv_ref[0:kl,pl.ds(ok,128)]
            v=lane_masks(qkv_ref[0:kl,pl.ds(ov,128)])
            ps=[]
            for h in range(2):
                s=dot_nt(q[h],k)
                row=lax.broadcasted_iota(jnp.int32,s.shape,0)+i*QB
                col=lax.broadcasted_iota(jnp.int32,s.shape,1)
                s=jnp.where(row>=col,s,-1e30)
                m=jnp.max(s,axis=-1,keepdims=True)
                e=jnp.exp2((s-m)*(attn_multiplier*LOG2E))
                pr=(e*(1.0/jnp.sum(e,axis=-1,keepdims=True))).astype(bf16)
                p_ref[2*t+h,i*QB:(i+1)*QB,0:kl]=pr
                ps.append(pr)
            o_ref[i*QB:(i+1)*QB,pl.ds(oq,128)]=dot_nn(jnp.concatenate(ps,1),jnp.concatenate(v,0)).astype(bf16)
        return carry
    lax.fori_loop(0,H//2,pair,0)

def phase_wo_norm2(o_ref,w_ref,x_ref,g_ref,hs_ref,n2_ref):
    L=x_ref.shape[0]; R=128
    def it(i,carry):
        r=pl.ds(pl.multiple_of(i*R,R),R)
        hs=x_ref[r,:].astype(f32)+dot_nn(o_ref[r,:],w_ref[2304:3072,:])
        hs_ref[r,:]=hs
        inv=norm_block(hs,None)
        n2_ref[r,:]=(hs*inv*g_ref[1:2,:]).astype(bf16)
        return carry
    lax.fori_loop(0,L//R,it,0)

def phase_ff(n2_ref,db2_ref,wff_ref,gff_ref,b2_ref,dn2_ref):
    sh=wff_ref.shape[2]; per=256//sh; nt=wff_ref.shape[0]//per
    def tile(t,carry):
        sl=pl.ds(t*per,per)
        wg=wff_ref[sl,0].reshape(256,768); wu=wff_ref[sl,1].reshape(256,768); wd=wff_ref[sl,2].reshape(256,768)
        n2=n2_ref[...]
        g=dot_nt(n2,wg); u=dot_nt(n2,wu)
        da=dot_nt(db2_ref[...],wd)
        sg=1.0/(1.0+jnp.exp2(g*(-LOG2E)))
        silu=g*sg
        a=(silu*u).astype(bf16)
        dg=(da*u*(sg*(1.0+g*(1.0-sg)))).astype(bf16)
        du=(da*silu).astype(bf16)
        b2=dot_nn(a,wd)
        dn=dot_nn(dg,wg)+dot_nn(du,wu)
        @pl.when(t==0)
        def _():
            b2_ref[...]=b2; dn2_ref[...]=dn
        @pl.when(t>0)
        def _():
            b2_ref[...]+=b2; dn2_ref[...]+=dn
        gff_ref[sl,0]=dot_tn(dg,n2).astype(bf16).reshape(per,sh,768)
        gff_ref[sl,1]=dot_tn(du,n2).astype(bf16).reshape(per,sh,768)
        gff_ref[sl,2]=dot_tn(a,db2_ref[...]).astype(bf16).reshape(per,sh,768)
        return carry
    lax.fori_loop(0,nt,tile,0)

def phase_mid(len_ref,c_ref,hs_ref,b2_ref,dn2_ref,g_ref,out_ref,dhs_ref,db1_ref,gg_ref):
    L=hs_ref.shape[0]
    n=len_ref[0]
    gg_ref[...]=jnp.zeros_like(gg_ref)
    def body(r,o):
        row=lax.broadcasted_iota(jnp.int32,(RB,768),0)+o
        hs=hs_ref[r,:]
        out_ref[r,:]=jnp.where(row<n,hs+b2_ref[r,:],0.0).astype(bf16)
        dy=jnp.where(row<n,c_ref[r,:].astype(f32),0.0)
        inv=norm_block(hs,None)
        dn=dn2_ref[r,:]
        q=dn*g_ref[1:2,:]
        gg_ref[1:2,:]+=jnp.sum(hs*inv*dn,axis=0,keepdims=True)
        dh=dy+(inv*q-hs*inv*inv*inv*jnp.mean(hs*q,axis=-1,keepdims=True))
        dhs_ref[r,:]=dh
        db1_ref[r,:]=dh.astype(bf16)
    rows_loop(L,body)

def phase_db2(len_ref,c_ref,db2_ref):
    n=len_ref[0]
    def body(r,o):
        row=lax.broadcasted_iota(jnp.int32,(RB,768),0)+o
        db2_ref[r,:]=jnp.where(row<n,c_ref[r,:].astype(f32),0.0).astype(bf16)
    rows_loop(c_ref.shape[0],body)

def phase_wo_back(db1_ref,o_ref,w_ref,do_ref,gatt_ref):
    def it(n,carry):
        o=pl.multiple_of(n*256,256)
        do_ref[:,pl.ds(o,256)]=dot_nt(db1_ref[...],w_ref[pl.ds(pl.multiple_of(2304+o,256),256),:]).astype(bf16)
        gatt_ref[pl.ds(pl.multiple_of(2304+o,256),256),:]=dot_tn(o_ref[:,pl.ds(o,256)],db1_ref[...]).astype(bf16)
        return carry
    lax.fori_loop(0,3,it,0)

def phase_attn_bwd(qkv_ref,p_ref,do_ref,cos_ref,sin_ref,dp_ref):
    L=qkv_ref.shape[0]; QB=256
    def pair(t,carry):
        oq=pl.multiple_of(t*128,128); ok=pl.multiple_of(768+t*128,128); ov=pl.multiple_of(1536+t*128,128)
        dkt=None; dvt=None
        for i in range(L//QB):
            kl=(i+1)*QB; r=slice(i*QB,(i+1)*QB)
            q=lane_masks(qkv_ref[r,pl.ds(oq,128)])
            k=lane_masks(qkv_ref[0:kl,pl.ds(ok,128)])
            v=qkv_ref[0:kl,pl.ds(ov,128)]
            do=lane_masks(do_ref[r,pl.ds(oq,128)])
            dss=[]; pls=[]
            for h in range(2):
                pb=p_ref[2*t+h,r,0:kl]
                p=pb.astype(f32)
                if i<L//QB:
                    row=lax.broadcasted_iota(jnp.int32,p.shape,0)+i*QB
                dpr=dot_nt(do[h],v)
                pd=p*dpr
                ds=(pd-p*jnp.sum(pd,axis=-1,keepdims=True)).astype(bf16)
                dss.append(ds); pls.append(pb)
            dq=dot_nn(jnp.concatenate(dss,1),jnp.concatenate(k,0))*attn_multiplier
            c=cos_ref[r,:]; s=sin_ref[r,:]
            dp_ref[r,pl.ds(oq,128)]=(dq*c-swap_halves(dq)*s).astype(bf16)
            a=dot_tn(jnp.concatenate(q,0),jnp.concatenate(dss,0))
            b=dot_tn(jnp.concatenate(do,0),jnp.concatenate(pls,0))
            if dkt is None: dkt,dvt=a,b
            else:
                w=dkt.shape[1]
                dkt=jnp.concatenate([dkt+a[:,:w],a[:,w:]],1); dvt=jnp.concatenate([dvt+b[:,:w],b[:,w:]],1)
        dk=dkt.T*attn_multiplier
        dp_ref[:,pl.ds(ok,128)]=(dk*cos_ref[...]-swap_halves(dk)*sin_ref[...]).astype(bf16)
        dp_ref[:,pl.ds(ov,128)]=dvt.T.astype(bf16)
        return carry
    lax.fori_loop(0,H//2,pair,0)

def phase_dn1(dp_ref,w_ref,x_ref,g_ref,dhs_ref,in_ref,gg_ref):
    L=x_ref.shape[0]; R=128
    def it(i,carry):
        r=pl.ds(pl.multiple_of(i*R,R),R)
        dn=dot_nn(dp_ref[r,:],w_ref[0:2304,:])
        xv=x_ref[r,:].astype(f32)
        inv=norm_block(xv,None)
        gg_ref[0:1,:]+=jnp.sum(xv*inv*dn,axis=0,keepdims=True)
        q=dn*g_ref[0:1,:]
        in_ref[r,:]=(dhs_ref[r,:]+(inv*q-xv*inv*inv*inv*jnp.mean(xv*q,axis=-1,keepdims=True))).astype(bf16)
        return carry
    lax.fori_loop(0,L//R,it,0)

def phase_wqkv_grad(dp_ref,n1_ref,gatt_ref):
    def it(n,carry):
        o=pl.multiple_of(n*256,256)
        gatt_ref[pl.ds(o,256),:]=dot_tn(dp_ref[:,pl.ds(o,256)],n1_ref[...]).astype(bf16)
        return carry
    lax.fori_loop(0,9,it,0)

def k2_kernel(len_ref,x_ref,c_ref,watt_ref,wff_ref,g_ref,cos_ref,sin_ref,
              out_ref,in_ref,gatt_ref,gff_ref,gg_ref,
              n1,qkv,pm,o,hs,n2,db2,b2,dn2,dhs,db1,do,dpj):
    phase_norm1(x_ref,g_ref,n1)
    phase_qkv(n1,watt_ref,cos_ref,sin_ref,qkv)
    phase_attn_fwd(qkv,pm,o)
    phase_wo_norm2(o,watt_ref,x_ref,g_ref,hs,n2)
    phase_db2(len_ref,c_ref,db2)
    phase_ff(n2,db2,wff_ref,gff_ref,b2,dn2)
    phase_mid(len_ref,c_ref,hs,b2,dn2,g_ref,out_ref,dhs,db1,gg_ref)
    phase_wo_back(db1,o,watt_ref,do,gatt_ref)
    phase_attn_bwd(qkv,pm,do,cos_ref,sin_ref,dpj)
    phase_dn1(dpj,watt_ref,x_ref,g_ref,dhs,in_ref,gg_ref)
    phase_wqkv_grad(dpj,n1,gatt_ref)

def k2(length,x,c,watt,wff,gains,cos,sin,kern=k2_kernel):
    L,D=x.shape
    V=pl.BlockSpec(memory_space=pltpu.VMEM)
    vm=lambda *s,dt=bf16: pltpu.VMEM(s,dt)
    return pl.pallas_call(kern,
        out_shape=(jax.ShapeDtypeStruct((L,D),bf16),jax.ShapeDtypeStruct((L,D),bf16),jax.ShapeDtypeStruct(watt.shape,bf16),jax.ShapeDtypeStruct(wff.shape,bf16),jax.ShapeDtypeStruct((8,D),f32)),
        in_specs=[pl.BlockSpec(memory_space=pltpu.SMEM)]+[V]*7,out_specs=(V,)*5,
        scratch_shapes=[vm(L,D),vm(L,3*D),vm(H,L,L),vm(L,D),vm(L,D,dt=f32),vm(L,D),vm(L,D),vm(L,D,dt=f32),vm(L,D,dt=f32),vm(L,D,dt=f32),vm(L,D),vm(L,D),vm(L,3*D)],
        compiler_params=pltpu.CompilerParams(vmem_limit_bytes=63*2**20),
        )(length,x,c,watt,wff,gains,cos,sin)
MESH=pl.DeviceIdType.MESH

class Topo:
    def __init__(s, nf, nd):
        assert nd==4 and nf%2==0
        s.Z=nf//2; s.N=nf*nd
        f=lax.axis_index("fsdp"); d=lax.axis_index("dp")
        s.z=f//2; s.y=lax.rem(f,2); s.x=d//2; s.c=lax.rem(d,2)
        s.me=f*4+d
        c=s.c
        s.y1=s.y+c*(1-2*s.y); s.x1=s.x+(1-c)*(1-2*s.x)
        s.y2=s.y+(1-c)*(1-2*s.y); s.x2=s.x+c*(1-2*s.x)
        s.yb=1-s.y; s.xb=1-s.x; s.cb=1-c
    def slot(s,z,y,x,c): return ((z*2+y)*2+x)*2+c
    def dev(s,z,y,x,c): return (z*2+y, x*2+c)
    def flat(s,i): return (i//4, lax.rem(i,4))
    def zk(s,k): return lax.rem(s.z+k,s.Z)
    @property
    def p1(s): return s.dev(s.z,s.y1,s.x1,s.c)
    @property
    def p2(s): return s.dev(s.z,s.y2,s.x2,s.c)
    @property
    def sib(s): return s.dev(s.z,s.y,s.x,s.cb)

def loop(lo,hi,body):
    lax.fori_loop(lo,hi,lambda i,c:(body(i),c)[1],0)

def rcopy(src,dst,ssem,rsem,dev):
    return pltpu.make_async_remote_copy(src_ref=src,dst_ref=dst,send_sem=ssem,recv_sem=rsem,device_id=dev,device_id_type=MESH)

def wait_bytes(ref,sem):
    pltpu.make_async_copy(ref,ref,sem).wait()

def barrier_all(t):
    b=pltpu.get_barrier_semaphore()
    def sig(k): pl.semaphore_signal(b,inc=1,device_id=t.flat(lax.rem(t.me+k,t.N)),device_id_type=MESH)
    loop(1,t.N,sig)
    pl.semaphore_wait(b,t.N-1)

class A2A:
    def __init__(s,t,src,dst,ssem,rsem,lsem): s.t,s.src,s.dst,s.ssem,s.rsem,s.lsem=t,src,dst,ssem,rsem,lsem
    def start(s):
        t=s.t
        pltpu.make_async_copy(s.src.at[t.me],s.dst.at[t.me],s.lsem).start()
        def f(k):
            d=lax.rem(t.me+k,t.N)
            rcopy(s.src.at[d],s.dst.at[t.me],s.ssem,s.rsem,t.flat(d)).start()
        loop(1,t.N,f)
    def wait_recv(s):
        n=s.t.N-1
        pltpu.make_async_copy(s.src.at[s.t.me],s.dst.at[s.t.me],s.lsem).wait()
        wait_bytes(s.dst.at[pl.ds(0,n)],s.rsem)
    def wait_send(s):
        wait_bytes(s.src.at[pl.ds(0,s.t.N-1)],s.ssem)

class Gather:
    def __init__(s,t,src,dst,ssem,rsem,lsem): s.t,s.src,s.dst,s.ssem,s.rsem,s.lsem=t,src,dst,ssem,rsem,lsem
    def send(s,slot,dev,src=None):
        rcopy(s.dst.at[slot] if src is None else src,s.dst.at[slot],s.ssem,s.rsem.at[slot],dev).start()
    def wait(s,slot):
        wait_bytes(s.dst.at[slot],s.rsem.at[slot])
    def start(s):
        t=s.t
        pltpu.make_async_copy(s.src,s.dst.at[t.me],s.lsem).start()
        for dev in (t.p1,t.p2,t.sib): s.send(t.me,dev,s.src)
        loop(1,t.Z,lambda k: s.send(t.me,t.dev(t.zk(k),t.y,t.x,t.c),s.src))
    def phase1(s):
        t=s.t
        def f(k):
            sl=t.slot(t.zk(k),t.y,t.x,t.c); s.wait(sl)
            for dev in (t.p1,t.p2,t.sib): s.send(sl,dev)
        loop(1,t.Z,f)
    def phase2(s):
        t=s.t
        def f(k):
            sl=t.slot(t.zk(k),t.y1,t.x1,t.c); s.wait(sl)
            for dev in (t.p2,t.sib): s.send(sl,dev)
        loop(0,t.Z,f)
    def phase3(s):
        t=s.t
        for y,x in ((t.y2,t.x2),(t.yb,t.xb)):
            def f(k):
                sl=t.slot(t.zk(k),y,x,t.c); s.wait(sl); s.send(sl,t.sib)
            loop(0,t.Z,f)
    def phase4(s):
        t=s.t
        for y,x in ((0,0),(0,1),(1,0),(1,1)):
            loop(0,t.Z,lambda k: s.wait(t.slot(t.zk(k),y,x,t.cb)))
    def finish(s):
        t=s.t
        pltpu.make_async_copy(s.src,s.dst.at[t.me],s.lsem).wait()
        wait_bytes(s.dst.at[pl.ds(0,t.N-1)],s.ssem)

def k1_kernel(nf,nd,perm,tok,cot0,gn,att,ff,xg,cg,gg,wa,wf,cot,ss,rs,ls,ars,frs):
    t=Topo(nf,nd)
    barrier_all(t)
    tk=A2A(t,tok,xg,ss.at[0],rs.at[0],ls.at[0])
    ct=A2A(t,cot,cg,ss.at[1],rs.at[1],ls.at[1])
    A=Gather(t,att,wa,ss.at[3],ars,ls.at[3]); F=Gather(t,ff,wf,ss.at[4],frs,ls.at[4])
    pltpu.make_async_copy(gn,gg.at[t.me],ls.at[2]).start()
    def gs(k): rcopy(gn,gg.at[t.me],ss.at[2],rs.at[2],t.flat(lax.rem(t.me+k,t.N))).start()
    loop(1,t.N,gs)
    A.start()
    tk.start()
    def pm(i): cot[i]=cot0[perm[i]]
    loop(0,t.N,pm)
    A.phase1()
    F.start()
    A.phase2()
    F.phase1()
    A.phase3()
    F.phase2()
    ct.start()
    A.phase4()
    F.phase3(); F.phase4()
    tk.wait_recv(); ct.wait_recv()
    pltpu.make_async_copy(gn,gg.at[t.me],ls.at[2]).wait()
    wait_bytes(gg.at[pl.ds(0,t.N-1)],rs.at[2]); wait_bytes(gg.at[pl.ds(0,t.N-1)],ss.at[2])
    A.finish(); F.finish(); tk.wait_send(); ct.wait_send()

def k1(perm,tok,cot,gn,att,ff):
    nf,nd=lax.axis_size("fsdp"),lax.axis_size("dp"); N=nf*nd
    anyv=pl.BlockSpec(memory_space=pl.ANY); D=pltpu.SemaphoreType.DMA
    sd=jax.ShapeDtypeStruct
    return pl.pallas_call(functools.partial(k1_kernel,nf,nd),
        out_shape=(sd(tok.shape,tok.dtype),sd(cot.shape,cot.dtype),sd((N,)+gn.shape,gn.dtype),sd((N,)+att.shape,att.dtype),sd((N,)+ff.shape,ff.dtype)),
        in_specs=[pl.BlockSpec(memory_space=pltpu.SMEM),anyv,pl.BlockSpec(memory_space=pltpu.VMEM),anyv,anyv,anyv],out_specs=(anyv,)*5,
        scratch_shapes=[pltpu.VMEM(cot.shape,cot.dtype),D((5,)),D((5,)),D((5,)),D((N,)),D((N,))],
        compiler_params=pltpu.CompilerParams(collective_id=0,has_side_effects=True))(perm,tok,cot,gn,att,ff)

class Scatter:
    def __init__(s,t,g,rc,r1,r2,rz,ss,rcs,r1s,r2s,rzs):
        s.t,s.g,s.rc,s.r1,s.r2,s.rz,s.ss,s.rcs,s.r1s,s.r2s,s.rzs=t,g,rc,r1,r2,rz,ss,rcs,r1s,r2s,rzs
        s.Z=t.Z
    def groups(s,sibling):
        t=s.t
        if sibling:
            return ((t.yb,t.xb),(t.y1,t.x1),(t.y2,t.x2),(t.y,t.x))
        return ((t.yb,t.xb),(t.y2,t.x2),(t.y1,t.x1),(t.y,t.x))
    def start(s):
        t=s.t; Z=s.Z
        for gi,(y,x) in enumerate(s.groups(True)):
            def f(k):
                rcopy(s.g.at[t.slot(t.zk(k),y,x,t.cb)],s.rc.at[gi*Z+k],s.ss.at[0],s.rcs.at[gi*Z+k],t.sib).start()
            loop(0,Z,f)
    def stage_c(s):
        t=s.t; Z=s.Z
        for gi,(y,x) in enumerate(s.groups(False)):
            def f(k):
                j=gi*Z+k
                wait_bytes(s.rc.at[j],s.rcs.at[j])
                s.rc[j]=s.rc[j]+s.g[t.slot(t.zk(k),y,x,t.c)]
                if gi<2: rcopy(s.rc.at[j],s.r1.at[j],s.ss.at[1],s.r1s.at[j],t.p2).start()
            loop(0,Z,f)
    def stage_1(s):
        t=s.t; Z=s.Z
        for gi in range(2):
            def f(k):
                j=gi*Z+k
                wait_bytes(s.r1.at[j],s.r1s.at[j])
                s.r1[j]=s.r1[j]+s.rc[2*Z+j]
                if gi==0: rcopy(s.r1.at[j],s.r2.at[k],s.ss.at[2],s.r2s.at[k],t.p1).start()
            loop(0,Z,f)
    def stage_2(s):
        t=s.t; Z=s.Z
        def f(k):
            wait_bytes(s.r2.at[k],s.r2s.at[k])
            s.r2[k]=s.r2[k]+s.r1[Z+k]
            rcopy(s.r2.at[k],s.rz.at[Z-k-1],s.ss.at[3],s.rzs.at[Z-k-1],t.dev(t.zk(k),t.y,t.x,t.c)).start()
        loop(1,Z,f)
        wait_bytes(s.r2.at[0],s.r2s.at[0])
    def final(s,out):
        Z=s.Z
        tot=s.r2[0].astype(f32)+s.r1[Z].astype(f32)
        for k in range(Z-1):
            wait_bytes(s.rz.at[k],s.rzs.at[k])
            tot=tot+s.rz[k].astype(f32)
        out[...]=tot
    def wait_send(s):
        Z=s.Z
        wait_bytes(s.rc,s.ss.at[0])
        wait_bytes(s.r1,s.ss.at[1])
        wait_bytes(s.r2,s.ss.at[2])
        wait_bytes(s.rz,s.ss.at[3])

def k3_kernel(nf,nd,perm,orow,irow,gg,ga,gf,oo0,io,ggo,ao,fo,oo,ggr,arc,ar1,ar2,arz,frc,fr1,fr2,frz,ss,rs,ls,ass,fss,acs,a1s,a2s,azs,fcs,f1s,f2s,fzs):
    t=Topo(nf,nd)
    barrier_all(t)
    A=Scatter(t,ga,arc,ar1,ar2,arz,ass,acs,a1s,a2s,azs)
    F=Scatter(t,gf,frc,fr1,fr2,frz,fss,fcs,f1s,f2s,fzs)
    F.start(); A.start()
    pltpu.make_async_copy(gg.at[t.me],ggr.at[t.me],ls.at[2]).start()
    def gs(k):
        d=lax.rem(t.me+k,t.N)
        rcopy(gg.at[d],ggr.at[t.me],ss.at[2],rs.at[2],t.flat(d)).start()
    loop(1,t.N,gs)
    F.stage_c()
    o=A2A(t,orow,oo,ss.at[0],rs.at[0],ls.at[0])
    i=A2A(t,irow,io,ss.at[1],rs.at[1],ls.at[1])
    o.start()
    A.stage_c()
    i.start()
    F.stage_1(); F.stage_2()
    A.stage_1(); A.stage_2()
    pltpu.make_async_copy(gg.at[t.me],ggr.at[t.me],ls.at[2]).wait()
    wait_bytes(ggr.at[pl.ds(0,t.N-1)],rs.at[2]); wait_bytes(ggr.at[pl.ds(0,t.N-1)],ss.at[2])
    tot=ggr[0]
    for k in range(1,t.N): tot=tot+ggr[k]
    ggo[...]=tot
    F.final(fo); A.final(ao)
    o.wait_recv()
    def pm(j): oo0[j]=oo[perm[j]]
    loop(0,t.N,pm)
    i.wait_recv(); o.wait_send(); i.wait_send()
    F.wait_send(); A.wait_send()

def k3(perm,orow,irow,gg,ga,gf):
    nf,nd=lax.axis_size("fsdp"),lax.axis_size("dp"); N=nf*nd; Z=nf//2
    anyv=pl.BlockSpec(memory_space=pl.ANY); V=pl.BlockSpec(memory_space=pltpu.VMEM); D=pltpu.SemaphoreType.DMA
    sd=jax.ShapeDtypeStruct
    ash,fsh=ga.shape[1:],gf.shape[1:]
    vm=lambda n,sh: pltpu.VMEM((n,)+sh,bf16)
    return pl.pallas_call(functools.partial(k3_kernel,nf,nd),
        out_shape=(sd(orow.shape,bf16),sd(irow.shape,bf16),sd(gg.shape[1:],f32),sd(ash,f32),sd(fsh,f32)),
        in_specs=[pl.BlockSpec(memory_space=pltpu.SMEM),anyv,anyv,V,V,V],out_specs=(V,anyv,V,V,V),
        scratch_shapes=[pltpu.VMEM(orow.shape,bf16),pltpu.VMEM(gg.shape,f32)]+[vm(n,sh) for sh in (ash,fsh) for n in (4*Z,2*Z,Z,Z-1)]+[D((3,)),D((3,)),D((3,)),D((4,)),D((4,))]+[D((n,)) for _ in range(2) for n in (4*Z,2*Z,Z,Z-1)],
        compiler_params=pltpu.CompilerParams(collective_id=1,has_side_effects=True,vmem_limit_bytes=60*2**20))(perm,orow,irow,gg,ga,gf)


from jax.sharding import PartitionSpec as P
AX = ("fsdp", "dp")
beta_first = 0.5
beta_second = 0.5
learning_rate = 0.03
weight_decay = 0.1
adam_epsilon = 1e-08


def adam_update(master, gradient, first_moment, second_moment, decay):
    first_new = beta_first * first_moment + (1.0 - beta_first) * gradient
    second_new = beta_second * second_moment + (1.0 - beta_second) * gradient * gradient
    first_hat = first_new / (1.0 - beta_first**STEP)
    second_hat = second_new / (1.0 - beta_second**STEP)
    master_new = master - learning_rate * (
        first_hat / (jnp.sqrt(second_hat) + adam_epsilon) + decay * master
    )
    return (first_new, second_new, master_new)


def local(tokens, cotangent, lengths, device_sequence, slot_device, attention_master, feedforward_master, gains_master,
          attention_mean, attention_square, feedforward_mean, feedforward_square, gains_mean, gains_square):
    N = lax.axis_size(AX)
    me = lax.axis_index(AX)
    positions, width = tokens.shape[1], tokens.shape[2]
    length = positions * N
    gl = gains_master.shape[1]
    counter = jnp.arange(N, dtype=jnp.int32)
    slot_sequence = jnp.sum(jnp.where(slot_device[:, None] == counter[None, :], device_sequence[None, :], 0), axis=1)
    slot_of_sequence = jnp.sum(jnp.where(slot_sequence[:, None] == counter[None, :], counter[:, None], 0), axis=0)
    att_low = attention_master.astype(bf16)
    ff_low = feedforward_master.transpose(1, 0, 2).astype(bf16)
    gn = jnp.zeros((8, 128), f32).at[:2, :gl].set(gains_master.astype(bf16).astype(f32))
    xg, cg, gg, wa, wf = k1(slot_of_sequence, tokens, cotangent, gn, att_low, ff_low)
    gains = jnp.zeros((8, width), f32).at[:2].set(gg[:, :2, :gl].transpose(1, 0, 2).reshape(2, width))
    C, S = tables(length)
    orow, irow, gatt, gff, ggr = k2(jnp.sum(jnp.where(counter == me, lengths, 0))[None], xg.reshape(length, width), cg.reshape(length, width),
                                    wa.reshape(-1, width), wf, gains, jnp.asarray(C), jnp.asarray(S))
    gblocks = jnp.zeros((N, 8, 128), f32).at[:, :2, :gl].set(ggr[:2].reshape(2, N, gl).transpose(1, 0, 2))
    oo, io, gsum, ag, fg = k3(slot_sequence, orow.reshape(N, positions, width), irow.reshape(N, positions, width), gblocks,
                              gatt.reshape(N, -1, width), gff)
    output = oo
    attention_gradient = ag
    feedforward_gradient = fg.transpose(1, 0, 2)
    gains_gradient = gsum[:2, :gl]
    mean_attention, square_attention, master_attention = adam_update(
        attention_master, attention_gradient, attention_mean, attention_square, weight_decay)
    mean_feedforward, square_feedforward, master_feedforward = adam_update(
        feedforward_master, feedforward_gradient, feedforward_mean, feedforward_square, weight_decay)
    mean_gains, square_gains, master_gains = adam_update(gains_master, gains_gradient, gains_mean, gains_square, 0.0)
    return (output, io, attention_gradient, feedforward_gradient, gains_gradient, mean_attention, square_attention,
            mean_feedforward, square_feedforward, mean_gains, square_gains, master_attention, master_feedforward,
            master_gains - gains_master, master_attention.astype(bf16), master_feedforward.astype(bf16))


class Topo2(Topo):
    def __init__(s, nf, nd):
        super().__init__(nf, nd)
    def flip(s, gi, cc):
        a, b = lax.rem(gi, 2), gi // 2
        fx, fy = (1 - cc) * a + cc * b, (1 - cc) * b + cc * a
        return s.y + fy * (1 - 2 * s.y), s.x + fx * (1 - 2 * s.x)
    def g8(s, gi, cc):
        y, x = s.flip(gi, cc)
        return (y * 2 + x) * 2 + cc


def near(t, i):
    r = 0
    for z in range(t.Z):
        by = sorted(range(t.Z), key=lambda q: (abs(q - z), q))
        for k in range(t.Z): r = r + jnp.where((t.z == z) & (i == k), by[k], 0)
    return r


class Gather2:
    def __init__(s, t, at, ssem, zsem, rsem): s.t, s.at, s.ssem, s.zsem, s.rsem = t, at, ssem, zsem, rsem
    def send(s, z, g, dev):
        rcopy(s.at(z, g), s.at(z, g), s.ssem, s.rsem.at[z, g], dev).start()
    def wait(s, z, g): wait_bytes(s.at(z, g), s.rsem.at[z, g])
    def along(s, z, g, side, f):
        t = s.t
        @pl.when((t.z + side >= 0) & (t.z + side < t.Z))
        def _(): f(rcopy(s.at(z, g), s.at(z, g), s.zsem.at[z, (side + 1) // 2], s.rsem.at[z, g], t.dev(t.z + side, t.y, t.x, t.c)))
    def start(s):
        t = s.t; g = t.g8(0, t.c)
        for side in (-1, 1): s.along(t.z, g, side, lambda c: c.start())
        for dev in (t.p1, t.p2, t.sib): s.send(t.z, g, dev)
    def sweep(s, lo, hi, f):
        t = s.t
        def step(j):
            @pl.when(t.z - j >= 0)
            def _(): f(t.z - j, -1)
            @pl.when(t.z + j < t.Z)
            def _(): f(t.z + j, 1)
        if lo == 0: f(t.z, 0)
        loop(max(lo, 1), hi, step)
    def take(s, gi, lo=0, hi=None):
        t = s.t; g = t.g8(gi, t.c)
        to = {0: (t.p1, t.p2, t.sib), 1: (t.p2, t.sib)}.get(gi, (t.sib,))
        def f(z, side):
            s.wait(z, g)
            if gi == 0: s.along(z, g, -side, lambda c: c.start())
            for dev in to: s.send(z, g, dev)
        s.sweep(lo, t.Z if hi is None else hi, f)
    def take_sib(s, gi, lo=0, hi=None):
        t = s.t; g = t.g8(gi, t.cb)
        s.sweep(lo, t.Z if hi is None else hi, lambda z, side: s.wait(z, g))
    def finish(s, bulk):
        t = s.t; g = t.g8(0, t.c)
        wait_bytes(bulk, s.ssem)
        for side in (-1, 1): s.along(t.z, g, side, lambda c: c.wait_send())
        s.sweep(1, t.Z, lambda z, side: s.along(z, g, -side, lambda c: c.wait_send()))


SEQ = ((0, 1), (1, 0), (0, 2), (1, 1), (2, 0), (0, 3), (1, 2), (2, 1), (3, 0), (1, 3), (2, 2), (3, 1), (2, 3), (3, 2), (3, 3))


class Scatter3:
    def __init__(s, t, at, ld, rc, r1, r2, rz, ss, rcs, r1s, r2s, rzs, zss, far=True):
        s.far = far
        s.t, s.at, s.ld, s.rc, s.r1, s.r2, s.rz, s.ss, s.rcs, s.r1s, s.r2s, s.rzs, s.zss = t, at, ld, rc, r1, r2, rz, ss, rcs, r1s, r2s, rzs, zss
        s.Z = Z = t.Z
        far_order = [sorted(range(Z), key=lambda q: (-abs(q - z), (q > z) == (z < Z // 2))) for z in range(Z)]
        s.order = far_order if far else [sorted(range(Z), key=lambda q: (abs(q - z), q)) for z in range(Z)]
    def zof(s, i):
        r = 0
        for z in range(s.Z): r = r + jnp.where(s.t.z == z, s.order[z][i], 0)
        return r
    def start(s, z):
        t = s.t
        for gi in range(4):
            j = (3 - gi) * s.Z + z
            rcopy(s.at(z, t.g8(gi, t.cb)), s.rc.at[j], s.ss.at[0], s.rcs.at[j], t.sib).start()
    def chip(s, z, gs):
        t = s.t; Z = s.Z
        for gi in gs:
            j = (3 - gi) * Z + z
            wait_bytes(s.rc.at[j], s.rcs.at[j])
            s.rc[j] = s.rc[j] + s.ld(z, t.g8(gi, t.c))
            if gi >= 2: rcopy(s.rc.at[j], s.r1.at[j], s.ss.at[1], s.r1s.at[j], t.p2).start()
    def first(s, z):
        t = s.t; Z = s.Z
        for h in range(2):
            j = h * Z + z
            wait_bytes(s.r1.at[j], s.r1s.at[j])
            s.r1[j] = s.r1[j] + s.rc[2 * Z + j]
            if h == 0: rcopy(s.r1.at[z], s.r2.at[z], s.ss.at[2], s.r2s.at[z], t.p1).start()
    def hop(s, z, side):
        t = s.t
        j = jnp.where((z == t.z + side) & (side < 0), s.Z, z)
        return rcopy(s.r2.at[z], s.rz.at[j], s.zss.at[z], s.rzs.at[j], t.dev(t.z + side, t.y, t.x, t.c))
    def second(s, z):
        t = s.t; Z = s.Z
        wait_bytes(s.r2.at[z], s.r2s.at[z])
        s.r2[z] = s.r2[z] + s.r1[Z + z]
    def line(s, z):
        t = s.t; Z = s.Z
        for side in (-1, 1):
            @pl.when((z - t.z) * side > 0)
            def _():
                @pl.when((t.z - side >= 0) & (t.z - side < Z))
                def _():
                    wait_bytes(s.rz.at[z], s.rzs.at[z])
                    s.r2[z] = s.r2[z] + s.rz[z]
                s.hop(z, side).start()
    def C(s, *ii):
        for i in ii: s.chip(s.zof(i), (3, 2, 1, 0))
    def F(s, *ii):
        for i in ii: s.first(s.zof(i))
    def straight(s, z):
        t = s.t
        return rcopy(s.r2.at[z], s.rz.at[t.z], s.zss.at[z], s.rzs.at[t.z], t.dev(z, t.y, t.x, t.c))
    def D(s, *ii):
        for i in ii:
            z = s.zof(i)
            s.second(z)
            @pl.when(z != s.t.z)
            def _(): s.straight(z).start()
    def S(s, *ii):
        for i in ii: s.second(s.zof(i)); s.line(s.zof(i))
    def total(s):
        t = s.t; Z = s.Z
        tot = s.r2[t.z].astype(f32)
        if not s.far:
            for q in range(Z):
                @pl.when(t.z != q)
                def _(): wait_bytes(s.rz.at[q], s.rzs.at[q])
                @pl.when(t.z == q)
                def _(): s.rz[q] = jnp.zeros(s.rz.shape[1:], bf16)
                tot = tot + s.rz[q].astype(f32)
            return tot
        below = jnp.where(t.z > 0, 1.0, 0.0); above = jnp.where(t.z < Z - 1, 1.0, 0.0)
        @pl.when(t.z > 0)
        def _(): wait_bytes(s.rz.at[t.z], s.rzs.at[t.z])
        @pl.when(t.z == 0)
        def _(): s.rz[t.z] = jnp.zeros(s.rz.shape[1:], bf16)
        @pl.when(t.z < Z - 1)
        def _(): wait_bytes(s.rz.at[Z], s.rzs.at[Z])
        @pl.when(t.z == Z - 1)
        def _(): s.rz[Z] = jnp.zeros(s.rz.shape[1:], bf16)
        return tot + (s.rz[t.z].astype(f32) + s.rz[Z].astype(f32))
    def wait_send(s):
        t = s.t; Z = s.Z
        wait_bytes(s.rc, s.ss.at[0]); wait_bytes(s.r1, s.ss.at[1]); wait_bytes(s.r2, s.ss.at[2])
        def f(z):
            if not s.far:
                @pl.when(z != t.z)
                def _(): s.straight(z).wait_send()
                return
            for side in (-1, 1):
                @pl.when((z - t.z) * side > 0)
                def _(): s.hop(z, side).wait_send()
        loop(0, Z, f)


class Exchange:
    def __init__(s, t, src, dst, sbulk, dbulk, ssem, rsem, lsem):
        s.t, s.src, s.dst, s.sbulk, s.dbulk, s.ssem, s.rsem, s.lsem = t, src, dst, sbulk, dbulk, ssem, rsem, lsem
        s.sent = 1
    def start(s): pltpu.make_async_copy(s.src(s.t.me), s.dst(s.t.me), s.lsem).start()
    def more(s, n):
        t = s.t
        def f(k):
            d = lax.rem(t.me + k, t.N)
            rcopy(s.src(d), s.dst(t.me), s.ssem, s.rsem, t.flat(d)).start()
        to = min(t.N, s.sent + n)
        if to > s.sent: loop(s.sent, to, f)
        s.sent = to
    def wait_recv(s):
        pltpu.make_async_copy(s.src(s.t.me), s.dst(s.t.me), s.lsem).wait()
        wait_bytes(s.dbulk, s.rsem)
    def wait_send(s): wait_bytes(s.sbulk, s.ssem)


def rows_of(ref, n):
    return lambda d: ref.at[pl.ds(pl.multiple_of(d * n, n), n)]


def attn_fwd2(qkv_ref, ps, o_ref, lo, hi):
    QB = 256
    def pair(t, carry):
        oq = pl.multiple_of(t * 128, 128); ok = pl.multiple_of(768 + t * 128, 128); ov = pl.multiple_of(1536 + t * 128, 128)
        for i in range(len(ps)):
            kl = (i + 1) * QB
            q = lane_masks(qkv_ref[i * QB:kl, pl.ds(oq, 128)])
            k = qkv_ref[0:kl, pl.ds(ok, 128)]
            v = lane_masks(qkv_ref[0:kl, pl.ds(ov, 128)])
            got = []
            for h in range(2):
                s = dot_nt(q[h], k)
                row = lax.broadcasted_iota(jnp.int32, s.shape, 0) + i * QB
                col = lax.broadcasted_iota(jnp.int32, s.shape, 1)
                s = jnp.where(row >= col, s, -1e30)
                m = jnp.max(s, axis=-1, keepdims=True)
                e = jnp.exp2((s - m) * (attn_multiplier * LOG2E))
                pr = (e * (1.0 / jnp.sum(e, axis=-1, keepdims=True))).astype(bf16)
                ps[i][2 * t + h] = pr
                got.append(pr)
            n = o_ref.shape[1]
            o_ref[i * QB // n:kl // n, :, pl.ds(oq, 128)] = dot_nn(jnp.concatenate(got, 1), jnp.concatenate(v, 0)).astype(bf16).reshape(QB // n, n, 128)
        return carry
    lax.fori_loop(lo, hi, pair, 0)


def attn_bwd2(qkv_ref, ps, do_ref, cos_ref, sin_ref, lo, hi):
    QB = 256
    def pair(t, carry):
        oq = pl.multiple_of(t * 128, 128); ok = pl.multiple_of(768 + t * 128, 128); ov = pl.multiple_of(1536 + t * 128, 128)
        dkt = None; dvt = None
        for i in range(len(ps)):
            kl = (i + 1) * QB; r = slice(i * QB, kl)
            q = lane_masks(qkv_ref[r, pl.ds(oq, 128)])
            k = lane_masks(qkv_ref[0:kl, pl.ds(ok, 128)])
            v = qkv_ref[0:kl, pl.ds(ov, 128)]
            do = lane_masks(do_ref[r, pl.ds(oq, 128)])
            dss = []; pls = []
            for h in range(2):
                pb = ps[i][2 * t + h]
                p = pb.astype(f32)
                pd = p * dot_nt(do[h], v)
                dss.append((pd - p * jnp.sum(pd, axis=-1, keepdims=True)).astype(bf16)); pls.append(pb)
            dq = dot_nn(jnp.concatenate(dss, 1), jnp.concatenate(k, 0)) * attn_multiplier
            a = dot_tn(jnp.concatenate(q, 0), jnp.concatenate(dss, 0))
            b = dot_tn(jnp.concatenate(do, 0), jnp.concatenate(pls, 0))
            qkv_ref[r, pl.ds(oq, 128)] = (dq * cos_ref[r, :] - swap_halves(dq) * sin_ref[r, :]).astype(bf16)
            if dkt is None: dkt, dvt = a, b
            else:
                w = dkt.shape[1]
                dkt = jnp.concatenate([dkt + a[:, :w], a[:, w:]], 1); dvt = jnp.concatenate([dvt + b[:, :w], b[:, w:]], 1)
        dk = dkt.T * attn_multiplier
        qkv_ref[:, pl.ds(ok, 128)] = (dk * cos_ref[...] - swap_halves(dk) * sin_ref[...]).astype(bf16)
        qkv_ref[:, pl.ds(ov, 128)] = dvt.T.astype(bf16)
        return carry
    lax.fori_loop(lo, hi, pair, 0)


def wo_norm2(o_ref, w_ref, x_ref, g_ref, hs_ref, n2_ref):
    L = x_ref.shape[0]; R = 128; n = o_ref.shape[1]
    def it(i, carry):
        r = pl.ds(pl.multiple_of(i * R, R), R)
        hs = x_ref[r, :].astype(f32) + dot_nn(o_ref[pl.ds(i * (R // n), R // n)].reshape(R, 768), w_ref[2304:3072, :])
        hs_ref[r, :] = hs
        n2_ref[r, :] = (hs * norm_block(hs, None) * g_ref[1:2, :]).astype(bf16)
        return carry
    lax.fori_loop(0, L // R, it, 0)


def wo_back2(db1_ref, o_ref, w_ref, do_ref, gatt_ref):
    def it(n, carry):
        o = pl.multiple_of(n * 256, 256); w = pl.ds(pl.multiple_of(2304 + o, 256), 256)
        do_ref[:, pl.ds(o, 256)] = dot_nt(db1_ref[...], w_ref[w, :]).astype(bf16)
        gatt_ref[w, :] = dot_tn(o_ref[:, :, pl.ds(o, 256)].reshape(-1, 256), db1_ref[...]).astype(bf16)
        return carry
    lax.fori_loop(0, 3, it, 0)


def mid2(n, cg, hs_ref, b2_ref, dn2_ref, g_ref, db1_ref, gg_ref):
    gg_ref[...] = jnp.zeros_like(gg_ref)
    def body(r, o):
        row = lax.broadcasted_iota(jnp.int32, (RB, 768), 0) + o
        hs = hs_ref[r, :]
        dy = cg[r, :].astype(f32)
        cg[r, :] = jnp.where(row < n, hs + b2_ref[r, :], 0.0).astype(bf16)
        inv = norm_block(hs, None)
        dn = dn2_ref[r, :]
        q = dn * g_ref[1:2, :]
        gg_ref[1:2, :] += jnp.sum(hs * inv * dn, axis=0, keepdims=True)
        dh = dy + (inv * q - hs * inv * inv * inv * jnp.mean(hs * q, axis=-1, keepdims=True))
        hs_ref[r, :] = dh
        db1_ref[r, :] = dh.astype(bf16)
    rows_loop(hs_ref.shape[0], body)


def all_kernel(nf, nd, perm, lens, tok, cot0, gm, am, fm, cos_ref, sin_ref,
               oo, io, ggo, ao, fo,
               xg, cg, cst, wa, wf, gt, gg, gains, ggb, gb, ggr,
               n1, qkv, p0, p1, o, hs, n2, b2, dn2, gatt, gff, cs, sn,
               arc, ar1, ar2, arz, frc, fr1, fr2, frz,
               ss, rs, ls, azs2, fzs2, ags, fgs, ass, fss, acs, a1s, a2s, azs, azq, fcs, f1s, f2s, fzs, fzq):
    t = Topo2(nf, nd)
    N, Z = t.N, t.Z
    L = xg.shape[0]; pos = L // N; ra = wa.shape[0] // N; gl = gm.shape[1]; R = wf.shape[2]
    ps = (p0, p1)
    row_at = lambda ref: (lambda z, g: ref.at[pl.ds(pl.multiple_of((z * 8 + g) * ra, ra), ra)])
    blk_at = lambda ref: (lambda z, g: ref.at[z * 8 + g])
    most = lambda ref: ref.at[pl.ds(0, L - pos)]
    f0 = b2.at[pl.ds(0, ra)], dn2.at[pl.ds(0, 3 * R)]
    near_w = [pltpu.make_async_copy(a, d, ls.at[5 + i]) for i, (a, d) in enumerate(((am, f0[0]), (fm, f0[1]), (cot0, o), (cos_ref, cs), (sin_ref, sn)))]
    for c in near_w: c.start()
    near_w[0].wait()
    wa[pl.ds(pl.multiple_of(t.me * ra, ra), ra), :] = f0[0][...].astype(bf16)
    near_w[1].wait()
    wf[t.me] = f0[1][...].astype(bf16).reshape(3, R, 768)
    gt[...] = jnp.zeros_like(gt)
    gt[0:2, 0:gl] = gm[...].astype(bf16).astype(f32)
    gg[t.me] = gt[...]
    barrier_all(t)
    A = Gather2(t, row_at(wa), ss.at[3], azs2, ags)
    F = Gather2(t, blk_at(wf), ss.at[4], fzs2, fgs)
    tk = Exchange(t, lambda d: tok.at[d], rows_of(xg, pos), most(xg), most(xg), ss.at[0], rs.at[0], ls.at[0])
    ct = Exchange(t, rows_of(cst, pos), rows_of(cg, pos), most(cg), most(cg), ss.at[1], rs.at[1], ls.at[1])
    def takes(X, lo, hi, *more):
        for g, d in SEQ[lo:hi]:
            X.take(g, d, d + 1)
            for e, k in more: e.more(k)
    tk.start()
    A.start()
    tk.more(8)
    takes(A, 0, 3, (tk, 3))
    F.start()
    near_w[2].wait()
    def pm(i): cst[pl.ds(pl.multiple_of(i * pos, pos), pos), :] = o[perm[i]]
    loop(0, N, pm)
    ct.start()
    def gs(k): rcopy(gt, gg.at[t.me], ss.at[2], rs.at[2], t.flat(lax.rem(t.me + k, N))).start()
    loop(1, N, gs)
    takes(A, 3, 8, (tk, 3))
    takes(F, 0, 1)
    takes(A, 8, 10, (tk, 8), (ct, 5))
    takes(F, 1, 2)
    takes(A, 10, 13, (ct, 5))
    takes(F, 2, 3)
    takes(A, 13, 15, (ct, 5))

    tk.more(N)
    for gi in range(4): A.take_sib(gi)
    tk.wait_recv()
    wait_bytes(gg.at[pl.ds(0, N - 1)], rs.at[2])
    tot = jnp.zeros((8, 768), f32)
    for d in range(N):
        wide = jnp.concatenate([gg[d], jnp.zeros((8, 640), f32)], 1)
        tot = tot + (pltpu.roll(wide, d * gl, 1) if d else wide)
    gains[...] = tot
    ct.more(N)

    phase_norm1(xg, gains, n1)
    takes(F, 3, 4)

    near_w[3].wait(); near_w[4].wait()
    phase_qkv(n1, wa, cs, sn, qkv)
    takes(F, 4, 5)
    def fwd(i):
        attn_fwd2(qkv, ps, o, i, i + 1)
    loop(0, 2, fwd)
    takes(F, 5, 6)
    loop(2, 4, fwd)
    takes(F, 6, 7)
    loop(4, 6, fwd)
    takes(F, 7, 8)

    ct.more(N)
    wo_norm2(o, wa, xg, gains, hs, n2)
    takes(F, 8, 9)

    ct.wait_recv()
    n = lens[t.me]
    def mask(r, of):
        row = lax.broadcasted_iota(jnp.int32, (RB, 768), 0) + of
        cg[r, :] = jnp.where(row < n, cg[r, :].astype(f32), 0.0).astype(bf16)
    rows_loop(L, mask)
    SA = Scatter3(t, row_at(gatt), lambda z, g: gatt[pl.ds(pl.multiple_of((z * 8 + g) * ra, ra), ra), :], arc, ar1, ar2, arz, ass, acs, a1s, a2s, azs, azq)
    SF = Scatter3(t, blk_at(gff), lambda z, g: gff[z * 8 + g], frc, fr1, fr2, frz, fss, fcs, f1s, f2s, fzs, fzq, far=False)
    def tile(i):
        z = near(t, i // 2)
        par = lax.rem(i, 2)
        cc = t.c + par * (1 - 2 * t.c)
        slots = [z * 8 + q * 2 + cc for q in range(4)]
        for k, lo, hi in ((1, 9, 11), (2, 11, 12), (3, 12, 13), (4, 13, 14), (6, 14, 15)):
            @pl.when(i == k)
            def _(): takes(F, lo, hi)
        for k in range(Z - 1):
            @pl.when(i == 2 * k + 3)
            def _(): SF.C(k)
        @pl.when(par == 1)
        def _():
            for q in range(4): F.wait(z, q * 2 + cc)
        wg, wu, wd = (jnp.concatenate([wf[sl, j] for sl in slots], 0) for j in range(3))
        nv = n2[...]
        ga = dot_nt(nv, wg); u = dot_nt(nv, wu)
        da = dot_nt(cg[...], wd)
        sg = 1.0 / (1.0 + jnp.exp2(ga * (-LOG2E)))
        silu = ga * sg
        a = (silu * u).astype(bf16)
        dg = (da * u * (sg * (1.0 + ga * (1.0 - sg)))).astype(bf16)
        du = (da * silu).astype(bf16)
        bb = dot_nn(a, wd)
        dn = dot_nn(dg, wg) + dot_nn(du, wu)
        @pl.when(i == 0)
        def _():
            b2[...] = bb; dn2[...] = dn
        @pl.when(i > 0)
        def _():
            b2[...] += bb; dn2[...] += dn
        for j, (lhs, rhs) in enumerate(((dg, nv), (du, nv), (a, cg[...]))):
            w = dot_tn(lhs, rhs).astype(bf16)
            for q, sl in enumerate(slots): gff[sl, j] = w[q * R:(q + 1) * R]
        @pl.when(par == 1)
        def _(): SF.start(z)
    loop(0, 8, tile)
    ox = Exchange(t, rows_of(cg, pos), lambda d: oo.at[d], most(cg), oo.at[pl.ds(0, N - 1)], ss.at[5], rs.at[3], ls.at[3])
    ix = Exchange(t, rows_of(n1, pos), lambda d: io.at[d], most(n1), io.at[pl.ds(0, N - 1)], ss.at[6], rs.at[4], ls.at[4])
    mid2(n, cg, hs, b2, dn2, gains, n2, ggb)
    SF.C(3)
    ox.start(); ox.more(8)
    ct.wait_send()
    wo_back2(n2, o, wa, cst, gatt)
    SF.F(0, 1); SF.D(0); ox.more(8)
    def back(i):
        attn_bwd2(qkv, ps, cst, cs, sn, i, i + 1)
    loop(0, 2, back)
    ox.more(8)
    loop(2, 4, back)
    SF.F(2); SF.D(1); ox.more(N)
    loop(4, 6, back)
    phase_wqkv_grad(qkv, n1, gatt)
    for i in range(Z): SA.start(SA.zof(i))
    SF.F(3); SF.D(2)
    SA.C(0, 1)
    phase_dn1(qkv, wa, xg, gains, hs, n1, ggb)
    ix.start(); ix.more(8)
    SF.D(3)
    for d in range(N):
        v = ggb[...]
        gb[d] = (pltpu.roll(v, 768 - d * gl, 1) if d else v)[:, 0:128]
    ggr[t.me] = gb[t.me]
    def gsend(k):
        d = lax.rem(t.me + k, N)
        rcopy(gb.at[d], ggr.at[t.me], ss.at[7], rs.at[5], t.flat(d)).start()
    loop(1, N, gsend)
    SA.F(0); SA.C(2); ix.more(8)
    SA.F(1); SA.S(0); SA.C(3); ix.more(N)
    SA.F(2); SA.S(1)
    f0[1][...] = SF.total().reshape(3 * R, 768)
    far = [pltpu.make_async_copy(f0[1], fo, ls.at[6]), pltpu.make_async_copy(f0[0], ao, ls.at[5])]
    far[0].start()
    SA.F(3); SA.S(2); SA.S(3)
    wait_bytes(ggr.at[pl.ds(0, N - 1)], rs.at[5])
    tot = ggr[0]
    for d in range(1, N): tot = tot + ggr[d]
    ggo[...] = tot
    f0[0][...] = SA.total()
    far[1].start()
    ox.wait_recv(); ix.wait_recv()
    for c in far: c.wait()
    tk.wait_send(); ox.wait_send(); ix.wait_send()
    wait_bytes(gg.at[pl.ds(0, N - 1)], ss.at[2]); wait_bytes(ggr.at[pl.ds(0, N - 1)], ss.at[7])
    A.finish(wa.at[pl.ds(0, 7 * Z * ra)])
    F.finish(wf.at[pl.ds(0, 7 * Z)])
    SF.wait_send(); SA.wait_send()


def all_call(perm, lens, tok, cot, gm, am, fm, C, S):
    nf, nd = lax.axis_size("fsdp"), lax.axis_size("dp"); N = nf * nd; Z = nf // 2
    pos, D = tok.shape[1:]; L = pos * N; ra = am.shape[0]; R = fm.shape[0] // 3
    hbm = pl.BlockSpec(memory_space=pltpu.HBM); V = pl.BlockSpec(memory_space=pltpu.VMEM); SM = pl.BlockSpec(memory_space=pltpu.SMEM)
    sd = jax.ShapeDtypeStruct; Q = pltpu.SemaphoreType.DMA
    vm = lambda *s, dt=bf16: pltpu.VMEM(s, dt)
    return pl.pallas_call(functools.partial(all_kernel, nf, nd),
        out_shape=(sd(tok.shape, bf16), sd(tok.shape, bf16), sd((8, 128), f32), sd((ra, D), f32), sd((3 * R, D), f32)),
        in_specs=[SM, SM, hbm, hbm, V, hbm, hbm, hbm, hbm], out_specs=(hbm, hbm, V, hbm, hbm),
        scratch_shapes=[vm(L, D), vm(L, D), vm(L, D), vm(N * ra, D), vm(N, 3, R, D), vm(8, 128, dt=f32), vm(N, 8, 128, dt=f32), vm(8, D, dt=f32),
                        vm(8, D, dt=f32), vm(N, 8, 128, dt=f32), vm(N, 8, 128, dt=f32),
                        vm(L, D), vm(L, 3 * D), vm(H, 256, 256), vm(H, 256, 512), vm(N, pos, D), vm(L, D, dt=f32), vm(L, D), vm(L, D, dt=f32), vm(L, D, dt=f32),
                        vm(N * ra, D), vm(N, 3, R, D), vm(L, 128, dt=f32), vm(L, 128, dt=f32)]
                       + [vm(n, *sh) for sh in ((ra, D), (3, R, D)) for n in (4 * Z, 2 * Z, Z, Z + 1)]
                       + [Q((8,)), Q((6,)), Q((10,)), Q((Z, 2)), Q((Z, 2)), Q((Z, 8)), Q((Z, 8)), Q((4,)), Q((4,))] + [Q((n,)) for _ in range(2) for n in (4 * Z, 2 * Z, Z, Z + 1, Z)],
        compiler_params=pltpu.CompilerParams(collective_id=2, has_side_effects=True, vmem_limit_bytes=64 * 2**20))(perm, lens, tok, cot, gm, am, fm, C, S)


def update(w, q, m, v, decay, mo, vo, wo):
    m2 = beta_first * m + (1.0 - beta_first) * q
    v2 = beta_second * v + (1.0 - beta_second) * q * q
    mo[...] = m2
    vo[...] = v2
    new = w - learning_rate * ((m2 / (1.0 - beta_first**STEP)) / (jnp.sqrt(v2 / (1.0 - beta_second**STEP)) + adam_epsilon) + decay * w)
    wo[...] = new
    return new


def last_kernel(slot, *refs):
    ins, outs, iv, ov, isem, osem = refs[:14], refs[14:30], refs[30:44], refs[44:57], refs[57], refs[58]
    oo, io, gs, ag, fg = ins[:5]
    N = oo.shape[0]; gl = ins[11].shape[1]
    order = [8, 9, 10, 4, 5, 6, 7, 3, 1, 11, 12, 13, 2, 0]
    src = {k: pltpu.make_async_copy(ins[k], iv[i], isem.at[i]) for i, k in enumerate(order)}
    val = {k: iv[i] for i, k in enumerate(order)}
    for k in order: src[k].start()
    done = []
    def copy(a, b, i):
        c = pltpu.make_async_copy(a, b, osem.at[i]); c.start(); done.append(c)
    put = {k: i for i, k in enumerate((0, 4, 5, 6, 7, 8, 9, 10, 11, 12, 13, 14, 15))}
    def out(k): copy(ov[put[k]], outs[k], k)
    at = lambda k: ov[put[k]]
    for w, q, m, v, ks in ((8, 4, 9, 10, (7, 8, 12, 15)), (5, 3, 6, 7, (5, 6, 11, 14))):
        for k in (w, q, m, v): src[k].wait()
        new = update(val[w][...], val[q][...], val[m][...], val[v][...], weight_decay, at(ks[0]), at(ks[1]), at(ks[2]))
        at(ks[3])[...] = new.astype(bf16)
        for k in ks: out(k)
        copy(val[q], outs[q - 1], q - 1)
    src[1].wait()
    copy(val[1], outs[1], 1)
    for k in (11, 12, 13, 2): src[k].wait()
    q = val[2][0:2, 0:gl]
    w = val[11][...]
    at(4)[...] = q
    at(13)[...] = update(w, q, val[12][...], val[13][...], 0.0, at(9), at(10), at(13)) - w
    for k in (4, 9, 10, 13): out(k)
    src[0].wait()
    def pm(j): at(0)[j] = val[0][slot[j]]
    loop(0, N, pm)
    out(0)
    for c in done: c.wait()


def last_call(slot, oo, io, gs, ag, fg, am, amm, amv, fm, fmm, fmv, gm, gmm, gmv):
    A = pl.BlockSpec(memory_space=pltpu.HBM); SM = pl.BlockSpec(memory_space=pltpu.SMEM)
    sd = lambda a, dt=None: jax.ShapeDtypeStruct(a.shape, dt or a.dtype)
    args = (oo, io, gs, ag, fg, am, amm, amv, fm, fmm, fmv, gm, gmm, gmv)
    res = (sd(oo), sd(io), sd(am), sd(fm), sd(gm), sd(am), sd(am), sd(fm), sd(fm), sd(gm), sd(gm), sd(am), sd(fm), sd(gm), sd(am, bf16), sd(fm, bf16))
    vm = lambda a: pltpu.VMEM(a.shape, a.dtype)
    return pl.pallas_call(last_kernel, in_specs=[SM] + [A] * 14, out_specs=(A,) * 16, out_shape=res,
        scratch_shapes=[vm(args[k]) for k in (8, 9, 10, 4, 5, 6, 7, 3, 1, 11, 12, 13, 2, 0)] + [vm(res[k]) for k in (0, 4, 5, 6, 7, 8, 9, 10, 11, 12, 13, 14, 15)]
                       + [pltpu.SemaphoreType.DMA((14,)), pltpu.SemaphoreType.DMA((16,))],
        compiler_params=pltpu.CompilerParams(vmem_limit_bytes=64 * 2**20))(slot, *args)


def local_one(tokens, cotangent, lengths, device_sequence, slot_device, attention_master, feedforward_master, gains_master,
              attention_mean, attention_square, feedforward_mean, feedforward_square, gains_mean, gains_square):
    N = lax.axis_size(AX)
    counter = jnp.arange(N, dtype=jnp.int32)
    slot_sequence = jnp.sum(jnp.where(slot_device[:, None] == counter[None, :], device_sequence[None, :], 0), axis=1)
    slot_of_sequence = jnp.sum(jnp.where(slot_sequence[:, None] == counter[None, :], counter[:, None], 0), axis=0)
    tr = lambda a: a.transpose(1, 0, 2)
    C, S = tables(tokens.shape[1] * N)
    width = tokens.shape[2]
    oo, io, gs, ag, fg = all_call(slot_of_sequence, lengths, tokens, cotangent, gains_master, attention_master,
                                  tr(feedforward_master).reshape(-1, width), jnp.asarray(C), jnp.asarray(S))
    fg = fg.reshape(3, -1, width)
    r = list(last_call(slot_sequence, oo, io, gs, ag, fg, attention_master, attention_mean, attention_square,
                       tr(feedforward_master), tr(feedforward_mean), tr(feedforward_square), gains_master, gains_mean, gains_square))
    for i in (3, 7, 8, 12, 15): r[i] = tr(r[i])
    return tuple(r)


def solution(mesh):
    t, r, f, g = P(None, AX, None), P(AX, None), P(AX, None, None), P(None, AX)
    in_specs = (t, t, P(), P(), P(), r, f, g, r, r, f, f, g, g)
    out_specs = (t, t, r, f, g, r, r, f, f, g, g, r, f, g, r, f)
    n = mesh.shape["fsdp"] * mesh.shape["dp"]
    body = local_one if 512 // n % 16 == 0 and 3072 // n % 16 == 0 else local
    return jax.shard_map(body, mesh=mesh, in_specs=in_specs, out_specs=out_specs, check_vma=False)
```
